32 devices in a mesh: dp: 8 (over y, x, core), mp: 4 (over z).
Axes of the slice: x: 2, y: 2, z: 4, core: 2. Of those that a mesh axis runs over, the one named last changes fastest.
Arguments:
- residues: bfloat16 [4096, 768], P('dp', 'mp'), may hold values from -6 to 6
- pair_input: bfloat16 [16, 256, 256, 256], P('dp', 'mp'), may hold values from -6 to 6
- out_grad: bfloat16 [4096, 768], P('dp', 'mp'), may hold values from -6 to 6
- bucket_layout: int32 [16], P('dp'), may hold values from 0 to 4
- time_bins: int32 [16, 4], P('dp'), may hold values from 0 to 63
- fold_class: int32 [16, 4], P('dp'), may hold values from 0 to 42
- attend_weight: float32 [768, 3, 768], P('dp', None, 'mp'), may hold values from -0.21875 to 0.21875
- attend_state: float32 [3, 768, 3, 768], P(None, 'dp', None, 'mp'), as said below
- merge_weight: float32 [768, 768], P('mp', 'dp'), may hold values from -0.625 to 0.625
- merge_state: float32 [3, 768, 768], P(None, 'mp', 'dp'), as said below
- expand_weight: float32 [768, 2, 3072], P('dp', None, 'mp'), may hold values from -0.21875 to 0.21875
- expand_state: float32 [3, 768, 2, 3072], P(None, 'dp', None, 'mp'), as said below
- shrink_weight: float32 [3072, 768], P('mp', 'dp'), may hold values from -0.109375 to 0.109375
- shrink_state: float32 [3, 3072, 768], P(None, 'mp', 'dp'), as said below
- modulate_weight: float32 [256, 6, 768], P('dp', None, 'mp'), may hold values from -0.375 to 0.375
- modulate_state: float32 [3, 256, 6, 768], P(None, 'dp', None, 'mp'), as said below
- pair_weight: float32 [256, 12], P('dp'), may hold values from -0.375 to 0.375
- pair_state: float32 [3, 256, 12], P(None, 'dp'), as said below
- class_weight: float32 [43, 256], P(None, 'dp'), may hold values from -4 to 4
- class_state: float32 [3, 43, 256], P(None, None, 'dp'), as said below
Outputs:
- output: bfloat16 [4096, 768], P('dp', 'mp')
- residue_grad: bfloat16 [4096, 768], P('dp', 'mp')
- pair_grad: bfloat16 [16, 256, 256, 256], P('dp', 'mp')
- attend_master: float32 [2, 768, 3, 768], P(None, 'dp', None, 'mp')
- attend_tracked: float32 [2, 768, 3, 768], P(None, 'dp', None, 'mp')
- merge_master: float32 [2, 768, 768], P(None, 'mp', 'dp')
- merge_tracked: float32 [2, 768, 768], P(None, 'mp', 'dp')
- expand_master: float32 [2, 768, 2, 3072], P(None, 'dp', None, 'mp')
- expand_tracked: float32 [2, 768, 2, 3072], P(None, 'dp', None, 'mp')
- shrink_master: float32 [2, 3072, 768], P(None, 'mp', 'dp')
- shrink_tracked: float32 [2, 3072, 768], P(None, 'mp', 'dp')
- modulate_master: float32 [2, 256, 6, 768], P(None, 'dp', None, 'mp')
- modulate_tracked: float32 [2, 256, 6, 768], P(None, 'dp', None, 'mp')
- pair_master: float32 [2, 256, 12], P(None, 'dp')
- pair_tracked: float32 [2, 256, 12], P(None, 'dp')
- class_master: float32 [2, 43, 256], P(None, None, 'dp')
- class_tracked: float32 [2, 43, 256], P(None, None, 'dp')
The draws below stay inside these ranges and needn't reach their ends.
Inputs may be any that keep to these rules, and one draw needn't show every extreme that they name: `bucket_layout`: each window of 256 residues holds whole proteins: 0 one of 256, 1 two of 128, 2 one of 128 then two of 64, 3 two of 64 then one of 128, 4 four of 64. `time_bins`: slot s of a window describes its s-th protein; slots past the window's proteins are unused. `fold_class`: slot s of a window describes its s-th protein; slots past the window's proteins are unused. `attend_state`: slices hold the first moment, the second moment (positive) and the weights' average. `merge_state`: slices hold the first moment, the second moment (positive) and the weights' average. `expand_state`: slices hold the first moment, the second moment (positive) and the weights' average. `shrink_state`: slices hold the first moment, the second moment (positive) and the weights' average. `modulate_state`: slices hold the first moment, the second moment (positive) and the weights' average. `pair_state`: slices hold the first moment, the second moment (positive) and the weights' average. `class_state`: slices hold the first moment, the second moment (positive) and the weights' average.
All inputs are finite; a program needn't handle non-finite values.
Results may differ from the reference program's by a relative error of at most 0.015.
The reference program's roundings to bfloat16 on the way count: a program that leaves them out, or rounds other values in their place, can miss the bound.
Values may be sent and summed in bfloat16 or wider, within the bound.
A program may use at most 128 MiB of HBM per device.

```python
import math
import jax
import jax.numpy as jnp
import numpy as np
from jax import lax

D = 768
HEADS = 12
HD = 64
FF = 3072
PAIR = 256
CDIM = 256
NCLASS = 43
TBINS = 64
SLOTS = 4
STEP = 10
WIN = 256
WINDOWS = 16
TOKENS = 4096


def adam_state(key, shape, gradient, spread):
    first_key, second_key, third_key = jax.random.split(key, 3)
    first = jax.random.normal(first_key, shape, jnp.float32) * (gradient * 0.1 / 0.9)
    ratio = 0.001 / 0.999
    second = gradient * gradient * ratio * jnp.exp(jax.random.uniform(second_key, shape, jnp.float32, 0.0, math.log(4.0)))
    third = jax.random.normal(third_key, shape, jnp.float32) * spread
    return jnp.stack([first, second, third]).astype(jnp.float32)


def draw_attend_state(key, part):
    slices = jnp.asarray([1.2, 1.2, 0.6], jnp.float32)[None, :, None] * math.sqrt(TOKENS)
    return adam_state(key, (D, 3, D), slices, D ** (-0.5))


def draw_merge_state(key, part):
    return adam_state(key, (D, D), 0.4 * math.sqrt(TOKENS), (D // 8) ** (-0.5))


def draw_expand_state(key, part):
    return adam_state(key, (D, 2, FF), 0.6 * math.sqrt(TOKENS), D ** (-0.5))


def draw_shrink_state(key, part):
    return adam_state(key, (FF, D), 0.9 * math.sqrt(TOKENS), FF ** (-0.5))


def draw_modulate_state(key, part):
    return adam_state(key, (CDIM, 6, D), math.sqrt(TOKENS), CDIM ** (-0.5))


def draw_pair_state(key, part):
    return adam_state(key, (PAIR, HEADS), 0.8 * math.sqrt(TOKENS * min(WIN, 32)), PAIR ** (-0.5))


def draw_class_state(key, part):
    return adam_state(key, (NCLASS, CDIM), 5.0 * math.sqrt(TOKENS / NCLASS), 1.0)


def set_ends(drawn, rng, low, top_value):
    longest = drawn.shape.index(max(drawn.shape))
    spots = []
    for shift in (0, 1):
        where = [jax.random.randint(jax.random.fold_in(rng, axis), (), 0, length) for axis, length in enumerate(drawn.shape)]
        where[longest] = (where[longest] + shift) % drawn.shape[longest]
        spots.append(tuple(where))
    return drawn.at[spots[0]].set(low).at[spots[1]].set(top_value)


def block_levels(rng, dims, cuts, low, largest):
    def one(axis_at, parts):
        draws = jax.random.uniform(jax.random.fold_in(jax.random.fold_in(rng, 6), axis_at), (parts,), jnp.float32, low / len(cuts), largest / len(cuts))
        return jnp.repeat(jnp.exp(draws), dims[axis_at] // parts).reshape((-1,) + (1,) * (len(dims) - axis_at - 1))

    level = one(*cuts[0])
    for cut in cuts[1:]:
        level = level * one(*cut)
    return level


def bell_draw(stream_key, extent, scale, most, shards=(), kind=jnp.bfloat16):
    drawn = jax.random.normal(stream_key, extent, jnp.float32) * scale
    if len(shards) > 0:
        drawn = block_levels(stream_key, extent, shards, -0.22, 0.18) * drawn
    return jnp.clip(drawn, min=-most, max=most).astype(kind)


def setup_inputs(seed: int = 0) -> dict:
    arg_keys = jax.random.split(jax.random.key(seed), 21)
    return {
        "residues": bell_draw(arg_keys[0], (TOKENS, D), 1.0, 6.0, ((0, 8), (1, 4))),
        "pair_input": bell_draw(arg_keys[1], (WINDOWS, WIN, WIN, PAIR), 1.0, 6.0, ((0, 8), (1, 4))),
        "out_grad": bell_draw(arg_keys[2], (TOKENS, D), 1.0, 6.0, ((0, 8), (1, 4))),
        "bucket_layout": set_ends(jax.random.randint(arg_keys[3], (WINDOWS,), 0, 5), jax.random.fold_in(arg_keys[3], 1), 0, 4).astype(jnp.int32),
        "time_bins": set_ends(jax.random.randint(arg_keys[4], (WINDOWS, SLOTS), 0, TBINS), jax.random.fold_in(arg_keys[4], 1), 0, TBINS - 1).astype(jnp.int32),
        "fold_class": set_ends(jax.random.randint(arg_keys[5], (WINDOWS, SLOTS), 0, NCLASS), jax.random.fold_in(arg_keys[5], 1), 0, NCLASS - 1).astype(jnp.int32),
        "attend_weight": bell_draw(arg_keys[6], (D, 3, D), D ** -0.5, 0.21875, ((0, 8), (2, 4)), jnp.float32),
        "attend_state": draw_attend_state(jax.random.fold_in(arg_keys[20], 71), 0),
        "merge_weight": bell_draw(arg_keys[8], (D, D), (D // 8) ** -0.5, 0.625, ((0, 4), (1, 8)), jnp.float32),
        "merge_state": draw_merge_state(jax.random.fold_in(arg_keys[20], 71), 0),
        "expand_weight": bell_draw(arg_keys[10], (D, 2, FF), D ** -0.5, 0.21875, ((0, 8), (2, 4)), jnp.float32),
        "expand_state": draw_expand_state(jax.random.fold_in(arg_keys[20], 71), 0),
        "shrink_weight": bell_draw(arg_keys[12], (FF, D), FF ** -0.5, 0.109375, ((0, 4), (1, 8)), jnp.float32),
        "shrink_state": draw_shrink_state(jax.random.fold_in(arg_keys[20], 71), 0),
        "modulate_weight": bell_draw(arg_keys[14], (CDIM, 6, D), CDIM ** -0.5, 0.375, ((0, 8), (2, 4)), jnp.float32),
        "modulate_state": draw_modulate_state(jax.random.fold_in(arg_keys[20], 71), 0),
        "pair_weight": bell_draw(arg_keys[16], (PAIR, HEADS), PAIR ** -0.5, 0.375, ((0, 8),), jnp.float32),
        "pair_state": draw_pair_state(jax.random.fold_in(arg_keys[20], 71), 0),
        "class_weight": bell_draw(arg_keys[18], (NCLASS, CDIM), 1.0, 4.0, ((1, 8),), jnp.float32),
        "class_state": draw_class_state(jax.random.fold_in(arg_keys[20], 71), 0),
    }


@jax.custom_vjp
def low(v):
    return lax.optimization_barrier(v.astype(jnp.bfloat16)).astype(jnp.float32)

@jax.custom_vjp
def low_back(v):
    return v

def low_keep(v):
    return (low(v), None)

def low_pass(kept, grad):
    return (grad,)

def back_keep(v):
    return (v, None)

def back_low(kept, grad):
    return (low(grad),)
low.defvjp(low_keep, low_pass)
low_back.defvjp(back_keep, back_low)
PATTERNS = np.array([[0, 0, 0, 0], [0, 0, 1, 1], [0, 0, 1, 2], [0, 1, 2, 2], [0, 1, 2, 3]], dtype=np.int32)
NORM_EPS = 1e-06
BETA_ONE = 0.9
BETA_TWO = 0.999
ADAM_EPS = 1e-08
DECAY = 0.01
AVERAGE = 0.999
MASKED = -1e+30
HIGH = lax.Precision.HIGHEST

def time_features(bins, width):
    half = width // 2
    moment = (bins.astype(jnp.float32) + 0.5) / TBINS
    freq = jnp.exp(-math.log(10000.0) * jnp.arange(half, dtype=jnp.float32) / half)
    angle = 1000.0 * moment[..., None] * freq
    return jnp.concatenate([jnp.sin(angle), jnp.cos(angle)], axis=-1)

def slot_ids(layout, window):
    unit = np.arange(window) // (window // 4)
    table = jnp.asarray(PATTERNS[:, unit])
    select = (layout[:, None] == jnp.arange(5, dtype=jnp.int32)[None, :]).astype(jnp.int32)
    return jnp.dot(select, table)

def layer_norm(hidden):
    center = lax.optimization_barrier(jnp.mean(hidden, axis=-1, keepdims=True))
    square = lax.optimization_barrier(jnp.mean(hidden * hidden, axis=-1, keepdims=True))
    return (hidden - center) * lax.rsqrt(square - center * center + NORM_EPS)

def adamw(master, state, grad, rate):
    first = BETA_ONE * state[0] + (1.0 - BETA_ONE) * grad
    second = BETA_TWO * state[1] + (1.0 - BETA_TWO) * grad * grad
    first_hat = first / (1.0 - BETA_ONE ** STEP)
    second_hat = second / (1.0 - BETA_TWO ** STEP)
    updated = master - rate * (first_hat / (jnp.sqrt(second_hat) + ADAM_EPS) + DECAY * master)
    average = AVERAGE * state[2] + (1.0 - AVERAGE) * updated
    return (jnp.stack([updated, average]), jnp.stack([first, second]))

def reference(residues, pair_input, out_grad, bucket_layout, time_bins, fold_class, attend_weight, attend_state, merge_weight, merge_state, expand_weight, expand_state, shrink_weight, shrink_state, modulate_weight, modulate_state, pair_weight, pair_state, class_weight, class_state):
    windows = bucket_layout.shape[0]
    slot = slot_ids(bucket_layout, WIN)
    pick = (slot[..., None] == jnp.arange(SLOTS, dtype=jnp.int32)).astype(jnp.float32)
    same = slot[:, :, None] == slot[:, None, :]
    class_pick = (fold_class[..., None] == jnp.arange(NCLASS, dtype=jnp.int32)).astype(jnp.float32)
    sinus = time_features(time_bins, CDIM)
    factor = HD ** (-0.5)

    def attend_window(items):
        query, keys, values, bias, mask = items
        query = query.reshape(WIN, HEADS, HD)
        keys = keys.reshape(WIN, HEADS, HD)
        values = values.reshape(WIN, HEADS, HD)
        scores = jnp.einsum('ihe,jhe->hij', query, keys, precision=HIGH) * factor + bias
        scores = low_back(scores)
        scores = jnp.where(mask[None], scores, MASKED)
        peak = lax.optimization_barrier(jnp.max(scores, axis=-1, keepdims=True))
        expo = jnp.exp(scores - peak)
        chance = expo / lax.optimization_barrier(jnp.sum(expo, axis=-1, keepdims=True))
        mixed = jnp.einsum('hij,jhe->ihe', low(chance), values, precision=HIGH).reshape(WIN, D)
        return low_back(low(mixed))

    def forward(hidden, pairs, attend, merge, expand, shrink, modulate, pairwise, classes):
        before = sinus + jnp.einsum('wsn,nc->wsc', class_pick, low(classes), precision=HIGH)
        condition = low(jax.nn.silu(before))
        modulation = jnp.einsum('wsc,cjd->wsjd', condition, low(modulate), precision=HIGH)
        per_token = jnp.einsum('wts,wsjd->wtjd', pick, modulation, precision=HIGH)
        start = hidden.reshape(windows, WIN, D)
        rows_one = low(layer_norm(start) * (1.0 + per_token[:, :, 1]) + per_token[:, :, 0])
        triple = jnp.einsum('wtd,dje->wtje', rows_one, low(attend), precision=HIGH)
        query = low_back(low(triple[:, :, 0]))
        keys = low_back(low(triple[:, :, 1]))
        values = low_back(low(triple[:, :, 2]))
        bias = low_back(low(jnp.einsum('wijc,ch->whij', pairs, low(pairwise), precision=HIGH)))
        mixed = lax.map(jax.checkpoint(attend_window), (query, keys, values, bias, same))
        attended = low_back(jnp.einsum('wtd,de->wte', mixed, low(merge), precision=HIGH))
        middle = start + per_token[:, :, 2] * attended
        rows_two = low(layer_norm(middle) * (1.0 + per_token[:, :, 4]) + per_token[:, :, 3])
        pair_up = low_back(jnp.einsum('wtd,dje->wtje', rows_two, low(expand), precision=HIGH))
        activated = low(jax.nn.silu(pair_up[:, :, 0]) * pair_up[:, :, 1])
        fed = low_back(jnp.einsum('wtf,fd->wtd', activated, low(shrink), precision=HIGH))
        return (middle + per_token[:, :, 5] * fed).reshape(windows * WIN, D)
    primals = (residues.astype(jnp.float32), pair_input.astype(jnp.float32), attend_weight, merge_weight, expand_weight, shrink_weight, modulate_weight, pair_weight, class_weight)
    output, pullback = jax.vjp(forward, *primals)
    grads = pullback(out_grad.astype(jnp.float32))
    rates = (2.0 / math.sqrt(D), 2.0 / math.sqrt(D // 8), 2.0 / math.sqrt(D), 2.0 / math.sqrt(FF), 2.0 / math.sqrt(CDIM), 2.0 / math.sqrt(PAIR), 2.0)
    states = (attend_state, merge_state, expand_state, shrink_state, modulate_state, pair_state, class_state)
    results = []
    for index in range(7):
        updated, tracked = adamw(primals[index + 2], states[index], grads[index + 2], rates[index])
        results.append(updated)
        results.append(tracked)
    return (output.astype(jnp.bfloat16), grads[0].astype(jnp.bfloat16), grads[1].astype(jnp.bfloat16), results[0], results[1], results[2], results[3], results[4], results[5], results[6], results[7], results[8], results[9], results[10], results[11], results[12], results[13])
```

```python
import math

import jax
import jax.numpy as jnp
import numpy as np
from jax import lax
from jax.experimental import pallas as pl
from jax.experimental.pallas import tpu as pltpu
from jax.sharding import PartitionSpec as P

D = 768
HD = 64
FF = 3072
PAIR = 256
CDIM = 256
TBINS = 64
STEP = 10


PATTERNS = np.array(
    [[0, 0, 0, 0], [0, 0, 1, 1], [0, 0, 1, 2], [0, 1, 2, 2], [0, 1, 2, 3]], dtype=np.int32
)
NORM_EPS = 1e-06
BETA_ONE = 0.9
BETA_TWO = 0.999
ADAM_EPS = 1e-08
DECAY = 0.01
AVERAGE = 0.999
MASKED = -1e30
HIGH = lax.Precision.HIGHEST


def time_features(bins, width):
    half = width // 2
    moment = (bins.astype(jnp.float32) + 0.5) / TBINS
    freq = jnp.exp(-math.log(10000.0) * jnp.arange(half, dtype=jnp.float32) / half)
    angle = 1000.0 * moment[..., None] * freq
    return jnp.concatenate([jnp.sin(angle), jnp.cos(angle)], axis=-1)


def slot_ids(layout, window):
    unit = np.arange(window) // (window // 4)
    table = jnp.asarray(PATTERNS[:, unit])
    select = (layout[:, None] == jnp.arange(5, dtype=jnp.int32)[None, :]).astype(jnp.int32)
    return jnp.dot(select, table)


def adamw(master, state, grad, rate):
    first = BETA_ONE * state[0] + (1.0 - BETA_ONE) * grad
    second = BETA_TWO * state[1] + (1.0 - BETA_TWO) * grad * grad
    first_hat = first / (1.0 - BETA_ONE**STEP)
    second_hat = second / (1.0 - BETA_TWO**STEP)
    updated = master - rate * (first_hat / (jnp.sqrt(second_hat) + ADAM_EPS) + DECAY * master)
    average = AVERAGE * state[2] + (1.0 - AVERAGE) * updated
    return (jnp.stack([updated, average]), jnp.stack([first, second]))


def normalize(hidden, shift, scale, width):
    totals = lax.psum((jnp.sum(hidden, axis=1), jnp.sum(hidden * hidden, axis=1)), "mp")
    center = totals[0] / width
    spread = lax.rsqrt(totals[1] / width - center * center + NORM_EPS)
    normed = (hidden - center[:, None]) * spread[:, None]
    rows = (normed * (1.0 + scale) + shift).astype(jnp.bfloat16)
    return (normed, spread, lax.all_gather(rows, "mp", axis=1, tiled=True))


def normalize_back(partial_value, normed, spread, scale, width):
    upstream = lax.psum_scatter(partial_value, "mp", scatter_dimension=1, tiled=True)
    inner = upstream * (1.0 + scale)
    totals = lax.psum((jnp.sum(inner, axis=1), jnp.sum(inner * normed, axis=1)), "mp")
    result = spread[:, None] * (
        inner - totals[0][:, None] / width - normed * (totals[1][:, None] / width)
    )
    return (upstream, result)


def branch_total(partial_value):
    return lax.psum_scatter(partial_value, "mp", scatter_dimension=1, tiled=True)


def gather_grad(value):
    return lax.all_gather(value, "mp", axis=1, tiled=True)


def attention_scores(query, keys, bias, same, factor):
    scores = jnp.einsum(
        "wihe,wjhe->whij", query, keys, preferred_element_type=jnp.float32
    ) * factor + bias.astype(jnp.float32)
    return jnp.where(same[:, None], scores, MASKED)


def local(
    residues,
    pair_input,
    out_grad,
    bucket_layout,
    time_bins,
    fold_class,
    attend_weight,
    attend_state,
    merge_weight,
    merge_state,
    expand_weight,
    expand_state,
    shrink_weight,
    shrink_state,
    modulate_weight,
    modulate_state,
    pair_weight,
    pair_state,
    class_weight,
    class_state,
):
    parts = lax.axis_size("mp")
    gathered = (
        lax.all_gather(attend_weight.astype(jnp.bfloat16), "dp", axis=0, tiled=True),
        lax.all_gather(merge_weight.astype(jnp.bfloat16), "dp", axis=1, tiled=True),
        lax.all_gather(expand_weight.astype(jnp.bfloat16), "dp", axis=0, tiled=True),
        lax.all_gather(shrink_weight.astype(jnp.bfloat16), "dp", axis=1, tiled=True),
        lax.all_gather(modulate_weight.astype(jnp.bfloat16), "dp", axis=0, tiled=True),
        lax.all_gather(pair_weight.astype(jnp.bfloat16), "dp", axis=0, tiled=True),
        lax.all_gather(class_weight.astype(jnp.bfloat16), "dp", axis=1, tiled=True),
    )
    attend_full, merge_full, expand_full, shrink_full, modulate_full, pair_full, class_full = (
        gathered
    )
    tokens, local_width = residues.shape
    windows = bucket_layout.shape[0]
    window = tokens // windows
    slots = time_bins.shape[1]
    classes_count = class_full.shape[0]
    heads_local = local_width // HD
    width = local_width * parts
    factor = HD ** (-0.5)
    slot = slot_ids(bucket_layout, window)
    pick = (slot[..., None] == jnp.arange(slots, dtype=jnp.int32)).astype(jnp.float32)
    same = slot[:, :, None] == slot[:, None, :]
    class_pick = (fold_class[..., None] == jnp.arange(classes_count, dtype=jnp.int32)).astype(
        jnp.float32
    )
    before = time_features(time_bins, class_full.shape[1]) + jnp.einsum(
        "wsn,nc->wsc", class_pick, class_full.astype(jnp.float32), precision=HIGH
    )
    condition = jax.nn.silu(before).astype(jnp.bfloat16)
    modulation = jnp.einsum(
        "wsc,cjd->wsjd", condition, modulate_full, preferred_element_type=jnp.float32
    )
    per_token = jnp.einsum("wts,wsjd->wtjd", pick, modulation, precision=HIGH).reshape(
        tokens, 6, local_width
    )
    hidden_in = residues.astype(jnp.float32)
    normed_one, spread_one, rows_one = normalize(hidden_in, per_token[:, 0], per_token[:, 1], width)
    triple = jnp.einsum(
        "td,dje->tje", rows_one, attend_full, preferred_element_type=jnp.float32
    ).astype(jnp.bfloat16)
    query = triple[:, 0].reshape(windows, window, heads_local, HD)
    keys = triple[:, 1].reshape(windows, window, heads_local, HD)
    values = triple[:, 2].reshape(windows, window, heads_local, HD)
    local_bias = jnp.einsum(
        "wijc,ch->whij", pair_input, pair_full, preferred_element_type=jnp.float32
    ).astype(jnp.bfloat16)
    bias = lax.all_to_all(local_bias, "mp", split_axis=1, concat_axis=2, tiled=True)
    scores = attention_scores(query, keys, bias, same, factor)
    peak = jnp.max(scores, axis=-1, keepdims=True)
    logsum = peak + jnp.log(jnp.sum(jnp.exp(scores - peak), axis=-1, keepdims=True))
    chance = jnp.exp(scores - logsum).astype(jnp.bfloat16)
    mixed = (
        jnp.einsum("whij,wjhe->wihe", chance, values, preferred_element_type=jnp.float32)
        .astype(jnp.bfloat16)
        .reshape(tokens, local_width)
    )
    attended = branch_total(jnp.dot(mixed, merge_full, preferred_element_type=jnp.float32))
    middle = hidden_in + per_token[:, 2] * attended
    normed_two, spread_two, rows_two = normalize(middle, per_token[:, 3], per_token[:, 4], width)
    pair_up = jnp.einsum("td,dje->tje", rows_two, expand_full, preferred_element_type=jnp.float32)
    gate = pair_up[:, 0]
    upward = pair_up[:, 1]
    sigma = jax.nn.sigmoid(gate)
    activated = (gate * sigma * upward).astype(jnp.bfloat16)
    fed = branch_total(jnp.dot(activated, shrink_full, preferred_element_type=jnp.float32))
    output = (middle + per_token[:, 5] * fed).astype(jnp.bfloat16)
    upper = out_grad.astype(jnp.float32)
    fed_grad = gather_grad((per_token[:, 5] * upper).astype(jnp.bfloat16))
    act_grad = lax.dot_general(
        fed_grad, shrink_full, (((1,), (1,)), ((), ())), preferred_element_type=jnp.float32
    )
    shrink_grad = lax.dot_general(
        activated, fed_grad, (((0,), (0,)), ((), ())), preferred_element_type=jnp.float32
    )
    slope = sigma * (1.0 + gate * (1.0 - sigma))
    up_grads = jnp.stack([act_grad * upward * slope, act_grad * gate * sigma], axis=1).astype(
        jnp.bfloat16
    )
    expand_grad = jnp.einsum("td,tje->dje", rows_two, up_grads, preferred_element_type=jnp.float32)
    partial_two = jnp.einsum(
        "tje,dje->td", up_grads, expand_full, preferred_element_type=jnp.float32
    )
    upstream_two, norm_two = normalize_back(
        partial_two, normed_two, spread_two, per_token[:, 4], width
    )
    middle_grad = upper + norm_two
    merged_grad = gather_grad((per_token[:, 2] * middle_grad).astype(jnp.bfloat16))
    mixed_grad = (
        lax.dot_general(
            merged_grad, merge_full, (((1,), (1,)), ((), ())), preferred_element_type=jnp.float32
        )
        .astype(jnp.bfloat16)
        .reshape(windows, window, heads_local, HD)
    )
    merge_grad = lax.dot_general(
        mixed, merged_grad, (((0,), (0,)), ((), ())), preferred_element_type=jnp.float32
    )
    again = attention_scores(query, keys, bias, same, factor)
    exact = jnp.exp(again - logsum)
    chance_grad = jnp.einsum(
        "wihe,wjhe->whij", mixed_grad, values, preferred_element_type=jnp.float32
    )
    score_grad = (
        exact * (chance_grad - jnp.sum(exact * chance_grad, axis=-1, keepdims=True))
    ).astype(jnp.bfloat16)
    value_grad = jnp.einsum(
        "whij,wihe->wjhe",
        exact.astype(jnp.bfloat16),
        mixed_grad,
        preferred_element_type=jnp.float32,
    )
    query_grad = (
        jnp.einsum("whij,wjhe->wihe", score_grad, keys, preferred_element_type=jnp.float32) * factor
    )
    keys_grad = (
        jnp.einsum("whij,wihe->wjhe", score_grad, query, preferred_element_type=jnp.float32)
        * factor
    )
    triple_grad = jnp.stack(
        [
            query_grad.reshape(tokens, local_width),
            keys_grad.reshape(tokens, local_width),
            value_grad.reshape(tokens, local_width),
        ],
        axis=1,
    ).astype(jnp.bfloat16)
    bias_grad = lax.all_to_all(score_grad, "mp", split_axis=2, concat_axis=1, tiled=True)
    pair_grad = jnp.einsum(
        "whij,ch->wijc", bias_grad, pair_full, preferred_element_type=jnp.float32
    ).astype(jnp.bfloat16)
    pairwise_grad = jnp.einsum(
        "wijc,whij->ch", pair_input, bias_grad, preferred_element_type=jnp.float32
    )
    attend_grad = jnp.einsum(
        "td,tje->dje", rows_one, triple_grad, preferred_element_type=jnp.float32
    )
    partial_one = jnp.einsum(
        "tje,dje->td", triple_grad, attend_full, preferred_element_type=jnp.float32
    )
    upstream_one, norm_one = normalize_back(
        partial_one, normed_one, spread_one, per_token[:, 1], width
    )
    residue_grad = (middle_grad + norm_one).astype(jnp.bfloat16)
    token_mod_grad = jnp.stack(
        [
            upstream_one,
            upstream_one * normed_one,
            middle_grad * attended,
            upstream_two,
            upstream_two * normed_two,
            upper * fed,
        ],
        axis=1,
    ).reshape(windows, window, 6, local_width)
    mod_grad = jnp.einsum("wts,wtjd->wsjd", pick, token_mod_grad, precision=HIGH)
    modulate_grad = jnp.einsum(
        "wsc,wsjd->cjd", condition.astype(jnp.float32), mod_grad, precision=HIGH
    )
    cond_grad = jnp.einsum(
        "wsjd,cjd->wsc", mod_grad, modulate_full.astype(jnp.float32), precision=HIGH
    )
    sig_before = jax.nn.sigmoid(before)
    before_grad = cond_grad * (sig_before * (1.0 + before * (1.0 - sig_before)))
    class_grad = jnp.einsum("wsn,wsc->nc", class_pick, before_grad, precision=HIGH)
    shared = lax.psum((pairwise_grad, class_grad), "mp")
    sums = (
        lax.psum_scatter(attend_grad, "dp", scatter_dimension=0, tiled=True),
        lax.psum_scatter(merge_grad, "dp", scatter_dimension=1, tiled=True),
        lax.psum_scatter(expand_grad, "dp", scatter_dimension=0, tiled=True),
        lax.psum_scatter(shrink_grad, "dp", scatter_dimension=1, tiled=True),
        lax.psum_scatter(modulate_grad, "dp", scatter_dimension=0, tiled=True),
        lax.psum_scatter(shared[0], "dp", scatter_dimension=0, tiled=True),
        lax.psum_scatter(shared[1], "dp", scatter_dimension=1, tiled=True),
    )
    rates = (
        2.0 / math.sqrt(D),
        2.0 / math.sqrt(D // 8),
        2.0 / math.sqrt(D),
        2.0 / math.sqrt(FF),
        2.0 / math.sqrt(CDIM),
        2.0 / math.sqrt(PAIR),
        2.0,
    )
    masters = (
        attend_weight,
        merge_weight,
        expand_weight,
        shrink_weight,
        modulate_weight,
        pair_weight,
        class_weight,
    )
    states = (
        attend_state,
        merge_state,
        expand_state,
        shrink_state,
        modulate_state,
        pair_state,
        class_state,
    )
    results = []
    for index in range(7):
        updated, tracked = adamw(masters[index], states[index], sums[index], rates[index])
        results.append(updated)
        results.append(tracked)
    return (
        output,
        residue_grad,
        pair_grad,
        results[0],
        results[1],
        results[2],
        results[3],
        results[4],
        results[5],
        results[6],
        results[7],
        results[8],
        results[9],
        results[10],
        results[11],
        results[12],
        results[13],
    )


RATES = (
    2.0 / math.sqrt(D),
    2.0 / math.sqrt(D // 8),
    2.0 / math.sqrt(D),
    2.0 / math.sqrt(FF),
    2.0 / math.sqrt(CDIM),
    2.0 / math.sqrt(PAIR),
    2.0,
)
f32 = jnp.float32
bf16 = jnp.bfloat16
NT = (((1,), (1,)), ((), ()))
NN = (((1,), (0,)), ((), ()))
TN = (((0,), (0,)), ((), ()))
HEADS = 12
GROUP = 16
UNIT = 64
CHUNK = 16
PAIRS = 8


def mm(a, b, dims=NN, precision=None):
    return lax.dot_general(a, b, dims, precision=precision, preferred_element_type=f32)


def head_mask(count):
    row = lax.broadcasted_iota(jnp.int32, (count, GROUP, D), 1)
    col = lax.broadcasted_iota(jnp.int32, (count, GROUP, D), 2) // HD
    return row == col


def spread_heads(rows):
    count = rows.shape[0]
    wide = jnp.broadcast_to(rows.astype(f32)[:, None, :], (count, GROUP, D))
    return jnp.where(head_mask(count), wide, 0.0).astype(bf16).reshape(count * GROUP, D)


def merge_heads(wide):
    count = wide.shape[0] // GROUP
    return jnp.sum(jnp.where(head_mask(count), wide.reshape(count, GROUP, D), 0.0), axis=1)


class Net:
    def __init__(self, send_sems, recv_sems):
        self.d = lax.axis_index("dp")
        self.m = lax.axis_index("mp")
        core = self.d % 2
        x = (self.d // 2) % 2
        y = self.d // 4
        self.core = core
        self.chip = self.d // 2
        self.chips = [self.chip, y * 2 + 1 - x, (1 - y) * 2 + x, (1 - y) * 2 + 1 - x]
        self.partner = self.chip * 2 + 1 - core
        self.send_sems = send_sems
        self.recv_sems = recv_sems
        self.sent = []
        self.open = []
        self.base = 0

    def z(self, t):
        return (self.m + t) % 4

    def peer(self, r):
        return self.chips[r] * 2 + self.core

    def sems(self, count):
        base = self.base
        self.base = base + count
        return base

    def barrier(self):
        sem = pltpu.get_barrier_semaphore()
        targets = [(self.d, self.z(t)) for t in (1, 2, 3)]
        targets += [(self.peer(r), self.m) for r in (1, 2, 3)] + [(self.partner, self.m)]
        for target in targets:
            pl.semaphore_signal(
                sem, inc=1, device_id=target, device_id_type=pl.DeviceIdType.MESH
            )
        pl.semaphore_wait(sem, len(targets))

    def copy(self, src, dst, recv, target, send=None):
        send = len(self.sent) if send is None else send
        return pltpu.make_async_remote_copy(
            src_ref=src,
            dst_ref=dst,
            send_sem=self.send_sems.at[send],
            recv_sem=self.recv_sems.at[recv],
            device_id=target,
            device_id_type=pl.DeviceIdType.MESH,
        )

    def send(self, src, dst, recv, target):
        made = self.copy(src, dst, recv, target)
        made.start()
        self.sent.append(made)
        self.open.append(made)
        return made

    def wait(self, dst, recv):
        self.copy(dst, dst, recv, (self.partner, self.m), 0).wait_recv()

    def drain(self):
        for made in self.open:
            made.wait_send()

    def settle(self, made):
        made.wait_send()
        self.open = [other for other in self.open if other is not made]


class Spread:
    def __init__(self, net, slot):
        self.net, self.slot, self.base = net, slot, net.sems(7)

    def start(self, src=None):
        net = self.net
        own = self.slot(net.d)
        src = own if src is None else src
        for r in (1, 2, 3):
            net.send(src, own, self.base + r, (net.peer(r), net.m))
        net.send(src, own, self.base, (net.partner, net.m))

    def forward(self, r):
        net = self.net
        slot = self.slot(net.peer(r))
        net.wait(slot, self.base + r)
        return net.send(slot, slot, self.base + 3 + r, (net.partner, net.m))

    def finish(self):
        net = self.net
        net.wait(self.slot(net.partner), self.base)
        for r in (1, 2, 3):
            net.wait(self.slot(net.chips[r] * 2 + 1 - net.core), self.base + 3 + r)


class Zline:
    def __init__(self, net, slot):
        self.net, self.slot, self.base = net, slot, net.sems(4)

    def send(self, t, src):
        net = self.net
        net.send(src, self.slot(net.m), self.base + net.m, (net.d, net.z(t)))

    def wait(self, t):
        net = self.net
        source = net.z(t)
        net.wait(self.slot(source), self.base + source)
        return source


def layer_kernel(
    ms, am, es, xp, gp, pair, sinus, pick, mask,
    out_o, res_o, ds_o, pw_o, am_o, es_o, mod_o, pc_o,
    msg, amg, esg, xg, gg, modu, modg, modf, bpg, pb, bias, n1, sp1, r1,
    kf, vf, qf, pr, mix, att, mid, n2, sp2, r2, fg, act, upg, fp, fl, p2, p2l, p2o, fpo,
    esp, epl, exl, eso, dkv, dkf, dvf, dqf, mgd, l2, rhs2, p1, p1l,
    amp, axl, aso, azs, azl, mps, mpl, mrg, pws, pwl, pwx, pwy, pco, pcl,
    ops, opl, rps, rpl, ctf, cfull,
    send_sems, recv_sems, pair_sems,
):
    net = Net(send_sems, recv_sems)
    d, m = net.d, net.m
    net.barrier()

    chunks = 16
    slots = pb.shape[0]

    def pair_copy(step):
        c = step % chunks
        return pltpu.make_async_copy(
            pair.at[c // 8, pl.ds((c % 8) * PAIRS, PAIRS)],
            pb.at[step % slots],
            pair_sems.at[step % slots],
        )

    for step in range(slots):
        pair_copy(step).start()

    ms_all = Spread(net, lambda i: msg.at[i])
    am_line = Zline(net, lambda s: amg.at[s, d])
    am_all = [Spread(net, lambda i, t=t: amg.at[net.z(t), i]) for t in range(4)]
    x_line = Zline(net, lambda s: xg.at[s])
    g_line = Zline(net, lambda s: gg.at[s])
    mod_line = Zline(net, lambda s: modg.at[s])
    bp_all = Spread(net, lambda i: bpg.at[i])
    es_all = Spread(net, lambda i: esg.at[i])

    ms_all.start(ms)
    for t in (1, 2, 3):
        am_line.send(t, am)
    am_all[0].start(am)
    for t in (1, 2, 3):
        x_line.send(t, xp)
    msg[d] = ms[...]
    amg[m, d] = am[...]
    esg[d] = es[...]
    xg[m] = xp[...]
    gg[m] = gp[...]
    for r in (1, 2, 3):
        ms_all.forward(r)
    ms_all.finish()

    slab = msg[:, :, 0:128].reshape(256, 128)
    select = (
        lax.broadcasted_iota(jnp.int32, (GROUP, 128), 1)
        == lax.broadcasted_iota(jnp.int32, (GROUP, 128), 0) + 64
    ) & (lax.broadcasted_iota(jnp.int32, (GROUP, 128), 0) < HEADS)
    pw_o[...] = mm(jnp.where(select, 1.0, 0.0).astype(bf16), slab, NT).astype(bf16)
    before = sinus[...] + mm(pick[...], slab, NT)
    condition = (before * jax.nn.sigmoid(before)).astype(bf16)
    modu[...] = mm(condition, msg[:, :, 128:1280].reshape(256, 1152))
    for t in (1, 2, 3):
        mod_line.send(t, modu)
    modg[m] = modu[...]
    bpg[d] = jnp.concatenate([before, pick[...].astype(f32)], axis=-1)

    def bias_chunk(step):
        slot = step % slots
        pair_copy(step).wait()

        def one(i, carry):
            part = mm(pw_o[...], pb[slot, i], NT)
            at = pl.multiple_of((step % 8) * PAIRS * GROUP + i * GROUP, GROUP)
            bias[step // 8, pl.ds(at, GROUP), :] = part.astype(bf16)
            return carry

        lax.fori_loop(0, PAIRS, one, 0, unroll=4)
        pair_copy(step + slots).start()

    for step in range(4):
        bias_chunk(step)
    for t in (1, 3, 2):
        am_line.wait(t)
        am_all[t].start()
        first = {1: 4, 3: 6, 2: 8}[t]
        bias_chunk(first)
        bias_chunk(first + 1)
    for r in (1, 2, 3):
        am_all[0].forward(r)
    es_all.start(es)
    for t in (1, 2, 3):
        g_line.send(t, gp)
    bp_all.start()
    bias_chunk(10)
    bias_chunk(11)
    for r in (1, 2, 3):
        am_all[1].forward(r)
    for step in range(12, 16):
        bias_chunk(step)

    for t in (1, 2, 3):
        mod_line.wait(t)
    for j in range(6):
        modf[j] = jnp.concatenate([modg[s, :, 192 * j : 192 * j + 192] for s in range(4)], axis=-1)
    for t in (1, 2, 3):
        x_line.wait(t)

    def unpack(ref, w, unit):
        parts = []
        for s in range(4):
            parts.append(ref[s, pl.ds(w * 256 + unit * UNIT, UNIT), :].astype(f32))
            low = ref[s, pl.ds(512 + unit * UNIT, UNIT), :].astype(f32)
            parts.append(low[:, 64 * w : 64 * w + 64])
        return jnp.concatenate(parts, axis=-1)

    def norm(v):
        center = jnp.mean(v, axis=-1, keepdims=True)
        spread = lax.rsqrt(jnp.mean(v * v, axis=-1, keepdims=True) - center * center + NORM_EPS)
        return (v - center) * spread, spread

    for w in range(2):

        def first_norm(unit, carry, w=w):
            v = unpack(xg, w, unit)
            rows = pl.ds(pl.multiple_of(w * 256 + unit * UNIT, UNIT), UNIT)
            normed, spread = norm(v)
            n1[rows, :] = normed
            sp1[rows, :] = jnp.broadcast_to(spread, (UNIT, 128))
            shift = modf[0, pl.ds(w * 4 + unit, 1), :]
            scale = modf[1, pl.ds(w * 4 + unit, 1), :]
            r1[rows, :] = (normed * (1.0 + scale) + shift).astype(bf16)
            return carry

        lax.fori_loop(0, 4, first_norm, 0)

    for t in (3, 2):
        for r in (1, 2, 3):
            am_all[t].forward(r)
    for t in (0, 1, 3, 2):
        am_all[t].finish()

    def own(w):
        return pl.ds(pl.multiple_of(w * 256 + m * UNIT, UNIT), UNIT)

    def weight(s, lo, hi):
        return amg[s, :, :, lo:hi].reshape(D, hi - lo)

    r1_own = jnp.concatenate([r1[own(0), :], r1[own(1), :]], axis=0)
    qf[...] = jnp.concatenate(
        [mm(r1_own, weight(s, 384, 768))[:, 0:192] for s in range(4)], axis=-1
    ).astype(bf16)
    for w in range(2):
        rows = slice(w * 256, w * 256 + 256)
        both = [mm(r1[rows, :], weight(s, 0, 384)) for s in range(4)]
        kf[rows, :] = jnp.concatenate([v[:, 0:192] for v in both], axis=-1).astype(bf16)
        vf[rows, :] = jnp.concatenate([v[:, 192:384] for v in both], axis=-1).astype(bf16)

    factor = HD ** (-0.5)

    def attend(c, carry):
        w = c // 4
        mine = pl.ds(pl.multiple_of(c * CHUNK, CHUNK), CHUNK)
        keys = pl.ds(pl.multiple_of(w * 256, 256), 256)
        wide = pl.ds(pl.multiple_of((c % 4) * CHUNK * GROUP, CHUNK * GROUP), CHUNK * GROUP)
        scores = mm(spread_heads(qf[mine, :]), kf[keys, :], NT) * factor
        scores = scores + bias[w, wide, :].astype(f32) + mask[pl.ds(w, 1), :]
        peak = jnp.max(scores, axis=-1, keepdims=True)
        expo = jnp.exp(scores - peak)
        chance = expo / jnp.sum(expo, axis=-1, keepdims=True)
        pr[w, wide, :] = chance
        mix[mine, :] = merge_heads(mm(chance.astype(bf16), vf[keys, :])).astype(bf16)
        return carry

    lax.fori_loop(0, 8, attend, 0)
    es_sent = [es_all.forward(r) for r in (1, 2, 3)]

    mixed = mix[...]
    blank = jnp.zeros((128, 192), bf16)
    attended = mm(
        jnp.concatenate([blank, mixed[:, 0:192]], axis=-1), weight(0, 384, 768), NT
    )
    for s in range(1, 4):
        part = jnp.concatenate([blank, mixed[:, 192 * s : 192 * s + 192]], axis=-1)
        attended = attended + mm(part, weight(s, 384, 768), NT)
    att[...] = attended

    def mod_row(j, w):
        return modf[j, pl.ds(w * 4 + m, 1), :]

    for w in range(2):
        half = slice(w * UNIT, w * UNIT + UNIT)
        middle = unpack(xg, w, m) + mod_row(2, w) * att[half, :]
        mid[half, :] = middle
        normed, spread = norm(middle)
        n2[half, :] = normed
        sp2[half, :] = jnp.broadcast_to(spread, (UNIT, 128))
        r2[m, half, :] = (normed * (1.0 + mod_row(4, w)) + mod_row(3, w)).astype(bf16)

    r2_line = Zline(net, lambda s: r2.at[s])
    for t in (1, 3, 2):
        r2_line.send(t, r2.at[m])
    for t in (1, 2, 3):
        g_line.wait(t)
    for s in range(4):
        for w in range(2):
            half = slice(w * UNIT, w * UNIT + UNIT)
            upper = unpack(gg, w, s)
            fg[s, half, :] = (modf[5, w * 4 + s : w * 4 + s + 1, :] * upper).astype(bf16)
    es_all.finish()

    p2_line = Zline(net, lambda s: p2l.at[s])
    f_line = Zline(net, lambda s: fl.at[s])

    def feed(s):
        expand = esg[:, :, 0:1536].reshape(D, 1536)
        shrink = esg[:, :, 1536:2304].reshape(D, 768)
        up = mm(r2[s], expand)
        gate = up[:, 0:768]
        upward = up[:, 768:1536]
        act_grad = mm(fg[s], shrink)
        sigma = jax.nn.sigmoid(gate)
        activated = (gate * sigma * upward).astype(bf16)
        act[s] = activated
        slope = sigma * (1.0 + gate * (1.0 - sigma))
        grads = jnp.concatenate(
            [(act_grad * upward * slope).astype(bf16), (act_grad * gate * sigma).astype(bf16)],
            axis=-1,
        )
        upg[s] = grads
        return mm(grads, expand, NT), mm(activated, shrink, NT)

    partial, fed = feed(m)
    p2o[...] = partial
    fpo[...] = fed
    for t in (1, 3, 2):
        source = r2_line.wait(t)
        partial, fed = feed(source)
        p2[source] = partial.astype(bf16)
        p2_line.send(t, p2.at[source])
        fp[source] = fed.astype(bf16)
    for t in (1, 3, 2):
        f_line.send(t, fp.at[net.z(t)])

    def put_es(left, right, at):
        for h in range(2):
            value = mm(left[:, :, 384 * h : 384 * h + 384].reshape(512, 384), right, TN)
            for i in range(4):
                part = value[96 * i : 96 * i + 96, :].astype(bf16)
                esp[i % 2, 2 * h + i // 2, :, at : at + 768] = part

    put_es(r2, upg[:, :, 0:768].reshape(512, 768), 0)
    put_es(r2, upg[:, :, 768:1536].reshape(512, 768), 768)
    put_es(fg, act[...].reshape(512, 768), 1536)
    for made in es_sent:
        net.settle(made)
    es_pair = net.sems(1)
    net.send(esp.at[1 - net.core], epl, es_pair, (net.partner, m))

    for t in (1, 3, 2):
        p2_line.wait(t)

    def norm_back(upstream, normed, spread, scale):
        inner = upstream * (1.0 + scale)
        first = jnp.mean(inner, axis=-1, keepdims=True)
        second = jnp.mean(inner * normed, axis=-1, keepdims=True)
        return spread * (inner - first - normed * second)

    def unit_sum(v):
        return jnp.sum(v, axis=0, keepdims=True)

    own_sums = [[None] * 6, [None] * 6]
    for w in range(2):
        half = slice(w * UNIT, w * UNIT + UNIT)
        upstream = p2o[half, :]
        for t in (1, 3, 2):
            upstream = upstream + p2l[net.z(t), half, :].astype(f32)
        normed = n2[half, :]
        back = norm_back(upstream, normed, sp2[half, 0:1], mod_row(4, w))
        grad = unpack(gg, w, m) + back
        p2o[half, :] = grad
        own_sums[w][2] = unit_sum(grad * att[half, :])
        own_sums[w][3] = unit_sum(upstream)
        own_sums[w][4] = unit_sum(upstream * normed)
        l2[slice(128 + w * UNIT, 128 + w * UNIT + UNIT), :] = (mod_row(2, w) * grad).astype(bf16)
        l2[half, :] = r1[own(w), :]
    merged_grad = l2[128:256, :]
    mgd[...] = jnp.concatenate(
        [mm(merged_grad, weight(s, 384, 768))[:, 192:384] for s in range(4)], axis=-1
    ).astype(bf16)

    net.wait(epl, es_pair)
    es_chip = net.sems(4)
    for r in (1, 2, 3, 0):
        total = esp[net.core, net.chips[r]].astype(f32) + epl[net.chips[r]].astype(f32)
        if r == 0:
            eso[...] = total
        else:
            esp[net.core, net.chips[r]] = total.astype(bf16)
            net.send(
                esp.at[net.core, net.chips[r]], exl.at[r - 1], es_chip + r, (net.peer(r), m)
            )

    dkf[...] = jnp.zeros_like(dkf)
    dvf[...] = jnp.zeros_like(dvf)

    def attend_back(c, carry):
        w = c // 4
        mine = pl.ds(pl.multiple_of(c * CHUNK, CHUNK), CHUNK)
        keys = pl.ds(pl.multiple_of(w * 256, 256), 256)
        wide = pl.ds(pl.multiple_of((c % 4) * CHUNK * GROUP, CHUNK * GROUP), CHUNK * GROUP)
        grad = spread_heads(mgd[mine, :])
        chance = pr[w, wide, :]
        chance_grad = mm(grad, vf[keys, :], NT)
        inner = jnp.sum(chance * chance_grad, axis=-1, keepdims=True)
        score = (chance * (chance_grad - inner)).astype(bf16)
        ds_o[w, wide, :] = score
        dqf[mine, :] = (merge_heads(mm(score, kf[keys, :])) * factor).astype(bf16)
        dvf[keys, :] += mm(chance.astype(bf16), grad, TN)
        dkf[keys, :] += mm(score, spread_heads(qf[mine, :]), TN) * factor
        return carry

    lax.fori_loop(0, 8, attend_back, 0)

    o_line = Zline(net, lambda s: opl.at[s])

    def pack(line, value, ref):
        for s in range(4):
            part = value[:, 192 * s : 192 * s + 192]
            ref[s, 0:128, :] = part[:, 0:128].astype(bf16)
            low = part[:, 128:192]
            ref[s, 128:192, :] = jnp.concatenate([low[0:64], low[64:128]], axis=-1).astype(bf16)
        for t in (1, 3, 2):
            line.send(t, ref.at[net.z(t)])

    def unpack_out(line, ref, mine, to):
        for t in (0, 1, 3, 2):
            s = net.z(t)
            block = mine if t == 0 else ref
            if t:
                line.wait(t)
            for w in range(2):
                rows = pl.ds(pl.multiple_of(w * 256 + s * UNIT, UNIT), UNIT)
                high = block[s, w * UNIT : w * UNIT + UNIT, :].astype(f32)
                low = block[s, 128:192, :].astype(f32)[:, 64 * w : 64 * w + 64]
                to[rows, :] = jnp.concatenate([high, low], axis=-1).astype(bf16)

    for t in (1, 3, 2):
        f_line.wait(t)
    done = []
    for w in range(2):
        half = slice(w * UNIT, w * UNIT + UNIT)
        fed = fpo[half, :]
        for t in (1, 3, 2):
            fed = fed + fl[net.z(t), half, :].astype(f32)
        own_sums[w][5] = unit_sum(unpack(gg, w, m) * fed)
        done.append(mid[half, :] + mod_row(5, w) * fed)
    pack(o_line, jnp.concatenate(done, axis=0), ops)

    for s in range(4):
        cols = slice(192 * s, 192 * s + 192)
        dkv[s] = jnp.concatenate([dkf[:, cols], dvf[:, cols]], axis=-1).astype(bf16)
        rhs2[s, 0:128, :] = jnp.concatenate([dqf[:, cols], blank], axis=-1)
        rhs2[s, 128:256, :] = jnp.concatenate([blank, mix[:, cols]], axis=-1)
    am_pair = net.sems(4)

    def apl(t):
        return esg.at[pl.ds(4 * (t // 3), 4), :, 768 * (t % 3) : 768 * (t % 3) + 768]

    for t in (1, 3, 2, 0):
        s = net.z(t)
        for h in range(2):
            cols = slice(384 * h, 384 * h + 384)
            for left, right, at in ((r1, dkv, 0), (l2, rhs2, 384)):
                value = mm(left[:, cols], right[s], TN)
                for i in range(4):
                    part = value[96 * i : 96 * i + 96, :].astype(bf16)
                    amp[s, i % 2, 2 * h + i // 2, :, at : at + 384] = part
        net.send(amp.at[s, 1 - net.core], apl(t), am_pair + t, (net.partner, m))

    for w in range(2):
        rows = slice(w * 256, w * 256 + 256)
        total = mm(dkv[0, rows, :], weight(0, 0, 384), NT)
        for s in range(1, 4):
            total = total + mm(dkv[s, rows, :], weight(s, 0, 384), NT)
        dkf[rows, :] = total
    total = mm(rhs2[0, 0:128, :], weight(0, 384, 768), NT)
    for s in range(1, 4):
        total = total + mm(rhs2[s, 0:128, :], weight(s, 384, 768), NT)
    for w in range(2):
        dkf[own(w), :] += total[w * UNIT : w * UNIT + UNIT, :]
    p1_line = Zline(net, lambda s: p1l.at[s])
    for t in (1, 3, 2):
        s = net.z(t)
        for w in range(2):
            rows = pl.ds(pl.multiple_of(w * 256 + s * UNIT, UNIT), UNIT)
            p1[s, w * UNIT : w * UNIT + UNIT, :] = dkf[rows, :].astype(bf16)
        p1_line.send(t, p1.at[s])

    sums = [[], []]
    for u in range(8):
        rows = slice(u * UNIT, u * UNIT + UNIT)
        sums[0].append(unit_sum(dkf[rows, :]))
        sums[1].append(unit_sum(dkf[rows, :] * n1[rows, :]))
    row = lax.broadcasted_iota(jnp.int32, (8, D), 0)
    table = [jnp.concatenate(sums[0], axis=0), jnp.concatenate(sums[1], axis=0)]
    for j in range(2, 6):
        first = jnp.broadcast_to(own_sums[0][j], (8, D))
        second = jnp.broadcast_to(own_sums[1][j], (8, D))
        table.append(jnp.where(row == m, first, jnp.where(row == m + 4, second, 0.0)))
    mod_sum = Zline(net, lambda s: mpl.at[s])
    for s in range(4):
        mps[s] = jnp.concatenate([v[:, 192 * s : 192 * s + 192] for v in table], axis=-1)
    for t in (1, 3, 2):
        mod_sum.send(t, mps.at[net.z(t)])

    def pair_chunk(step, acc):
        slot = step % slots
        pair_copy(step).wait()

        def one(i, acc):
            at = pl.multiple_of((step % 8) * PAIRS * GROUP + i * GROUP, GROUP)
            return acc + mm(ds_o[(step - 16) // 8, pl.ds(at, GROUP), :], pb[slot, i])

        acc = lax.fori_loop(0, PAIRS, one, acc, unroll=4)
        if step + slots < 2 * chunks:
            pair_copy(step + slots).start()
        return acc

    pairwise = jnp.zeros((GROUP, 256), f32)
    am_chip = net.sems(16)
    step = 16
    for t in (1, 3, 2, 0):
        s = net.z(t)
        net.wait(apl(t), am_pair + t)
        base, cols = 4 * (t // 3), slice(768 * (t % 3), 768 * (t % 3) + 768)
        for r in (1, 2, 3, 0):
            total = amp[s, net.core, net.chips[r]].astype(f32)
            total = total + esg[base + net.chips[r], :, cols].astype(f32)
            if r == 0:
                aso[s] = total
            else:
                amp[s, net.core, net.chips[r]] = total.astype(bf16)
                net.send(
                    amp.at[s, net.core, net.chips[r]],
                    axl.at[s, r - 1],
                    am_chip + 4 * t + r,
                    (net.peer(r), m),
                )
        for _ in range(4):
            pairwise = pair_chunk(step, pairwise)
            step += 1

    for r in (1, 2, 3):
        bp_all.forward(r)
    bp_all.finish()

    wide = jnp.concatenate([pairwise, jnp.zeros((112, 256), f32)], axis=0).T
    for i in range(8):
        pws[i % 2, i // 2] = wide[32 * i : 32 * i + 32, :]
    pw_pair = net.sems(1)
    net.send(pws.at[1 - net.core], pwl, pw_pair, (net.partner, m))

    for t in (1, 3, 2):
        mod_sum.wait(t)
    mod_grad = mps[m]
    for t in (1, 3, 2):
        mod_grad = mod_grad + mpl[net.z(t)]
    mrg[d] = mod_grad
    mr_all = Spread(net, lambda i: mrg.at[i])
    mr_all.start()

    for t in (1, 3, 2):
        p1_line.wait(t)
    r_line = Zline(net, lambda s: rpl.at[s])
    done = []
    for w in range(2):
        half = slice(w * UNIT, w * UNIT + UNIT)
        upstream = dkf[own(w), :]
        for t in (1, 3, 2):
            upstream = upstream + p1l[net.z(t), half, :].astype(f32)
        back = norm_back(upstream, n1[own(w), :], sp1[own(w), :][:, 0:1], mod_row(1, w))
        done.append(p2o[half, :] + back)
    pack(r_line, jnp.concatenate(done, axis=0), rps)

    total = eso[...]
    for r in (1, 2, 3):
        net.wait(exl.at[r - 1], es_chip + r)
        total = total + exl[r - 1].astype(f32)
    es_o[...] = total

    net.wait(pwl, pw_pair)
    pw_chip = net.sems(4)
    for r in (1, 2, 3):
        pwx[r] = pws[net.core, net.chips[r]] + pwl[net.chips[r]]
        net.send(pwx.at[r], pwy.at[r], pw_chip + r, (net.peer(r), m))
    pair_sum = pws[net.core, net.chip] + pwl[net.chip]

    am_z = Zline(net, lambda s: azl.at[s])
    for t in (1, 3, 2, 0):
        s = net.z(t)
        total = aso[s]
        for r in (1, 2, 3):
            net.wait(axl.at[s, r - 1], am_chip + 4 * t + r)
            total = total + axl[s, r - 1].astype(f32)
        if t:
            azs[s] = total.astype(bf16)
            am_z.send(t, azs.at[s])
        else:
            aso[s] = total
        if t == 1:
            for r in (1, 2, 3):
                mr_all.forward(r)

    mr_all.finish()
    before = bpg[:, :, 0:256].reshape(64, 256)
    sig = jax.nn.sigmoid(before)
    condition = (before * sig).astype(bf16).astype(f32)
    picks = bpg[:, :, 256:384].reshape(64, 128)
    grads = mrg[...].reshape(64, 1152)
    ctf[...] = condition.T
    mod_o[...] = mm(ctf[pl.ds(pl.multiple_of(d * 32, 32), 32), :], grads, NN, HIGH)
    cond_grad = mm(grads, msg[:, :, 128:1280].reshape(256, 1152).astype(f32), NT, HIGH)
    before_grad = cond_grad * (sig * (1.0 + before * (1.0 - sig)))
    cfull[...] = mm(before_grad, picks, TN, HIGH)
    for r in (1, 2, 3):
        net.wait(pwy.at[r], pw_chip + r)
        pair_sum = pair_sum + pwy[r]
    pco[...] = jnp.concatenate(
        [pair_sum, cfull[pl.ds(pl.multiple_of(d * 32, 32), 32), :]], axis=-1
    )
    pc_line = Zline(net, lambda s: pcl.at[s])
    for t in (1, 3, 2):
        pc_line.send(t, pco)

    unpack_out(o_line, opl, ops, out_o)
    unpack_out(r_line, rpl, rps, res_o)
    total = aso[m]
    for t in (1, 3, 2):
        total = total + azl[am_z.wait(t)].astype(f32)
    am_o[...] = total
    total = pco[...]
    for t in (1, 3, 2):
        total = total + pcl[pc_line.wait(t)]
    pc_o[...] = total
    net.drain()


def layer_call(*args):
    V = pltpu.VMEM
    scratch = [
        V((8, 32, 1280), bf16), V((4, 8, 96, 768), bf16), V((8, 96, 2304), bf16),
        V((4, 768, 128), bf16), V((4, 768, 128), bf16),
        V((8, 1152), f32), V((4, 8, 1152), f32), V((6, 8, 768), f32), V((8, 8, 384), f32),
        V((2, PAIRS, 256, 256), bf16), V((2, 1024, 256), bf16),
        V((512, 768), f32), V((512, 128), f32), V((512, 768), bf16),
        V((512, 768), bf16), V((512, 768), bf16), V((128, 768), bf16), V((2, 1024, 256), f32),
        V((128, 768), bf16), V((128, 768), f32), V((128, 768), f32), V((128, 768), f32),
        V((128, 128), f32),
        V((4, 128, 768), bf16), V((4, 128, 768), bf16), V((4, 128, 768), bf16),
        V((4, 128, 1536), bf16), V((4, 128, 768), bf16), V((4, 128, 768), bf16),
        V((4, 128, 768), bf16), V((4, 128, 768), bf16), V((128, 768), f32), V((128, 768), f32),
        V((2, 4, 96, 2304), bf16), V((4, 96, 2304), bf16), V((3, 96, 2304), bf16),
        V((96, 2304), f32),
        V((4, 512, 384), bf16), V((512, 768), f32), V((512, 768), f32), V((128, 768), bf16),
        V((128, 768), bf16), V((256, 768), bf16), V((4, 256, 384), bf16),
        V((4, 128, 768), bf16), V((4, 128, 768), bf16),
        V((4, 2, 4, 96, 768), bf16), V((4, 3, 96, 768), bf16),
        V((4, 96, 768), f32), V((4, 96, 768), bf16), V((4, 96, 768), bf16),
        V((4, 8, 1152), f32), V((4, 8, 1152), f32), V((8, 8, 1152), f32),
        V((2, 4, 32, 128), f32), V((4, 32, 128), f32), V((4, 32, 128), f32), V((4, 32, 128), f32),
        V((32, 256), f32), V((4, 32, 256), f32),
        V((4, 192, 128), bf16), V((4, 192, 128), bf16), V((4, 192, 128), bf16),
        V((4, 192, 128), bf16), V((256, 64), f32), V((256, 128), f32),
        pltpu.SemaphoreType.DMA((160,)), pltpu.SemaphoreType.DMA((160,)),
        pltpu.SemaphoreType.DMA((2,)),
    ]
    whole = pl.BlockSpec(memory_space=pltpu.VMEM)
    outs = (
        ((512, 192), bf16), ((512, 192), bf16), ((2, 1024, 256), bf16), ((16, 256), bf16),
        ((96, 768), f32), ((96, 2304), f32), ((32, 1152), f32), ((32, 256), f32),
    )
    return pl.pallas_call(
        layer_kernel,
        out_shape=tuple(jax.ShapeDtypeStruct(s, t) for s, t in outs),
        in_specs=[pl.BlockSpec(memory_space=pl.ANY) if i == 5 else whole for i in range(9)],
        out_specs=(whole,) * len(outs),
        scratch_shapes=scratch,
        compiler_params=pltpu.CompilerParams(
            collective_id=0, has_side_effects=True, vmem_limit_bytes=67043328
        ),
        name="layer",
    )(*args)


def pair_kernel(ds, pw, out):
    for i in range(8):
        out[0, i] = mm(ds[0, GROUP * i : GROUP * i + GROUP, :], pw[...], TN).astype(bf16)


def pair_call(ds, pw):
    return pl.pallas_call(
        pair_kernel,
        grid=(2, 8),
        out_shape=jax.ShapeDtypeStruct((2, 64, 256, 256), bf16),
        in_specs=[
            pl.BlockSpec((1, 128, 256), lambda w, i: (w, i, 0)),
            pl.BlockSpec((16, 256), lambda w, i: (0, 0)),
        ],
        out_specs=pl.BlockSpec((1, 8, 256, 256), lambda w, i: (w, i, 0, 0)),
        name="pair",
    )(ds, pw)


def fast_local(
    residues, pair_input, out_grad, bucket_layout, time_bins, fold_class,
    attend_weight, attend_state, merge_weight, merge_state, expand_weight, expand_state,
    shrink_weight, shrink_state, modulate_weight, modulate_state, pair_weight, pair_state,
    class_weight, class_state,
):
    m = lax.axis_index("mp")
    classes = class_weight.shape[0]
    am = jnp.concatenate(
        [attend_weight[:, 1], attend_weight[:, 2], attend_weight[:, 0], merge_weight.T], axis=1
    ).astype(bf16)
    es = jnp.concatenate(
        [expand_weight[:, 0], expand_weight[:, 1], shrink_weight.T], axis=1
    ).astype(bf16)
    ms = jnp.concatenate(
        [
            jnp.pad(class_weight.T, ((0, 0), (0, 64 - classes))),
            jnp.pad(pair_weight, ((0, 0), (0, 52))),
            modulate_weight.reshape(32, 1152),
        ],
        axis=1,
    ).astype(bf16)

    def packed(v):
        low = v[:, 128:]
        return jnp.concatenate([v[:, :128], jnp.concatenate([low[:256], low[256:]], axis=1)], axis=0)

    table = jnp.asarray(PATTERNS)
    layout = (bucket_layout[:, None] == jnp.arange(5, dtype=jnp.int32)).astype(jnp.int32)
    unit_slot = jnp.sum(layout[:, :, None] * table[None], axis=1)
    pick_slot = (unit_slot[..., None] == jnp.arange(4, dtype=jnp.int32)).astype(jnp.int32)
    unit_bin = jnp.sum(pick_slot * time_bins[:, None, :], axis=-1).reshape(8)
    unit_class = jnp.sum(pick_slot * fold_class[:, None, :], axis=-1).reshape(8)
    sinus = time_features(unit_bin, 256)
    pick = (unit_class[:, None] == jnp.arange(128, dtype=jnp.int32)).astype(bf16)
    mine = jnp.sum(
        unit_slot * (jnp.arange(4, dtype=jnp.int32)[None] == m).astype(jnp.int32),
        axis=1,
        keepdims=True,
    )
    seen = jnp.where(unit_slot == mine, 0.0, MASKED)
    mask = jnp.broadcast_to(seen[:, :, None], (2, 4, UNIT)).reshape(2, 256)

    out, res, ds, pw, am_g, es_g, mod_g, pc_g = layer_call(
        ms, am, es, packed(residues), packed(out_grad), pair_input, sinus, pick, mask
    )
    pair_grad = pair_call(ds, pw)
    grads = (
        jnp.stack([am_g[:, 384:576], am_g[:, 0:192], am_g[:, 192:384]], axis=1),
        am_g[:, 576:768].T,
        jnp.stack([es_g[:, 0:768], es_g[:, 768:1536]], axis=1),
        es_g[:, 1536:2304].T,
        mod_g.reshape(32, 6, 192),
        pc_g[:, 0:HEADS],
        pc_g[:, 128 : 128 + classes].T,
    )
    masters = (
        attend_weight, merge_weight, expand_weight, shrink_weight, modulate_weight, pair_weight,
        class_weight,
    )
    states = (
        attend_state, merge_state, expand_state, shrink_state, modulate_state, pair_state,
        class_state,
    )
    results = []
    for master, state, grad, rate in zip(masters, states, grads, RATES):
        results.extend(adamw(master, state, grad, rate))
    return (out, res, pair_grad, *results)


def solution(mesh):
    quick = mesh.shape["dp"] == 8 and mesh.shape["mp"] == 4
    placed = (
        P("dp", "mp"),
        P("dp", "mp", None, None),
        P("dp", "mp"),
        P("dp"),
        P("dp", None),
        P("dp", None),
        P("dp", None, "mp"),
        P(None, "dp", None, "mp"),
        P("mp", "dp"),
        P(None, "mp", "dp"),
        P("dp", None, "mp"),
        P(None, "dp", None, "mp"),
        P("mp", "dp"),
        P(None, "mp", "dp"),
        P("dp", None, "mp"),
        P(None, "dp", None, "mp"),
        P("dp", None),
        P(None, "dp", None),
        P(None, "dp"),
        P(None, None, "dp"),
    )
    return jax.shard_map(
        fast_local if quick else local,
        mesh=mesh,
        in_specs=placed,
        out_specs=(
            P("dp", "mp"),
            P("dp", "mp"),
            P("dp", "mp", None, None),
            P(None, "dp", None, "mp"),
            P(None, "dp", None, "mp"),
            P(None, "mp", "dp"),
            P(None, "mp", "dp"),
            P(None, "dp", None, "mp"),
            P(None, "dp", None, "mp"),
            P(None, "mp", "dp"),
            P(None, "mp", "dp"),
            P(None, "dp", None, "mp"),
            P(None, "dp", None, "mp"),
            P(None, "dp", None),
            P(None, "dp", None),
            P(None, None, "dp"),
            P(None, None, "dp"),
        ),
        check_vma=False,
    )
```

```python
import math

import jax
import jax.numpy as jnp
import numpy as np
from jax import lax
from jax.experimental import pallas as pl
from jax.experimental.pallas import tpu as pltpu
from jax.sharding import PartitionSpec as P

D = 768
HD = 64
FF = 3072
PAIR = 256
CDIM = 256
TBINS = 64
STEP = 10


PATTERNS = np.array(
    [[0, 0, 0, 0], [0, 0, 1, 1], [0, 0, 1, 2], [0, 1, 2, 2], [0, 1, 2, 3]], dtype=np.int32
)
NORM_EPS = 1e-06
BETA_ONE = 0.9
BETA_TWO = 0.999
ADAM_EPS = 1e-08
DECAY = 0.01
AVERAGE = 0.999
MASKED = -1e30
HIGH = lax.Precision.HIGHEST


def time_features(bins, width):
    half = width // 2
    moment = (bins.astype(jnp.float32) + 0.5) / TBINS
    freq = jnp.exp(-math.log(10000.0) * jnp.arange(half, dtype=jnp.float32) / half)
    angle = 1000.0 * moment[..., None] * freq
    return jnp.concatenate([jnp.sin(angle), jnp.cos(angle)], axis=-1)


def slot_ids(layout, window):
    unit = np.arange(window) // (window // 4)
    table = jnp.asarray(PATTERNS[:, unit])
    select = (layout[:, None] == jnp.arange(5, dtype=jnp.int32)[None, :]).astype(jnp.int32)
    return jnp.dot(select, table)


def adamw(master, state, grad, rate):
    first = BETA_ONE * state[0] + (1.0 - BETA_ONE) * grad
    second = BETA_TWO * state[1] + (1.0 - BETA_TWO) * grad * grad
    first_hat = first / (1.0 - BETA_ONE**STEP)
    second_hat = second / (1.0 - BETA_TWO**STEP)
    updated = master - rate * (first_hat / (jnp.sqrt(second_hat) + ADAM_EPS) + DECAY * master)
    average = AVERAGE * state[2] + (1.0 - AVERAGE) * updated
    return (jnp.stack([updated, average]), jnp.stack([first, second]))


def normalize(hidden, shift, scale, width):
    totals = lax.psum((jnp.sum(hidden, axis=1), jnp.sum(hidden * hidden, axis=1)), "mp")
    center = totals[0] / width
    spread = lax.rsqrt(totals[1] / width - center * center + NORM_EPS)
    normed = (hidden - center[:, None]) * spread[:, None]
    rows = (normed * (1.0 + scale) + shift).astype(jnp.bfloat16)
    return (normed, spread, lax.all_gather(rows, "mp", axis=1, tiled=True))


def normalize_back(partial_value, normed, spread, scale, width):
    upstream = lax.psum_scatter(partial_value, "mp", scatter_dimension=1, tiled=True)
    inner = upstream * (1.0 + scale)
    totals = lax.psum((jnp.sum(inner, axis=1), jnp.sum(inner * normed, axis=1)), "mp")
    result = spread[:, None] * (
        inner - totals[0][:, None] / width - normed * (totals[1][:, None] / width)
    )
    return (upstream, result)


def branch_total(partial_value):
    return lax.psum_scatter(partial_value, "mp", scatter_dimension=1, tiled=True)


def gather_grad(value):
    return lax.all_gather(value, "mp", axis=1, tiled=True)


def attention_scores(query, keys, bias, same, factor):
    scores = jnp.einsum(
        "wihe,wjhe->whij", query, keys, preferred_element_type=jnp.float32
    ) * factor + bias.astype(jnp.float32)
    return jnp.where(same[:, None], scores, MASKED)


def local(
    residues,
    pair_input,
    out_grad,
    bucket_layout,
    time_bins,
    fold_class,
    attend_weight,
    attend_state,
    merge_weight,
    merge_state,
    expand_weight,
    expand_state,
    shrink_weight,
    shrink_state,
    modulate_weight,
    modulate_state,
    pair_weight,
    pair_state,
    class_weight,
    class_state,
):
    parts = lax.axis_size("mp")
    gathered = (
        lax.all_gather(attend_weight.astype(jnp.bfloat16), "dp", axis=0, tiled=True),
        lax.all_gather(merge_weight.astype(jnp.bfloat16), "dp", axis=1, tiled=True),
        lax.all_gather(expand_weight.astype(jnp.bfloat16), "dp", axis=0, tiled=True),
        lax.all_gather(shrink_weight.astype(jnp.bfloat16), "dp", axis=1, tiled=True),
        lax.all_gather(modulate_weight.astype(jnp.bfloat16), "dp", axis=0, tiled=True),
        lax.all_gather(pair_weight.astype(jnp.bfloat16), "dp", axis=0, tiled=True),
        lax.all_gather(class_weight.astype(jnp.bfloat16), "dp", axis=1, tiled=True),
    )
    attend_full, merge_full, expand_full, shrink_full, modulate_full, pair_full, class_full = (
        gathered
    )
    tokens, local_width = residues.shape
    windows = bucket_layout.shape[0]
    window = tokens // windows
    slots = time_bins.shape[1]
    classes_count = class_full.shape[0]
    heads_local = local_width // HD
    width = local_width * parts
    factor = HD ** (-0.5)
    slot = slot_ids(bucket_layout, window)
    pick = (slot[..., None] == jnp.arange(slots, dtype=jnp.int32)).astype(jnp.float32)
    same = slot[:, :, None] == slot[:, None, :]
    class_pick = (fold_class[..., None] == jnp.arange(classes_count, dtype=jnp.int32)).astype(
        jnp.float32
    )
    before = time_features(time_bins, class_full.shape[1]) + jnp.einsum(
        "wsn,nc->wsc", class_pick, class_full.astype(jnp.float32), precision=HIGH
    )
    condition = jax.nn.silu(before).astype(jnp.bfloat16)
    modulation = jnp.einsum(
        "wsc,cjd->wsjd", condition, modulate_full, preferred_element_type=jnp.float32
    )
    per_token = jnp.einsum("wts,wsjd->wtjd", pick, modulation, precision=HIGH).reshape(
        tokens, 6, local_width
    )
    hidden_in = residues.astype(jnp.float32)
    normed_one, spread_one, rows_one = normalize(hidden_in, per_token[:, 0], per_token[:, 1], width)
    triple = jnp.einsum(
        "td,dje->tje", rows_one, attend_full, preferred_element_type=jnp.float32
    ).astype(jnp.bfloat16)
    query = triple[:, 0].reshape(windows, window, heads_local, HD)
    keys = triple[:, 1].reshape(windows, window, heads_local, HD)
    values = triple[:, 2].reshape(windows, window, heads_local, HD)
    local_bias = jnp.einsum(
        "wijc,ch->whij", pair_input, pair_full, preferred_element_type=jnp.float32
    ).astype(jnp.bfloat16)
    bias = lax.all_to_all(local_bias, "mp", split_axis=1, concat_axis=2, tiled=True)
    scores = attention_scores(query, keys, bias, same, factor)
    peak = jnp.max(scores, axis=-1, keepdims=True)
    logsum = peak + jnp.log(jnp.sum(jnp.exp(scores - peak), axis=-1, keepdims=True))
    chance = jnp.exp(scores - logsum).astype(jnp.bfloat16)
    mixed = (
        jnp.einsum("whij,wjhe->wihe", chance, values, preferred_element_type=jnp.float32)
        .astype(jnp.bfloat16)
        .reshape(tokens, local_width)
    )
    attended = branch_total(jnp.dot(mixed, merge_full, preferred_element_type=jnp.float32))
    middle = hidden_in + per_token[:, 2] * attended
    normed_two, spread_two, rows_two = normalize(middle, per_token[:, 3], per_token[:, 4], width)
    pair_up = jnp.einsum("td,dje->tje", rows_two, expand_full, preferred_element_type=jnp.float32)
    gate = pair_up[:, 0]
    upward = pair_up[:, 1]
    sigma = jax.nn.sigmoid(gate)
    activated = (gate * sigma * upward).astype(jnp.bfloat16)
    fed = branch_total(jnp.dot(activated, shrink_full, preferred_element_type=jnp.float32))
    output = (middle + per_token[:, 5] * fed).astype(jnp.bfloat16)
    upper = out_grad.astype(jnp.float32)
    fed_grad = gather_grad((per_token[:, 5] * upper).astype(jnp.bfloat16))
    act_grad = lax.dot_general(
        fed_grad, shrink_full, (((1,), (1,)), ((), ())), preferred_element_type=jnp.float32
    )
    shrink_grad = lax.dot_general(
        activated, fed_grad, (((0,), (0,)), ((), ())), preferred_element_type=jnp.float32
    )
    slope = sigma * (1.0 + gate * (1.0 - sigma))
    up_grads = jnp.stack([act_grad * upward * slope, act_grad * gate * sigma], axis=1).astype(
        jnp.bfloat16
    )
    expand_grad = jnp.einsum("td,tje->dje", rows_two, up_grads, preferred_element_type=jnp.float32)
    partial_two = jnp.einsum(
        "tje,dje->td", up_grads, expand_full, preferred_element_type=jnp.float32
    )
    upstream_two, norm_two = normalize_back(
        partial_two, normed_two, spread_two, per_token[:, 4], width
    )
    middle_grad = upper + norm_two
    merged_grad = gather_grad((per_token[:, 2] * middle_grad).astype(jnp.bfloat16))
    mixed_grad = (
        lax.dot_general(
            merged_grad, merge_full, (((1,), (1,)), ((), ())), preferred_element_type=jnp.float32
        )
        .astype(jnp.bfloat16)
        .reshape(windows, window, heads_local, HD)
    )
    merge_grad = lax.dot_general(
        mixed, merged_grad, (((0,), (0,)), ((), ())), preferred_element_type=jnp.float32
    )
    again = attention_scores(query, keys, bias, same, factor)
    exact = jnp.exp(again - logsum)
    chance_grad = jnp.einsum(
        "wihe,wjhe->whij", mixed_grad, values, preferred_element_type=jnp.float32
    )
    score_grad = (
        exact * (chance_grad - jnp.sum(exact * chance_grad, axis=-1, keepdims=True))
    ).astype(jnp.bfloat16)
    value_grad = jnp.einsum(
        "whij,wihe->wjhe",
        exact.astype(jnp.bfloat16),
        mixed_grad,
        preferred_element_type=jnp.float32,
    )
    query_grad = (
        jnp.einsum("whij,wjhe->wihe", score_grad, keys, preferred_element_type=jnp.float32) * factor
    )
    keys_grad = (
        jnp.einsum("whij,wihe->wjhe", score_grad, query, preferred_element_type=jnp.float32)
        * factor
    )
    triple_grad = jnp.stack(
        [
            query_grad.reshape(tokens, local_width),
            keys_grad.reshape(tokens, local_width),
            value_grad.reshape(tokens, local_width),
        ],
        axis=1,
    ).astype(jnp.bfloat16)
    bias_grad = lax.all_to_all(score_grad, "mp", split_axis=2, concat_axis=1, tiled=True)
    pair_grad = jnp.einsum(
        "whij,ch->wijc", bias_grad, pair_full, preferred_element_type=jnp.float32
    ).astype(jnp.bfloat16)
    pairwise_grad = jnp.einsum(
        "wijc,whij->ch", pair_input, bias_grad, preferred_element_type=jnp.float32
    )
    attend_grad = jnp.einsum(
        "td,tje->dje", rows_one, triple_grad, preferred_element_type=jnp.float32
    )
    partial_one = jnp.einsum(
        "tje,dje->td", triple_grad, attend_full, preferred_element_type=jnp.float32
    )
    upstream_one, norm_one = normalize_back(
        partial_one, normed_one, spread_one, per_token[:, 1], width
    )
    residue_grad = (middle_grad + norm_one).astype(jnp.bfloat16)
    token_mod_grad = jnp.stack(
        [
            upstream_one,
            upstream_one * normed_one,
            middle_grad * attended,
            upstream_two,
            upstream_two * normed_two,
            upper * fed,
        ],
        axis=1,
    ).reshape(windows, window, 6, local_width)
    mod_grad = jnp.einsum("wts,wtjd->wsjd", pick, token_mod_grad, precision=HIGH)
    modulate_grad = jnp.einsum(
        "wsc,wsjd->cjd", condition.astype(jnp.float32), mod_grad, precision=HIGH
    )
    cond_grad = jnp.einsum(
        "wsjd,cjd->wsc", mod_grad, modulate_full.astype(jnp.float32), precision=HIGH
    )
    sig_before = jax.nn.sigmoid(before)
    before_grad = cond_grad * (sig_before * (1.0 + before * (1.0 - sig_before)))
    class_grad = jnp.einsum("wsn,wsc->nc", class_pick, before_grad, precision=HIGH)
    shared = lax.psum((pairwise_grad, class_grad), "mp")
    sums = (
        lax.psum_scatter(attend_grad, "dp", scatter_dimension=0, tiled=True),
        lax.psum_scatter(merge_grad, "dp", scatter_dimension=1, tiled=True),
        lax.psum_scatter(expand_grad, "dp", scatter_dimension=0, tiled=True),
        lax.psum_scatter(shrink_grad, "dp", scatter_dimension=1, tiled=True),
        lax.psum_scatter(modulate_grad, "dp", scatter_dimension=0, tiled=True),
        lax.psum_scatter(shared[0], "dp", scatter_dimension=0, tiled=True),
        lax.psum_scatter(shared[1], "dp", scatter_dimension=1, tiled=True),
    )
    rates = (
        2.0 / math.sqrt(D),
        2.0 / math.sqrt(D // 8),
        2.0 / math.sqrt(D),
        2.0 / math.sqrt(FF),
        2.0 / math.sqrt(CDIM),
        2.0 / math.sqrt(PAIR),
        2.0,
    )
    masters = (
        attend_weight,
        merge_weight,
        expand_weight,
        shrink_weight,
        modulate_weight,
        pair_weight,
        class_weight,
    )
    states = (
        attend_state,
        merge_state,
        expand_state,
        shrink_state,
        modulate_state,
        pair_state,
        class_state,
    )
    results = []
    for index in range(7):
        updated, tracked = adamw(masters[index], states[index], sums[index], rates[index])
        results.append(updated)
        results.append(tracked)
    return (
        output,
        residue_grad,
        pair_grad,
        results[0],
        results[1],
        results[2],
        results[3],
        results[4],
        results[5],
        results[6],
        results[7],
        results[8],
        results[9],
        results[10],
        results[11],
        results[12],
        results[13],
    )


RATES = (
    2.0 / math.sqrt(D),
    2.0 / math.sqrt(D // 8),
    2.0 / math.sqrt(D),
    2.0 / math.sqrt(FF),
    2.0 / math.sqrt(CDIM),
    2.0 / math.sqrt(PAIR),
    2.0,
)
f32 = jnp.float32
bf16 = jnp.bfloat16
NT = (((1,), (1,)), ((), ()))
NN = (((1,), (0,)), ((), ()))
TN = (((0,), (0,)), ((), ()))
HEADS = 12
GROUP = 16
UNIT = 64
CHUNK = 16
PAIRS = 8


def mm(a, b, dims=NN, precision=None):
    return lax.dot_general(a, b, dims, precision=precision, preferred_element_type=f32)


def head_mask(count):
    row = lax.broadcasted_iota(jnp.int32, (count, GROUP, D), 1)
    col = lax.broadcasted_iota(jnp.int32, (count, GROUP, D), 2) // HD
    return row == col


def spread_heads(rows):
    count = rows.shape[0]
    wide = jnp.broadcast_to(rows.astype(f32)[:, None, :], (count, GROUP, D))
    return jnp.where(head_mask(count), wide, 0.0).astype(bf16).reshape(count * GROUP, D)


def merge_heads(wide):
    count = wide.shape[0] // GROUP
    return jnp.sum(jnp.where(head_mask(count), wide.reshape(count, GROUP, D), 0.0), axis=1)


class Net:
    def __init__(self, send_sems, recv_sems):
        self.d = lax.axis_index("dp")
        self.m = lax.axis_index("mp")
        core = self.d % 2
        x = (self.d // 2) % 2
        y = self.d // 4
        self.core = core
        self.chip = self.d // 2
        self.chips = [self.chip, y * 2 + 1 - x, (1 - y) * 2 + x, (1 - y) * 2 + 1 - x]
        self.partner = self.chip * 2 + 1 - core
        self.send_sems = send_sems
        self.recv_sems = recv_sems
        self.sent = []
        self.open = []
        self.base = 0

    def z(self, t):
        return (self.m + t) % 4

    def peer(self, r):
        return self.chips[r] * 2 + self.core

    def sems(self, count):
        base = self.base
        self.base = base + count
        return base

    def barrier(self):
        sem = pltpu.get_barrier_semaphore()
        targets = [(self.d, self.z(t)) for t in (1, 2, 3)]
        targets += [(self.peer(r), self.m) for r in (1, 2, 3)] + [(self.partner, self.m)]
        for target in targets:
            pl.semaphore_signal(
                sem, inc=1, device_id=target, device_id_type=pl.DeviceIdType.MESH
            )
        pl.semaphore_wait(sem, len(targets))

    def copy(self, src, dst, recv, target, send=None):
        send = len(self.sent) if send is None else send
        return pltpu.make_async_remote_copy(
            src_ref=src,
            dst_ref=dst,
            send_sem=self.send_sems.at[send],
            recv_sem=self.recv_sems.at[recv],
            device_id=target,
            device_id_type=pl.DeviceIdType.MESH,
        )

    def send(self, src, dst, recv, target):
        made = self.copy(src, dst, recv, target)
        made.start()
        self.sent.append(made)
        self.open.append(made)
        return made

    def wait(self, dst, recv):
        self.copy(dst, dst, recv, (self.partner, self.m), 0).wait_recv()

    def drain(self):
        for made in self.open:
            made.wait_send()

    def settle(self, made):
        made.wait_send()
        self.open = [other for other in self.open if other is not made]


class Spread:
    def __init__(self, net, slot):
        self.net, self.slot, self.base = net, slot, net.sems(7)

    def start(self, src=None):
        net = self.net
        own = self.slot(net.d)
        src = own if src is None else src
        for r in (1, 2, 3):
            net.send(src, own, self.base + r, (net.peer(r), net.m))
        net.send(src, own, self.base, (net.partner, net.m))

    def forward(self, r):
        net = self.net
        slot = self.slot(net.peer(r))
        net.wait(slot, self.base + r)
        return net.send(slot, slot, self.base + 3 + r, (net.partner, net.m))

    def finish(self):
        net = self.net
        net.wait(self.slot(net.partner), self.base)
        for r in (1, 2, 3):
            net.wait(self.slot(net.chips[r] * 2 + 1 - net.core), self.base + 3 + r)


class Zline:
    def __init__(self, net, slot):
        self.net, self.slot, self.base = net, slot, net.sems(4)

    def send(self, t, src):
        net = self.net
        net.send(src, self.slot(net.m), self.base + net.m, (net.d, net.z(t)))

    def wait(self, t):
        net = self.net
        source = net.z(t)
        net.wait(self.slot(source), self.base + source)
        return source


def layer_kernel(
    ms, am, es, xp, gp, pair, sinus, pick, mask,
    out_o, res_o, ds_o, pw_o, at_o, mg_o, ex_o, sh_o, mod_o, pair_o, class_o,
    msg, amg, esg, xg, gg, modu, modg, modf, bpg, pb, bias, n1, sp1, r1,
    kf, vf, qf, pr, mix, att, mid, n2, sp2, r2, fg, act, upg, fp, fl, p2, p2l, p2o, fpo,
    esp, epl, exl, eso, dkv, dkf, dvf, dqf, mgd, l2, rhs2, p1, p1l,
    amp, axl, aso, azs, azl, mps, mpl, mrg, pws, pwl, pwx, pwy, pco, pcl,
    ops, opl, rps, rpl, ctf, cfull,
    send_sems, recv_sems, pair_sems,
):
    net = Net(send_sems, recv_sems)
    d, m = net.d, net.m
    net.barrier()

    chunks = 16
    slots = pb.shape[0]

    def pair_copy(step):
        c = step % chunks
        return pltpu.make_async_copy(
            pair.at[c // 8, pl.ds((c % 8) * PAIRS, PAIRS)],
            pb.at[step % slots],
            pair_sems.at[step % slots],
        )

    for step in range(slots):
        pair_copy(step).start()

    ms_all = Spread(net, lambda i: msg.at[i])
    am_line = Zline(net, lambda s: amg.at[s, d])
    am_all = [Spread(net, lambda i, t=t: amg.at[net.z(t), i]) for t in range(4)]
    x_line = Zline(net, lambda s: xg.at[s])
    g_line = Zline(net, lambda s: gg.at[s])
    mod_line = Zline(net, lambda s: modg.at[s])
    bp_all = Spread(net, lambda i: bpg.at[i])
    es_all = Spread(net, lambda i: esg.at[i])

    ms_all.start(ms)
    for t in (1, 2, 3):
        am_line.send(t, am)
    am_all[0].start(am)
    for t in (1, 2, 3):
        x_line.send(t, xp)
    msg[d] = ms[...]
    amg[m, d] = am[...]
    esg[d] = es[...]
    xg[m] = xp[...]
    gg[m] = gp[...]
    for r in (1, 2, 3):
        ms_all.forward(r)
    ms_all.finish()

    slab = msg[:, :, 0:128].reshape(256, 128)
    select = (
        lax.broadcasted_iota(jnp.int32, (GROUP, 128), 1)
        == lax.broadcasted_iota(jnp.int32, (GROUP, 128), 0) + 64
    ) & (lax.broadcasted_iota(jnp.int32, (GROUP, 128), 0) < HEADS)
    pw_o[...] = mm(jnp.where(select, 1.0, 0.0).astype(bf16), slab, NT).astype(bf16)
    before = sinus[...] + mm(pick[...], slab, NT)
    condition = (before * jax.nn.sigmoid(before)).astype(bf16)
    modu[...] = mm(condition, msg[:, :, 128:1280].reshape(256, 1152))
    for t in (1, 2, 3):
        mod_line.send(t, modu)
    modg[m] = modu[...]
    bpg[d] = jnp.concatenate([before, pick[...].astype(f32)], axis=-1)

    def bias_chunk(step):
        slot = step % slots
        pair_copy(step).wait()

        def one(i, carry):
            part = mm(pw_o[...], pb[slot, i], NT)
            at = pl.multiple_of((step % 8) * PAIRS * GROUP + i * GROUP, GROUP)
            bias[step // 8, pl.ds(at, GROUP), :] = part.astype(bf16)
            return carry

        lax.fori_loop(0, PAIRS, one, 0, unroll=4)
        pair_copy(step + slots).start()

    for step in range(4):
        bias_chunk(step)
    for t in (1, 3, 2):
        am_line.wait(t)
        am_all[t].start()
        first = {1: 4, 3: 6, 2: 8}[t]
        bias_chunk(first)
        bias_chunk(first + 1)
    for r in (1, 2, 3):
        am_all[0].forward(r)
    es_all.start(es)
    for t in (1, 2, 3):
        g_line.send(t, gp)
    bp_all.start()
    bias_chunk(10)
    bias_chunk(11)
    for r in (1, 2, 3):
        am_all[1].forward(r)
    for step in range(12, 16):
        bias_chunk(step)

    for t in (1, 2, 3):
        mod_line.wait(t)
    for j in range(6):
        modf[j] = jnp.concatenate([modg[s, :, 192 * j : 192 * j + 192] for s in range(4)], axis=-1)
    for t in (1, 2, 3):
        x_line.wait(t)

    def unpack(ref, w, unit):
        parts = []
        for s in range(4):
            parts.append(ref[s, pl.ds(w * 256 + unit * UNIT, UNIT), :].astype(f32))
            low = ref[s, pl.ds(512 + unit * UNIT, UNIT), :].astype(f32)
            parts.append(low[:, 64 * w : 64 * w + 64])
        return jnp.concatenate(parts, axis=-1)

    def norm(v):
        center = jnp.mean(v, axis=-1, keepdims=True)
        spread = lax.rsqrt(jnp.mean(v * v, axis=-1, keepdims=True) - center * center + NORM_EPS)
        return (v - center) * spread, spread

    for w in range(2):

        def first_norm(unit, carry, w=w):
            v = unpack(xg, w, unit)
            rows = pl.ds(pl.multiple_of(w * 256 + unit * UNIT, UNIT), UNIT)
            normed, spread = norm(v)
            n1[rows, :] = normed
            sp1[rows, :] = jnp.broadcast_to(spread, (UNIT, 128))
            shift = modf[0, pl.ds(w * 4 + unit, 1), :]
            scale = modf[1, pl.ds(w * 4 + unit, 1), :]
            r1[rows, :] = (normed * (1.0 + scale) + shift).astype(bf16)
            return carry

        lax.fori_loop(0, 4, first_norm, 0)

    for t in (3, 2):
        for r in (1, 2, 3):
            am_all[t].forward(r)
    for t in (0, 1, 3, 2):
        am_all[t].finish()

    def own(w):
        return pl.ds(pl.multiple_of(w * 256 + m * UNIT, UNIT), UNIT)

    def weight(s, lo, hi):
        return amg[s, :, :, lo:hi].reshape(D, hi - lo)

    r1_own = jnp.concatenate([r1[own(0), :], r1[own(1), :]], axis=0)
    qf[...] = jnp.concatenate(
        [mm(r1_own, weight(s, 384, 768))[:, 0:192] for s in range(4)], axis=-1
    ).astype(bf16)
    for w in range(2):
        rows = slice(w * 256, w * 256 + 256)
        both = [mm(r1[rows, :], weight(s, 0, 384)) for s in range(4)]
        kf[rows, :] = jnp.concatenate([v[:, 0:192] for v in both], axis=-1).astype(bf16)
        vf[rows, :] = jnp.concatenate([v[:, 192:384] for v in both], axis=-1).astype(bf16)

    factor = HD ** (-0.5)

    def attend(c, carry):
        w = c // 4
        mine = pl.ds(pl.multiple_of(c * CHUNK, CHUNK), CHUNK)
        keys = pl.ds(pl.multiple_of(w * 256, 256), 256)
        wide = pl.ds(pl.multiple_of((c % 4) * CHUNK * GROUP, CHUNK * GROUP), CHUNK * GROUP)
        scores = mm(spread_heads(qf[mine, :]), kf[keys, :], NT) * factor
        scores = scores + bias[w, wide, :].astype(f32) + mask[pl.ds(w, 1), :]
        peak = jnp.max(scores, axis=-1, keepdims=True)
        expo = jnp.exp(scores - peak)
        chance = expo / jnp.sum(expo, axis=-1, keepdims=True)
        pr[w, wide, :] = chance
        mix[mine, :] = merge_heads(mm(chance.astype(bf16), vf[keys, :])).astype(bf16)
        return carry

    lax.fori_loop(0, 8, attend, 0)
    es_sent = [es_all.forward(r) for r in (1, 2, 3)]

    mixed = mix[...]
    blank = jnp.zeros((128, 192), bf16)
    attended = mm(
        jnp.concatenate([blank, mixed[:, 0:192]], axis=-1), weight(0, 384, 768), NT
    )
    for s in range(1, 4):
        part = jnp.concatenate([blank, mixed[:, 192 * s : 192 * s + 192]], axis=-1)
        attended = attended + mm(part, weight(s, 384, 768), NT)
    att[...] = attended

    def mod_row(j, w):
        return modf[j, pl.ds(w * 4 + m, 1), :]

    for w in range(2):
        half = slice(w * UNIT, w * UNIT + UNIT)
        middle = unpack(xg, w, m) + mod_row(2, w) * att[half, :]
        mid[half, :] = middle
        normed, spread = norm(middle)
        n2[half, :] = normed
        sp2[half, :] = jnp.broadcast_to(spread, (UNIT, 128))
        r2[m, half, :] = (normed * (1.0 + mod_row(4, w)) + mod_row(3, w)).astype(bf16)

    r2_line = Zline(net, lambda s: r2.at[s])
    for t in (1, 3, 2):
        r2_line.send(t, r2.at[m])
    for t in (1, 2, 3):
        g_line.wait(t)
    for s in range(4):
        for w in range(2):
            half = slice(w * UNIT, w * UNIT + UNIT)
            upper = unpack(gg, w, s)
            fg[s, half, :] = (modf[5, w * 4 + s : w * 4 + s + 1, :] * upper).astype(bf16)
    es_all.finish()

    p2_line = Zline(net, lambda s: p2l.at[s])
    f_line = Zline(net, lambda s: fl.at[s])

    def feed(s):
        expand = esg[:, :, 0:1536].reshape(D, 1536)
        shrink = esg[:, :, 1536:2304].reshape(D, 768)
        up = mm(r2[s], expand)
        gate = up[:, 0:768]
        upward = up[:, 768:1536]
        act_grad = mm(fg[s], shrink)
        sigma = jax.nn.sigmoid(gate)
        activated = (gate * sigma * upward).astype(bf16)
        act[s] = activated
        slope = sigma * (1.0 + gate * (1.0 - sigma))
        grads = jnp.concatenate(
            [(act_grad * upward * slope).astype(bf16), (act_grad * gate * sigma).astype(bf16)],
            axis=-1,
        )
        upg[s] = grads
        return mm(grads, expand, NT), mm(activated, shrink, NT)

    partial, fed = feed(m)
    p2o[...] = partial
    fpo[...] = fed
    for t in (1, 3, 2):
        source = r2_line.wait(t)
        partial, fed = feed(source)
        p2[source] = partial.astype(bf16)
        p2_line.send(t, p2.at[source])
        fp[source] = fed.astype(bf16)
    for t in (1, 3, 2):
        f_line.send(t, fp.at[net.z(t)])

    def put_es(left, right, at):
        for h in range(2):
            value = mm(left[:, :, 384 * h : 384 * h + 384].reshape(512, 384), right, TN)
            for i in range(4):
                part = value[96 * i : 96 * i + 96, :].astype(bf16)
                esp[i % 2, 2 * h + i // 2, :, at : at + 768] = part

    put_es(r2, upg[:, :, 0:768].reshape(512, 768), 0)
    put_es(r2, upg[:, :, 768:1536].reshape(512, 768), 768)
    put_es(fg, act[...].reshape(512, 768), 1536)
    for made in es_sent:
        net.settle(made)
    es_pair = net.sems(1)
    net.send(esp.at[1 - net.core], epl, es_pair, (net.partner, m))

    for t in (1, 3, 2):
        p2_line.wait(t)

    def norm_back(upstream, normed, spread, scale):
        inner = upstream * (1.0 + scale)
        first = jnp.mean(inner, axis=-1, keepdims=True)
        second = jnp.mean(inner * normed, axis=-1, keepdims=True)
        return spread * (inner - first - normed * second)

    def unit_sum(v):
        return jnp.sum(v, axis=0, keepdims=True)

    own_sums = [[None] * 6, [None] * 6]
    for w in range(2):
        half = slice(w * UNIT, w * UNIT + UNIT)
        upstream = p2o[half, :]
        for t in (1, 3, 2):
            upstream = upstream + p2l[net.z(t), half, :].astype(f32)
        normed = n2[half, :]
        back = norm_back(upstream, normed, sp2[half, 0:1], mod_row(4, w))
        grad = unpack(gg, w, m) + back
        p2o[half, :] = grad
        own_sums[w][2] = unit_sum(grad * att[half, :])
        own_sums[w][3] = unit_sum(upstream)
        own_sums[w][4] = unit_sum(upstream * normed)
        l2[slice(128 + w * UNIT, 128 + w * UNIT + UNIT), :] = (mod_row(2, w) * grad).astype(bf16)
        l2[half, :] = r1[own(w), :]
    merged_grad = l2[128:256, :]
    mgd[...] = jnp.concatenate(
        [mm(merged_grad, weight(s, 384, 768))[:, 192:384] for s in range(4)], axis=-1
    ).astype(bf16)

    net.wait(epl, es_pair)
    es_chip = net.sems(4)
    for r in (1, 2, 3, 0):
        total = esp[net.core, net.chips[r]].astype(f32) + epl[net.chips[r]].astype(f32)
        if r == 0:
            eso[...] = total
        else:
            esp[net.core, net.chips[r]] = total.astype(bf16)
            net.send(
                esp.at[net.core, net.chips[r]], exl.at[r - 1], es_chip + r, (net.peer(r), m)
            )

    dkf[...] = jnp.zeros_like(dkf)
    dvf[...] = jnp.zeros_like(dvf)

    def attend_back(c, carry):
        w = c // 4
        mine = pl.ds(pl.multiple_of(c * CHUNK, CHUNK), CHUNK)
        keys = pl.ds(pl.multiple_of(w * 256, 256), 256)
        wide = pl.ds(pl.multiple_of((c % 4) * CHUNK * GROUP, CHUNK * GROUP), CHUNK * GROUP)
        grad = spread_heads(mgd[mine, :])
        chance = pr[w, wide, :]
        chance_grad = mm(grad, vf[keys, :], NT)
        inner = jnp.sum(chance * chance_grad, axis=-1, keepdims=True)
        score = (chance * (chance_grad - inner)).astype(bf16)
        ds_o[w, wide, :] = score
        dqf[mine, :] = (merge_heads(mm(score, kf[keys, :])) * factor).astype(bf16)
        dvf[keys, :] += mm(chance.astype(bf16), grad, TN)
        dkf[keys, :] += mm(score, spread_heads(qf[mine, :]), TN) * factor
        return carry

    lax.fori_loop(0, 8, attend_back, 0)

    o_line = Zline(net, lambda s: opl.at[s])

    def pack(line, value, ref):
        for s in range(4):
            part = value[:, 192 * s : 192 * s + 192]
            ref[s, 0:128, :] = part[:, 0:128].astype(bf16)
            low = part[:, 128:192]
            ref[s, 128:192, :] = jnp.concatenate([low[0:64], low[64:128]], axis=-1).astype(bf16)
        for t in (1, 3, 2):
            line.send(t, ref.at[net.z(t)])

    def unpack_out(line, ref, mine, to):
        for t in (0, 1, 3, 2):
            s = net.z(t)
            block = mine if t == 0 else ref
            if t:
                line.wait(t)
            for w in range(2):
                rows = pl.ds(pl.multiple_of(w * 256 + s * UNIT, UNIT), UNIT)
                high = block[s, w * UNIT : w * UNIT + UNIT, :].astype(f32)
                low = block[s, 128:192, :].astype(f32)[:, 64 * w : 64 * w + 64]
                to[rows, :] = jnp.concatenate([high, low], axis=-1).astype(bf16)

    for t in (1, 3, 2):
        f_line.wait(t)
    done = []
    for w in range(2):
        half = slice(w * UNIT, w * UNIT + UNIT)
        fed = fpo[half, :]
        for t in (1, 3, 2):
            fed = fed + fl[net.z(t), half, :].astype(f32)
        own_sums[w][5] = unit_sum(unpack(gg, w, m) * fed)
        done.append(mid[half, :] + mod_row(5, w) * fed)
    pack(o_line, jnp.concatenate(done, axis=0), ops)

    for s in range(4):
        cols = slice(192 * s, 192 * s + 192)
        dkv[s] = jnp.concatenate([dkf[:, cols], dvf[:, cols]], axis=-1).astype(bf16)
        rhs2[s, 0:128, :] = jnp.concatenate([dqf[:, cols], blank], axis=-1)
        rhs2[s, 128:256, :] = jnp.concatenate([blank, mix[:, cols]], axis=-1)
    am_pair = net.sems(4)

    def apl(t):
        return esg.at[pl.ds(4 * (t // 3), 4), :, 768 * (t % 3) : 768 * (t % 3) + 768]

    for t in (1, 3, 2, 0):
        s = net.z(t)
        for h in range(2):
            cols = slice(384 * h, 384 * h + 384)
            for left, right, at in ((r1, dkv, 0), (l2, rhs2, 384)):
                value = mm(left[:, cols], right[s], TN)
                for i in range(4):
                    part = value[96 * i : 96 * i + 96, :].astype(bf16)
                    amp[s, i % 2, 2 * h + i // 2, :, at : at + 384] = part
        net.send(amp.at[s, 1 - net.core], apl(t), am_pair + t, (net.partner, m))

    for w in range(2):
        rows = slice(w * 256, w * 256 + 256)
        total = mm(dkv[0, rows, :], weight(0, 0, 384), NT)
        for s in range(1, 4):
            total = total + mm(dkv[s, rows, :], weight(s, 0, 384), NT)
        dkf[rows, :] = total
    total = mm(rhs2[0, 0:128, :], weight(0, 384, 768), NT)
    for s in range(1, 4):
        total = total + mm(rhs2[s, 0:128, :], weight(s, 384, 768), NT)
    for w in range(2):
        dkf[own(w), :] += total[w * UNIT : w * UNIT + UNIT, :]
    p1_line = Zline(net, lambda s: p1l.at[s])
    for t in (1, 3, 2):
        s = net.z(t)
        for w in range(2):
            rows = pl.ds(pl.multiple_of(w * 256 + s * UNIT, UNIT), UNIT)
            p1[s, w * UNIT : w * UNIT + UNIT, :] = dkf[rows, :].astype(bf16)
        p1_line.send(t, p1.at[s])

    sums = [[], []]
    for u in range(8):
        rows = slice(u * UNIT, u * UNIT + UNIT)
        sums[0].append(unit_sum(dkf[rows, :]))
        sums[1].append(unit_sum(dkf[rows, :] * n1[rows, :]))
    row = lax.broadcasted_iota(jnp.int32, (8, D), 0)
    table = [jnp.concatenate(sums[0], axis=0), jnp.concatenate(sums[1], axis=0)]
    for j in range(2, 6):
        first = jnp.broadcast_to(own_sums[0][j], (8, D))
        second = jnp.broadcast_to(own_sums[1][j], (8, D))
        table.append(jnp.where(row == m, first, jnp.where(row == m + 4, second, 0.0)))
    mod_sum = Zline(net, lambda s: mpl.at[s])
    for s in range(4):
        mps[s] = jnp.concatenate([v[:, 192 * s : 192 * s + 192] for v in table], axis=-1)
    for t in (1, 3, 2):
        mod_sum.send(t, mps.at[net.z(t)])

    def pair_chunk(step, acc):
        slot = step % slots
        pair_copy(step).wait()

        def one(i, acc):
            at = pl.multiple_of((step % 8) * PAIRS * GROUP + i * GROUP, GROUP)
            return acc + mm(ds_o[(step - 16) // 8, pl.ds(at, GROUP), :], pb[slot, i])

        acc = lax.fori_loop(0, PAIRS, one, acc, unroll=4)
        if step + slots < 2 * chunks:
            pair_copy(step + slots).start()
        return acc

    pairwise = jnp.zeros((GROUP, 256), f32)
    am_chip = net.sems(16)
    step = 16
    for t in (1, 3, 2, 0):
        s = net.z(t)
        net.wait(apl(t), am_pair + t)
        base, cols = 4 * (t // 3), slice(768 * (t % 3), 768 * (t % 3) + 768)
        for r in (1, 2, 3, 0):
            total = amp[s, net.core, net.chips[r]].astype(f32)
            total = total + esg[base + net.chips[r], :, cols].astype(f32)
            if r == 0:
                aso[s] = total
            else:
                amp[s, net.core, net.chips[r]] = total.astype(bf16)
                net.send(
                    amp.at[s, net.core, net.chips[r]],
                    axl.at[s, r - 1],
                    am_chip + 4 * t + r,
                    (net.peer(r), m),
                )
        for _ in range(4):
            pairwise = pair_chunk(step, pairwise)
            step += 1

    for r in (1, 2, 3):
        bp_all.forward(r)
    bp_all.finish()

    wide = jnp.concatenate([pairwise, jnp.zeros((112, 256), f32)], axis=0).T
    for i in range(8):
        pws[i % 2, i // 2] = wide[32 * i : 32 * i + 32, :]
    pw_pair = net.sems(1)
    net.send(pws.at[1 - net.core], pwl, pw_pair, (net.partner, m))

    for t in (1, 3, 2):
        mod_sum.wait(t)
    mod_grad = mps[m]
    for t in (1, 3, 2):
        mod_grad = mod_grad + mpl[net.z(t)]
    mrg[d] = mod_grad
    mr_all = Spread(net, lambda i: mrg.at[i])
    mr_all.start()

    for t in (1, 3, 2):
        p1_line.wait(t)
    r_line = Zline(net, lambda s: rpl.at[s])
    done = []
    for w in range(2):
        half = slice(w * UNIT, w * UNIT + UNIT)
        upstream = dkf[own(w), :]
        for t in (1, 3, 2):
            upstream = upstream + p1l[net.z(t), half, :].astype(f32)
        back = norm_back(upstream, n1[own(w), :], sp1[own(w), :][:, 0:1], mod_row(1, w))
        done.append(p2o[half, :] + back)
    pack(r_line, jnp.concatenate(done, axis=0), rps)

    total = eso[...]
    for r in (1, 2, 3):
        net.wait(exl.at[r - 1], es_chip + r)
        total = total + exl[r - 1].astype(f32)
    for k in range(2):
        ex_o[:, k, :] = total[:, 768 * k : 768 * k + 768]
    sh_o[...] = total[:, 1536:2304]

    net.wait(pwl, pw_pair)
    pw_chip = net.sems(4)
    for r in (1, 2, 3):
        pwx[r] = pws[net.core, net.chips[r]] + pwl[net.chips[r]]
        net.send(pwx.at[r], pwy.at[r], pw_chip + r, (net.peer(r), m))
    pair_sum = pws[net.core, net.chip] + pwl[net.chip]

    am_z = Zline(net, lambda s: azl.at[s])
    for t in (1, 3, 2, 0):
        s = net.z(t)
        total = aso[s]
        for r in (1, 2, 3):
            net.wait(axl.at[s, r - 1], am_chip + 4 * t + r)
            total = total + axl[s, r - 1].astype(f32)
        if t:
            azs[s] = total.astype(bf16)
            am_z.send(t, azs.at[s])
        else:
            aso[s] = total
        if t == 1:
            for r in (1, 2, 3):
                mr_all.forward(r)

    mr_all.finish()
    before = bpg[:, :, 0:256].reshape(64, 256)
    sig = jax.nn.sigmoid(before)
    condition = (before * sig).astype(bf16).astype(f32)
    picks = bpg[:, :, 256:384].reshape(64, 128)
    grads = mrg[...].reshape(64, 1152)
    ctf[...] = condition.T
    mod_sums = mm(ctf[pl.ds(pl.multiple_of(d * 32, 32), 32), :], grads, NN, HIGH)
    for j in range(6):
        mod_o[j] = mod_sums[:, 192 * j : 192 * j + 192]
    cond_grad = mm(grads, msg[:, :, 128:1280].reshape(256, 1152).astype(f32), NT, HIGH)
    before_grad = cond_grad * (sig * (1.0 + before * (1.0 - sig)))
    cfull[...] = mm(before_grad, picks, TN, HIGH)
    for r in (1, 2, 3):
        net.wait(pwy.at[r], pw_chip + r)
        pair_sum = pair_sum + pwy[r]
    pco[...] = jnp.concatenate(
        [pair_sum, cfull[pl.ds(pl.multiple_of(d * 32, 32), 32), :]], axis=-1
    )
    pc_line = Zline(net, lambda s: pcl.at[s])
    for t in (1, 3, 2):
        pc_line.send(t, pco)

    unpack_out(o_line, opl, ops, out_o)
    unpack_out(r_line, rpl, rps, res_o)
    total = aso[m]
    for t in (1, 3, 2):
        total = total + azl[am_z.wait(t)].astype(f32)
    at_o[0] = total[:, 384:576]
    at_o[1] = total[:, 0:192]
    at_o[2] = total[:, 192:384]
    tall = jnp.concatenate([total[:, 512:768], jnp.zeros((32, 256), f32)], axis=0).T
    mg_o[...] = tall[64:256, 0:96]
    total = pco[...]
    for t in (1, 3, 2):
        total = total + pcl[pc_line.wait(t)]
    tall = jnp.concatenate([total[:, 0:128], jnp.zeros((96, 128), f32)], axis=0).T
    pair_o[...] = tall[0:HEADS, 0:32]
    class_o[...] = total[:, 128 : 128 + class_o.shape[1]]
    net.drain()


def layer_call(classes, *args):
    V = pltpu.VMEM
    scratch = [
        V((8, 32, 1280), bf16), V((4, 8, 96, 768), bf16), V((8, 96, 2304), bf16),
        V((4, 768, 128), bf16), V((4, 768, 128), bf16),
        V((8, 1152), f32), V((4, 8, 1152), f32), V((6, 8, 768), f32), V((8, 8, 384), f32),
        V((2, PAIRS, 256, 256), bf16), V((2, 1024, 256), bf16),
        V((512, 768), f32), V((512, 128), f32), V((512, 768), bf16),
        V((512, 768), bf16), V((512, 768), bf16), V((128, 768), bf16), V((2, 1024, 256), f32),
        V((128, 768), bf16), V((128, 768), f32), V((128, 768), f32), V((128, 768), f32),
        V((128, 128), f32),
        V((4, 128, 768), bf16), V((4, 128, 768), bf16), V((4, 128, 768), bf16),
        V((4, 128, 1536), bf16), V((4, 128, 768), bf16), V((4, 128, 768), bf16),
        V((4, 128, 768), bf16), V((4, 128, 768), bf16), V((128, 768), f32), V((128, 768), f32),
        V((2, 4, 96, 2304), bf16), V((4, 96, 2304), bf16), V((3, 96, 2304), bf16),
        V((96, 2304), f32),
        V((4, 512, 384), bf16), V((512, 768), f32), V((512, 768), f32), V((128, 768), bf16),
        V((128, 768), bf16), V((256, 768), bf16), V((4, 256, 384), bf16),
        V((4, 128, 768), bf16), V((4, 128, 768), bf16),
        V((4, 2, 4, 96, 768), bf16), V((4, 3, 96, 768), bf16),
        V((4, 96, 768), f32), V((4, 96, 768), bf16), V((4, 96, 768), bf16),
        V((4, 8, 1152), f32), V((4, 8, 1152), f32), V((8, 8, 1152), f32),
        V((2, 4, 32, 128), f32), V((4, 32, 128), f32), V((4, 32, 128), f32), V((4, 32, 128), f32),
        V((32, 256), f32), V((4, 32, 256), f32),
        V((4, 192, 128), bf16), V((4, 192, 128), bf16), V((4, 192, 128), bf16),
        V((4, 192, 128), bf16), V((256, 64), f32), V((256, 128), f32),
        pltpu.SemaphoreType.DMA((160,)), pltpu.SemaphoreType.DMA((160,)),
        pltpu.SemaphoreType.DMA((2,)),
    ]
    whole = pl.BlockSpec(memory_space=pltpu.VMEM)
    outs = (
        ((512, 192), bf16), ((512, 192), bf16), ((2, 1024, 256), bf16), ((16, 256), bf16),
        ((3, 96, 192), f32), ((192, 96), f32), ((96, 2, 768), f32), ((96, 768), f32),
        ((6, 32, 192), f32), ((HEADS, 32), f32), ((32, classes), f32),
    )
    return pl.pallas_call(
        layer_kernel,
        out_shape=tuple(jax.ShapeDtypeStruct(s, t) for s, t in outs),
        in_specs=[pl.BlockSpec(memory_space=pl.ANY) if i == 5 else whole for i in range(9)],
        out_specs=(whole,) * len(outs),
        scratch_shapes=scratch,
        compiler_params=pltpu.CompilerParams(
            collective_id=0, has_side_effects=True, vmem_limit_bytes=67043328
        ),
        name="layer",
    )(*args)


def finish_kernel(*refs):
    ds, pw, out, res = refs[0:4]
    groups = [refs[4 + 3 * i : 7 + 3 * i] for i in range(7)]
    out_t, res_t, pair = refs[25:28]
    results = [refs[28 + 2 * i : 30 + 2 * i] for i in range(7)]
    block, sems = refs[42:44]
    step = pl.program_id(0)

    def put(c, at):
        rows = pl.ds((at % 2) * 32 + 8 * c, 8)
        return pltpu.make_async_copy(block.at[c], pair.at[at // 2, rows], sems.at[c])

    def update(index):
        (master, state, grad), (fresh, kept) = groups[index], results[index]
        old, slope = master[...], grad[...]
        first = BETA_ONE * state[0] + (1.0 - BETA_ONE) * slope
        second = BETA_TWO * state[1] + (1.0 - BETA_TWO) * slope * slope
        first_hat = first / (1.0 - BETA_ONE**STEP)
        second_hat = second / (1.0 - BETA_TWO**STEP)
        new = old - RATES[index] * (first_hat / (jnp.sqrt(second_hat) + ADAM_EPS) + DECAY * old)
        average = AVERAGE * state[2] + (1.0 - AVERAGE) * new
        for ref, values in ((fresh, (new, average)), (kept, (first, second))):
            for i in range(2):
                if index == 5:
                    ref[:, i, :] = values[i]
                else:
                    ref[i] = values[i]

    def turn(source, target):
        wide = jnp.concatenate([source[...].astype(f32), jnp.zeros((128, 64), f32)], axis=-1)
        target[...] = wide.T[0:192, :].astype(bf16)

    for c in range(4):

        @pl.when(step > 0)
        def _(c=c):
            put(c, step - 1).wait()

        for i in range(8):
            at = GROUP * (8 * c + i)
            block[c, i] = mm(ds[0, at : at + GROUP, :], pw[...], TN).astype(bf16)
        if c == 0:
            update(0)
            update(1)
            turn(out, out_t)
        elif c == 1:
            update(2)
        elif c == 2:
            update(3)
            turn(res, res_t)
        else:
            for index in (4, 5, 6):
                update(index)
        put(c, step).start()

    @pl.when(step == 3)
    def _():
        for c in range(4):
            put(c, step).wait()


def finish_call(ds, pw, out, res, *groups):
    def rows(shape, axis=-2):
        at = len(shape) + axis
        block = (*shape[:at], shape[at] // 4, *shape[at + 1 :])
        return pl.BlockSpec(block, lambda i: (0,) * at + (i,) + (0,) * (-1 - axis))

    def whole(shape):
        return pl.BlockSpec(tuple(shape), lambda i: (0,) * len(shape))

    in_specs = [
        pl.BlockSpec((1, 512, 256), lambda i: (i // 2, i % 2, 0)), whole((16, 256)),
        rows((512, 192)), rows((512, 192)),
    ]
    turned = pl.BlockSpec((192, 128), lambda i: (0, i))
    out_specs = [turned, turned, pl.BlockSpec(memory_space=pl.ANY)]
    outs = [
        jax.ShapeDtypeStruct((192, 512), bf16), jax.ShapeDtypeStruct((192, 512), bf16),
        jax.ShapeDtypeStruct((2, 64, 256, 256), bf16),
    ]
    for index in range(7):
        master, state, grad = groups[3 * index : 3 * index + 3]
        make = rows if index < 5 else whole
        if index == 2:
            make = lambda shape: rows(shape, -3)
        in_specs += [make(master.shape), make(state.shape), make(grad.shape)]
        shape = (2, *master.shape)
        if index == 5:
            shape = (master.shape[0], 2, master.shape[1])
        out_specs += [make(shape)] * 2
        outs += [jax.ShapeDtypeStruct(shape, f32)] * 2
    return pl.pallas_call(
        finish_kernel,
        grid=(4,),
        out_shape=tuple(outs),
        in_specs=in_specs,
        out_specs=tuple(out_specs),
        scratch_shapes=[pltpu.VMEM((4, 8, 256, 256), bf16), pltpu.SemaphoreType.DMA((4,))],
        compiler_params=pltpu.CompilerParams(vmem_limit_bytes=67043328),
        name="finish",
    )(ds, pw, out, res, *groups)


def fast_local(
    residues, pair_input, out_grad, bucket_layout, time_bins, fold_class,
    attend_weight, attend_state, merge_weight, merge_state, expand_weight, expand_state,
    shrink_weight, shrink_state, modulate_weight, modulate_state, pair_weight, pair_state,
    class_weight, class_state,
):
    m = lax.axis_index("mp")
    classes = class_weight.shape[0]
    am = jnp.concatenate(
        [attend_weight[:, 1], attend_weight[:, 2], attend_weight[:, 0], merge_weight.T], axis=1
    ).astype(bf16)
    es = jnp.concatenate(
        [expand_weight[:, 0], expand_weight[:, 1], shrink_weight.T], axis=1
    ).astype(bf16)
    ms = jnp.concatenate(
        [
            jnp.pad(class_weight.T, ((0, 0), (0, 64 - classes))),
            jnp.pad(pair_weight, ((0, 0), (0, 52))),
            modulate_weight.reshape(32, 1152),
        ],
        axis=1,
    ).astype(bf16)

    def packed(v):
        low = v[:, 128:]
        return jnp.concatenate([v[:, :128], jnp.concatenate([low[:256], low[256:]], axis=1)], axis=0)

    table = jnp.asarray(PATTERNS)
    layout = (bucket_layout[:, None] == jnp.arange(5, dtype=jnp.int32)).astype(jnp.int32)
    unit_slot = jnp.sum(layout[:, :, None] * table[None], axis=1)
    pick_slot = (unit_slot[..., None] == jnp.arange(4, dtype=jnp.int32)).astype(jnp.int32)
    unit_bin = jnp.sum(pick_slot * time_bins[:, None, :], axis=-1).reshape(8)
    unit_class = jnp.sum(pick_slot * fold_class[:, None, :], axis=-1).reshape(8)
    sinus = time_features(unit_bin, 256)
    pick = (unit_class[:, None] == jnp.arange(128, dtype=jnp.int32)).astype(bf16)
    mine = jnp.sum(
        unit_slot * (jnp.arange(4, dtype=jnp.int32)[None] == m).astype(jnp.int32),
        axis=1,
        keepdims=True,
    )
    seen = jnp.where(unit_slot == mine, 0.0, MASKED)
    mask = jnp.broadcast_to(seen[:, :, None], (2, 4, UNIT)).reshape(2, 256)

    out, res, ds, pw, *grads = layer_call(
        classes, ms, am, es, packed(residues), packed(out_grad), pair_input, sinus, pick, mask
    )

    def thirds(v):
        return jnp.swapaxes(v, -3, -2).reshape(*v.shape[:-3], -1, v.shape[-1])

    def turned(v):
        return jnp.swapaxes(v, -2, -1)

    def same(v):
        return v

    views = (thirds, same, same, turned, thirds, turned, turned)
    masters = (
        attend_weight, merge_weight, expand_weight, shrink_weight, modulate_weight, pair_weight,
        class_weight,
    )
    states = (
        attend_state, merge_state, expand_state, shrink_state, modulate_state, pair_state,
        class_state,
    )
    groups = []
    for view, master, state, grad in zip(views, masters, states, grads):
        master = view(master)
        groups += [master, view(state), grad.reshape(master.shape)]
    out, res, pair_grad, *results = finish_call(ds, pw, out, res, *groups)

    def back(index, v):
        if index in (0, 4):
            count = masters[index].shape[1]
            return jnp.swapaxes(v.reshape(2, count, -1, v.shape[-1]), 1, 2)
        if index == 5:
            return jnp.transpose(v, (1, 2, 0))
        return v if index in (1, 2) else turned(v)

    return (out.T, res.T, pair_grad, *(back(i // 2, v) for i, v in enumerate(results)))


def solution(mesh):
    quick = mesh.shape["dp"] == 8 and mesh.shape["mp"] == 4
    placed = (
        P("dp", "mp"),
        P("dp", "mp", None, None),
        P("dp", "mp"),
        P("dp"),
        P("dp", None),
        P("dp", None),
        P("dp", None, "mp"),
        P(None, "dp", None, "mp"),
        P("mp", "dp"),
        P(None, "mp", "dp"),
        P("dp", None, "mp"),
        P(None, "dp", None, "mp"),
        P("mp", "dp"),
        P(None, "mp", "dp"),
        P("dp", None, "mp"),
        P(None, "dp", None, "mp"),
        P("dp", None),
        P(None, "dp", None),
        P(None, "dp"),
        P(None, None, "dp"),
    )
    return jax.shard_map(
        fast_local if quick else local,
        mesh=mesh,
        in_specs=placed,
        out_specs=(
            P("dp", "mp"),
            P("dp", "mp"),
            P("dp", "mp", None, None),
            P(None, "dp", None, "mp"),
            P(None, "dp", None, "mp"),
            P(None, "mp", "dp"),
            P(None, "mp", "dp"),
            P(None, "dp", None, "mp"),
            P(None, "dp", None, "mp"),
            P(None, "mp", "dp"),
            P(None, "mp", "dp"),
            P(None, "dp", None, "mp"),
            P(None, "dp", None, "mp"),
            P(None, "dp", None),
            P(None, "dp", None),
            P(None, None, "dp"),
            P(None, None, "dp"),
        ),
        check_vma=False,
    )
```

```python
import math

import jax
import jax.numpy as jnp
import numpy as np
from jax import lax
from jax.experimental import pallas as pl
from jax.experimental.pallas import tpu as pltpu
from jax.sharding import PartitionSpec as P

D = 768
HD = 64
FF = 3072
PAIR = 256
CDIM = 256
TBINS = 64
STEP = 10


PATTERNS = np.array(
    [[0, 0, 0, 0], [0, 0, 1, 1], [0, 0, 1, 2], [0, 1, 2, 2], [0, 1, 2, 3]], dtype=np.int32
)
NORM_EPS = 1e-06
BETA_ONE = 0.9
BETA_TWO = 0.999
ADAM_EPS = 1e-08
DECAY = 0.01
AVERAGE = 0.999
MASKED = -1e30
HIGH = lax.Precision.HIGHEST


def time_features(bins, width):
    half = width // 2
    moment = (bins.astype(jnp.float32) + 0.5) / TBINS
    freq = jnp.exp(-math.log(10000.0) * jnp.arange(half, dtype=jnp.float32) / half)
    angle = 1000.0 * moment[..., None] * freq
    return jnp.concatenate([jnp.sin(angle), jnp.cos(angle)], axis=-1)


def slot_ids(layout, window):
    unit = np.arange(window) // (window // 4)
    table = jnp.asarray(PATTERNS[:, unit])
    select = (layout[:, None] == jnp.arange(5, dtype=jnp.int32)[None, :]).astype(jnp.int32)
    return jnp.dot(select, table)


def adamw(master, state, grad, rate):
    first = BETA_ONE * state[0] + (1.0 - BETA_ONE) * grad
    second = BETA_TWO * state[1] + (1.0 - BETA_TWO) * grad * grad
    first_hat = first / (1.0 - BETA_ONE**STEP)
    second_hat = second / (1.0 - BETA_TWO**STEP)
    updated = master - rate * (first_hat / (jnp.sqrt(second_hat) + ADAM_EPS) + DECAY * master)
    average = AVERAGE * state[2] + (1.0 - AVERAGE) * updated
    return (jnp.stack([updated, average]), jnp.stack([first, second]))


def normalize(hidden, shift, scale, width):
    totals = lax.psum((jnp.sum(hidden, axis=1), jnp.sum(hidden * hidden, axis=1)), "mp")
    center = totals[0] / width
    spread = lax.rsqrt(totals[1] / width - center * center + NORM_EPS)
    normed = (hidden - center[:, None]) * spread[:, None]
    rows = (normed * (1.0 + scale) + shift).astype(jnp.bfloat16)
    return (normed, spread, lax.all_gather(rows, "mp", axis=1, tiled=True))


def normalize_back(partial_value, normed, spread, scale, width):
    upstream = lax.psum_scatter(partial_value, "mp", scatter_dimension=1, tiled=True)
    inner = upstream * (1.0 + scale)
    totals = lax.psum((jnp.sum(inner, axis=1), jnp.sum(inner * normed, axis=1)), "mp")
    result = spread[:, None] * (
        inner - totals[0][:, None] / width - normed * (totals[1][:, None] / width)
    )
    return (upstream, result)


def branch_total(partial_value):
    return lax.psum_scatter(partial_value, "mp", scatter_dimension=1, tiled=True)


def gather_grad(value):
    return lax.all_gather(value, "mp", axis=1, tiled=True)


def attention_scores(query, keys, bias, same, factor):
    scores = jnp.einsum(
        "wihe,wjhe->whij", query, keys, preferred_element_type=jnp.float32
    ) * factor + bias.astype(jnp.float32)
    return jnp.where(same[:, None], scores, MASKED)


def local(
    residues,
    pair_input,
    out_grad,
    bucket_layout,
    time_bins,
    fold_class,
    attend_weight,
    attend_state,
    merge_weight,
    merge_state,
    expand_weight,
    expand_state,
    shrink_weight,
    shrink_state,
    modulate_weight,
    modulate_state,
    pair_weight,
    pair_state,
    class_weight,
    class_state,
):
    parts = lax.axis_size("mp")
    gathered = (
        lax.all_gather(attend_weight.astype(jnp.bfloat16), "dp", axis=0, tiled=True),
        lax.all_gather(merge_weight.astype(jnp.bfloat16), "dp", axis=1, tiled=True),
        lax.all_gather(expand_weight.astype(jnp.bfloat16), "dp", axis=0, tiled=True),
        lax.all_gather(shrink_weight.astype(jnp.bfloat16), "dp", axis=1, tiled=True),
        lax.all_gather(modulate_weight.astype(jnp.bfloat16), "dp", axis=0, tiled=True),
        lax.all_gather(pair_weight.astype(jnp.bfloat16), "dp", axis=0, tiled=True),
        lax.all_gather(class_weight.astype(jnp.bfloat16), "dp", axis=1, tiled=True),
    )
    attend_full, merge_full, expand_full, shrink_full, modulate_full, pair_full, class_full = (
        gathered
    )
    tokens, local_width = residues.shape
    windows = bucket_layout.shape[0]
    window = tokens // windows
    slots = time_bins.shape[1]
    classes_count = class_full.shape[0]
    heads_local = local_width // HD
    width = local_width * parts
    factor = HD ** (-0.5)
    slot = slot_ids(bucket_layout, window)
    pick = (slot[..., None] == jnp.arange(slots, dtype=jnp.int32)).astype(jnp.float32)
    same = slot[:, :, None] == slot[:, None, :]
    class_pick = (fold_class[..., None] == jnp.arange(classes_count, dtype=jnp.int32)).astype(
        jnp.float32
    )
    before = time_features(time_bins, class_full.shape[1]) + jnp.einsum(
        "wsn,nc->wsc", class_pick, class_full.astype(jnp.float32), precision=HIGH
    )
    condition = jax.nn.silu(before).astype(jnp.bfloat16)
    modulation = jnp.einsum(
        "wsc,cjd->wsjd", condition, modulate_full, preferred_element_type=jnp.float32
    )
    per_token = jnp.einsum("wts,wsjd->wtjd", pick, modulation, precision=HIGH).reshape(
        tokens, 6, local_width
    )
    hidden_in = residues.astype(jnp.float32)
    normed_one, spread_one, rows_one = normalize(hidden_in, per_token[:, 0], per_token[:, 1], width)
    triple = jnp.einsum(
        "td,dje->tje", rows_one, attend_full, preferred_element_type=jnp.float32
    ).astype(jnp.bfloat16)
    query = triple[:, 0].reshape(windows, window, heads_local, HD)
    keys = triple[:, 1].reshape(windows, window, heads_local, HD)
    values = triple[:, 2].reshape(windows, window, heads_local, HD)
    local_bias = jnp.einsum(
        "wijc,ch->whij", pair_input, pair_full, preferred_element_type=jnp.float32
    ).astype(jnp.bfloat16)
    bias = lax.all_to_all(local_bias, "mp", split_axis=1, concat_axis=2, tiled=True)
    scores = attention_scores(query, keys, bias, same, factor)
    peak = jnp.max(scores, axis=-1, keepdims=True)
    logsum = peak + jnp.log(jnp.sum(jnp.exp(scores - peak), axis=-1, keepdims=True))
    chance = jnp.exp(scores - logsum).astype(jnp.bfloat16)
    mixed = (
        jnp.einsum("whij,wjhe->wihe", chance, values, preferred_element_type=jnp.float32)
        .astype(jnp.bfloat16)
        .reshape(tokens, local_width)
    )
    attended = branch_total(jnp.dot(mixed, merge_full, preferred_element_type=jnp.float32))
    middle = hidden_in + per_token[:, 2] * attended
    normed_two, spread_two, rows_two = normalize(middle, per_token[:, 3], per_token[:, 4], width)
    pair_up = jnp.einsum("td,dje->tje", rows_two, expand_full, preferred_element_type=jnp.float32)
    gate = pair_up[:, 0]
    upward = pair_up[:, 1]
    sigma = jax.nn.sigmoid(gate)
    activated = (gate * sigma * upward).astype(jnp.bfloat16)
    fed = branch_total(jnp.dot(activated, shrink_full, preferred_element_type=jnp.float32))
    output = (middle + per_token[:, 5] * fed).astype(jnp.bfloat16)
    upper = out_grad.astype(jnp.float32)
    fed_grad = gather_grad((per_token[:, 5] * upper).astype(jnp.bfloat16))
    act_grad = lax.dot_general(
        fed_grad, shrink_full, (((1,), (1,)), ((), ())), preferred_element_type=jnp.float32
    )
    shrink_grad = lax.dot_general(
        activated, fed_grad, (((0,), (0,)), ((), ())), preferred_element_type=jnp.float32
    )
    slope = sigma * (1.0 + gate * (1.0 - sigma))
    up_grads = jnp.stack([act_grad * upward * slope, act_grad * gate * sigma], axis=1).astype(
        jnp.bfloat16
    )
    expand_grad = jnp.einsum("td,tje->dje", rows_two, up_grads, preferred_element_type=jnp.float32)
    partial_two = jnp.einsum(
        "tje,dje->td", up_grads, expand_full, preferred_element_type=jnp.float32
    )
    upstream_two, norm_two = normalize_back(
        partial_two, normed_two, spread_two, per_token[:, 4], width
    )
    middle_grad = upper + norm_two
    merged_grad = gather_grad((per_token[:, 2] * middle_grad).astype(jnp.bfloat16))
    mixed_grad = (
        lax.dot_general(
            merged_grad, merge_full, (((1,), (1,)), ((), ())), preferred_element_type=jnp.float32
        )
        .astype(jnp.bfloat16)
        .reshape(windows, window, heads_local, HD)
    )
    merge_grad = lax.dot_general(
        mixed, merged_grad, (((0,), (0,)), ((), ())), preferred_element_type=jnp.float32
    )
    again = attention_scores(query, keys, bias, same, factor)
    exact = jnp.exp(again - logsum)
    chance_grad = jnp.einsum(
        "wihe,wjhe->whij", mixed_grad, values, preferred_element_type=jnp.float32
    )
    score_grad = (
        exact * (chance_grad - jnp.sum(exact * chance_grad, axis=-1, keepdims=True))
    ).astype(jnp.bfloat16)
    value_grad = jnp.einsum(
        "whij,wihe->wjhe",
        exact.astype(jnp.bfloat16),
        mixed_grad,
        preferred_element_type=jnp.float32,
    )
    query_grad = (
        jnp.einsum("whij,wjhe->wihe", score_grad, keys, preferred_element_type=jnp.float32) * factor
    )
    keys_grad = (
        jnp.einsum("whij,wihe->wjhe", score_grad, query, preferred_element_type=jnp.float32)
        * factor
    )
    triple_grad = jnp.stack(
        [
            query_grad.reshape(tokens, local_width),
            keys_grad.reshape(tokens, local_width),
            value_grad.reshape(tokens, local_width),
        ],
        axis=1,
    ).astype(jnp.bfloat16)
    bias_grad = lax.all_to_all(score_grad, "mp", split_axis=2, concat_axis=1, tiled=True)
    pair_grad = jnp.einsum(
        "whij,ch->wijc", bias_grad, pair_full, preferred_element_type=jnp.float32
    ).astype(jnp.bfloat16)
    pairwise_grad = jnp.einsum(
        "wijc,whij->ch", pair_input, bias_grad, preferred_element_type=jnp.float32
    )
    attend_grad = jnp.einsum(
        "td,tje->dje", rows_one, triple_grad, preferred_element_type=jnp.float32
    )
    partial_one = jnp.einsum(
        "tje,dje->td", triple_grad, attend_full, preferred_element_type=jnp.float32
    )
    upstream_one, norm_one = normalize_back(
        partial_one, normed_one, spread_one, per_token[:, 1], width
    )
    residue_grad = (middle_grad + norm_one).astype(jnp.bfloat16)
    token_mod_grad = jnp.stack(
        [
            upstream_one,
            upstream_one * normed_one,
            middle_grad * attended,
            upstream_two,
            upstream_two * normed_two,
            upper * fed,
        ],
        axis=1,
    ).reshape(windows, window, 6, local_width)
    mod_grad = jnp.einsum("wts,wtjd->wsjd", pick, token_mod_grad, precision=HIGH)
    modulate_grad = jnp.einsum(
        "wsc,wsjd->cjd", condition.astype(jnp.float32), mod_grad, precision=HIGH
    )
    cond_grad = jnp.einsum(
        "wsjd,cjd->wsc", mod_grad, modulate_full.astype(jnp.float32), precision=HIGH
    )
    sig_before = jax.nn.sigmoid(before)
    before_grad = cond_grad * (sig_before * (1.0 + before * (1.0 - sig_before)))
    class_grad = jnp.einsum("wsn,wsc->nc", class_pick, before_grad, precision=HIGH)
    shared = lax.psum((pairwise_grad, class_grad), "mp")
    sums = (
        lax.psum_scatter(attend_grad, "dp", scatter_dimension=0, tiled=True),
        lax.psum_scatter(merge_grad, "dp", scatter_dimension=1, tiled=True),
        lax.psum_scatter(expand_grad, "dp", scatter_dimension=0, tiled=True),
        lax.psum_scatter(shrink_grad, "dp", scatter_dimension=1, tiled=True),
        lax.psum_scatter(modulate_grad, "dp", scatter_dimension=0, tiled=True),
        lax.psum_scatter(shared[0], "dp", scatter_dimension=0, tiled=True),
        lax.psum_scatter(shared[1], "dp", scatter_dimension=1, tiled=True),
    )
    rates = (
        2.0 / math.sqrt(D),
        2.0 / math.sqrt(D // 8),
        2.0 / math.sqrt(D),
        2.0 / math.sqrt(FF),
        2.0 / math.sqrt(CDIM),
        2.0 / math.sqrt(PAIR),
        2.0,
    )
    masters = (
        attend_weight,
        merge_weight,
        expand_weight,
        shrink_weight,
        modulate_weight,
        pair_weight,
        class_weight,
    )
    states = (
        attend_state,
        merge_state,
        expand_state,
        shrink_state,
        modulate_state,
        pair_state,
        class_state,
    )
    results = []
    for index in range(7):
        updated, tracked = adamw(masters[index], states[index], sums[index], rates[index])
        results.append(updated)
        results.append(tracked)
    return (
        output,
        residue_grad,
        pair_grad,
        results[0],
        results[1],
        results[2],
        results[3],
        results[4],
        results[5],
        results[6],
        results[7],
        results[8],
        results[9],
        results[10],
        results[11],
        results[12],
        results[13],
    )


RATES = (
    2.0 / math.sqrt(D),
    2.0 / math.sqrt(D // 8),
    2.0 / math.sqrt(D),
    2.0 / math.sqrt(FF),
    2.0 / math.sqrt(CDIM),
    2.0 / math.sqrt(PAIR),
    2.0,
)
f32 = jnp.float32
bf16 = jnp.bfloat16
NT = (((1,), (1,)), ((), ()))
NN = (((1,), (0,)), ((), ()))
TN = (((0,), (0,)), ((), ()))
HEADS = 12
GROUP = 16
UNIT = 64
CHUNK = 16
PAIRS = 8


def mm(a, b, dims=NN, precision=None):
    return lax.dot_general(a, b, dims, precision=precision, preferred_element_type=f32)


def head_mask(count):
    row = lax.broadcasted_iota(jnp.int32, (count, GROUP, D), 1)
    col = lax.broadcasted_iota(jnp.int32, (count, GROUP, D), 2) // HD
    return row == col


def spread_heads(rows):
    count = rows.shape[0]
    wide = jnp.broadcast_to(rows.astype(f32)[:, None, :], (count, GROUP, D))
    return jnp.where(head_mask(count), wide, 0.0).astype(bf16).reshape(count * GROUP, D)


def merge_heads(wide):
    count = wide.shape[0] // GROUP
    return jnp.sum(jnp.where(head_mask(count), wide.reshape(count, GROUP, D), 0.0), axis=1)


class Net:
    def __init__(self, send_sems, recv_sems):
        self.d = lax.axis_index("dp")
        self.m = lax.axis_index("mp")
        core = self.d % 2
        x = (self.d // 2) % 2
        y = self.d // 4
        self.core = core
        self.chip = self.d // 2
        self.chips = [self.chip, y * 2 + 1 - x, (1 - y) * 2 + x, (1 - y) * 2 + 1 - x]
        self.partner = self.chip * 2 + 1 - core
        self.send_sems = send_sems
        self.recv_sems = recv_sems
        self.sent = []
        self.open = []
        self.base = 0

    def z(self, t):
        return (self.m + t) % 4

    def peer(self, r):
        return self.chips[r] * 2 + self.core

    def sems(self, count):
        base = self.base
        self.base = base + count
        return base

    def barrier(self):
        sem = pltpu.get_barrier_semaphore()
        targets = [(self.d, self.z(t)) for t in (1, 2, 3)]
        targets += [(self.peer(r), self.m) for r in (1, 2, 3)] + [(self.partner, self.m)]
        for target in targets:
            pl.semaphore_signal(
                sem, inc=1, device_id=target, device_id_type=pl.DeviceIdType.MESH
            )
        pl.semaphore_wait(sem, len(targets))

    def copy(self, src, dst, recv, target, send=None):
        send = len(self.sent) if send is None else send
        return pltpu.make_async_remote_copy(
            src_ref=src,
            dst_ref=dst,
            send_sem=self.send_sems.at[send],
            recv_sem=self.recv_sems.at[recv],
            device_id=target,
            device_id_type=pl.DeviceIdType.MESH,
        )

    def send(self, src, dst, recv, target):
        made = self.copy(src, dst, recv, target)
        made.start()
        self.sent.append(made)
        self.open.append(made)
        return made

    def wait(self, dst, recv):
        self.copy(dst, dst, recv, (self.partner, self.m), 0).wait_recv()

    def drain(self):
        for made in self.open:
            made.wait_send()

    def settle(self, made):
        made.wait_send()
        self.open = [other for other in self.open if other is not made]


class Spread:
    def __init__(self, net, slot):
        self.net, self.slot, self.base = net, slot, net.sems(7)

    def start(self, src=None):
        net = self.net
        own = self.slot(net.d)
        src = own if src is None else src
        for r in (1, 2, 3):
            net.send(src, own, self.base + r, (net.peer(r), net.m))
        net.send(src, own, self.base, (net.partner, net.m))

    def forward(self, r):
        net = self.net
        slot = self.slot(net.peer(r))
        net.wait(slot, self.base + r)
        return [net.send(slot, slot, self.base + 3 + r, (net.partner, net.m))]

    def finish(self):
        net = self.net
        net.wait(self.slot(net.partner), self.base)
        for r in (1, 2, 3):
            net.wait(self.slot(net.chips[r] * 2 + 1 - net.core), self.base + 3 + r)


class Zline:
    def __init__(self, net, slot):
        self.net, self.slot, self.base = net, slot, net.sems(4)

    def send(self, t, src):
        net = self.net
        net.send(src, self.slot(net.m), self.base + net.m, (net.d, net.z(t)))

    def wait(self, t):
        net = self.net
        source = net.z(t)
        net.wait(self.slot(source), self.base + source)
        return source


def layer_kernel(
    ms, am, es, xp, gp, pair, sinus, pick, mask,
    out_o, res_o, ds_o, pw_o, at_o, mg_o, ex_o, sh_o, mod_o, pair_o, class_o,
    msg, amg, esg, xg, gg, modu, modg, modf, bpg, pb, bias, n1, sp1, r1,
    kf, vf, qf, pr, mix, att, mid, n2, sp2, r2, fg, act, upg, fp, fl, p2, p2l, p2o, fpo,
    esp, epl, exl, eso, dkv, dkf, dvf, dqf, mgd, l2, rhs2, p1, p1l,
    amp, axl, aso, azs, azl, mps, mpl, mrg, pws, pwl, pwx, pwy, pco, pcl,
    ops, opl, rps, rpl, ctf, cfull,
    send_sems, recv_sems, pair_sems,
):
    net = Net(send_sems, recv_sems)
    d, m = net.d, net.m
    net.barrier()

    chunks = 16
    slots = pb.shape[0]

    def pair_copy(step):
        c = step % chunks
        return pltpu.make_async_copy(
            pair.at[c // 8, pl.ds((c % 8) * PAIRS, PAIRS)],
            pb.at[step % slots],
            pair_sems.at[step % slots],
        )

    for step in range(slots):
        pair_copy(step).start()

    cp_all = Spread(net, lambda i: msg.at[i, :, 0:128])
    ms_all = Spread(net, lambda i: msg.at[i, :, 128:1280])
    am_line = Zline(net, lambda s: amg.at[s, d])
    am_all = [Spread(net, lambda i, t=t: amg.at[net.z(t), i]) for t in range(4)]
    x_line = Zline(net, lambda s: xg.at[s])
    g_line = Zline(net, lambda s: gg.at[s])
    mod_line = Zline(net, lambda s: modg.at[s])
    bp_all = Spread(net, lambda i: bpg.at[i])
    es_all = Spread(net, lambda i: esg.at[i])

    cp_all.start(ms.at[:, 0:128])
    for t in (1, 3, 2):
        am_line.send(t, am)
    ms_all.start(ms.at[:, 128:1280])
    am_all[0].start(am)
    msg[d] = ms[...]
    amg[m, d] = am[...]
    esg[d] = es[...]
    xg[m] = xp[...]
    gg[m] = gp[...]
    for r in (1, 2, 3):
        cp_all.forward(r)
    cp_all.finish()

    slab = msg[:, :, 0:128].reshape(256, 128)
    select = (
        lax.broadcasted_iota(jnp.int32, (GROUP, 128), 1)
        == lax.broadcasted_iota(jnp.int32, (GROUP, 128), 0) + 64
    ) & (lax.broadcasted_iota(jnp.int32, (GROUP, 128), 0) < HEADS)
    pw_o[...] = mm(jnp.where(select, 1.0, 0.0).astype(bf16), slab, NT).astype(bf16)
    before = sinus[...] + mm(pick[...], slab, NT)
    condition = (before * jax.nn.sigmoid(before)).astype(bf16)
    bpg[d] = jnp.concatenate([before, pick[...].astype(f32)], axis=-1)

    def bias_chunk(step):
        slot = step % slots
        pair_copy(step).wait()

        def one(i, carry):
            part = mm(pw_o[...], pb[slot, i], NT)
            at = pl.multiple_of((step % 8) * PAIRS * GROUP + i * GROUP, GROUP)
            bias[step // 8, pl.ds(at, GROUP), :] = part.astype(bf16)
            return carry

        lax.fori_loop(0, PAIRS, one, 0, unroll=4)
        pair_copy(step + slots).start()

    bias_chunk(0)
    bias_chunk(1)
    for r in (1, 2, 3):
        ms_all.forward(r)
    bias_chunk(2)
    am_line.wait(1)
    am_all[1].start()
    bias_chunk(3)
    ms_all.finish()
    modu[...] = mm(condition, msg[:, :, 128:1280].reshape(256, 1152))
    modg[m] = modu[...]
    am_line.wait(3)
    am_all[3].start()
    bias_chunk(4)
    for r in (1, 2):
        am_all[0].forward(r)
    bias_chunk(5)
    am_line.wait(2)
    am_all[2].start()
    for t in (1, 2, 3):
        x_line.send(t, xp)
    for t in (1, 2, 3):
        mod_line.send(t, modu)
    bias_chunk(6)
    am_all[0].forward(3)
    bias_chunk(7)
    for r in (1, 2):
        am_all[1].forward(r)
    for step in (8, 9, 10):
        bias_chunk(step)
    am_all[1].forward(3)
    for r in (1, 2):
        am_all[3].forward(r)
    for step in (11, 12, 13):
        bias_chunk(step)
    am_all[3].forward(3)
    for r in (1, 2):
        am_all[2].forward(r)
    bias_chunk(14)
    bias_chunk(15)

    for t in (1, 2, 3):
        mod_line.wait(t)
    for j in range(6):
        modf[j] = jnp.concatenate([modg[s, :, 192 * j : 192 * j + 192] for s in range(4)], axis=-1)
    for t in (1, 2, 3):
        x_line.wait(t)

    def unpack(ref, w, unit):
        parts = []
        for s in range(4):
            parts.append(ref[s, pl.ds(w * 256 + unit * UNIT, UNIT), :].astype(f32))
            low = ref[s, pl.ds(512 + unit * UNIT, UNIT), :].astype(f32)
            parts.append(low[:, 64 * w : 64 * w + 64])
        return jnp.concatenate(parts, axis=-1)

    def norm(v):
        center = jnp.mean(v, axis=-1, keepdims=True)
        spread = lax.rsqrt(jnp.mean(v * v, axis=-1, keepdims=True) - center * center + NORM_EPS)
        return (v - center) * spread, spread

    for w in range(2):

        def first_norm(unit, carry, w=w):
            v = unpack(xg, w, unit)
            rows = pl.ds(pl.multiple_of(w * 256 + unit * UNIT, UNIT), UNIT)
            normed, spread = norm(v)
            n1[rows, :] = normed
            sp1[rows, :] = jnp.broadcast_to(spread, (UNIT, 128))
            shift = modf[0, pl.ds(w * 4 + unit, 1), :]
            scale = modf[1, pl.ds(w * 4 + unit, 1), :]
            r1[rows, :] = (normed * (1.0 + scale) + shift).astype(bf16)
            return carry

        lax.fori_loop(0, 4, first_norm, 0)

    am_all[2].forward(3)
    es_all.start(es)
    for t in (1, 2, 3):
        g_line.send(t, gp)
    bp_all.start()
    for t in (0, 1, 3, 2):
        am_all[t].finish()

    def own(w):
        return pl.ds(pl.multiple_of(w * 256 + m * UNIT, UNIT), UNIT)

    def weight(s, lo, hi):
        return amg[s, :, :, lo:hi].reshape(D, hi - lo)

    r1_own = jnp.concatenate([r1[own(0), :], r1[own(1), :]], axis=0)
    qf[...] = jnp.concatenate(
        [mm(r1_own, weight(s, 384, 768))[:, 0:192] for s in range(4)], axis=-1
    ).astype(bf16)
    for w in range(2):
        rows = slice(w * 256, w * 256 + 256)
        both = [mm(r1[rows, :], weight(s, 0, 384)) for s in range(4)]
        kf[rows, :] = jnp.concatenate([v[:, 0:192] for v in both], axis=-1).astype(bf16)
        vf[rows, :] = jnp.concatenate([v[:, 192:384] for v in both], axis=-1).astype(bf16)

    factor = HD ** (-0.5)

    def attend(c, carry):
        w = c // 4
        mine = pl.ds(pl.multiple_of(c * CHUNK, CHUNK), CHUNK)
        keys = pl.ds(pl.multiple_of(w * 256, 256), 256)
        wide = pl.ds(pl.multiple_of((c % 4) * CHUNK * GROUP, CHUNK * GROUP), CHUNK * GROUP)
        scores = mm(spread_heads(qf[mine, :]), kf[keys, :], NT) * factor
        scores = scores + bias[w, wide, :].astype(f32) + mask[pl.ds(w, 1), :]
        peak = jnp.max(scores, axis=-1, keepdims=True)
        expo = jnp.exp(scores - peak)
        chance = expo / jnp.sum(expo, axis=-1, keepdims=True)
        pr[w, wide, :] = chance
        mix[mine, :] = merge_heads(mm(chance.astype(bf16), vf[keys, :])).astype(bf16)
        return carry

    def mod_row(j, w):
        return modf[j, pl.ds(w * 4 + m, 1), :]

    blank = jnp.zeros((128, 192), bf16)
    r2_lines = []
    es_sent = []
    for w in range(2):
        half = slice(w * UNIT, w * UNIT + UNIT)
        lax.fori_loop(4 * w, 4 * w + 4, attend, 0)
        mixed = mix[half, :]
        attended = 0.0
        for s in range(4):
            part = jnp.concatenate([blank[:UNIT], mixed[:, 192 * s : 192 * s + 192]], axis=-1)
            attended = attended + mm(part, weight(s, 384, 768), NT)
        att[half, :] = attended
        middle = unpack(xg, w, m) + mod_row(2, w) * attended
        mid[half, :] = middle
        normed, spread = norm(middle)
        n2[half, :] = normed
        sp2[half, :] = jnp.broadcast_to(spread, (UNIT, 128))
        r2[m, half, :] = (normed * (1.0 + mod_row(4, w)) + mod_row(3, w)).astype(bf16)
        line = Zline(net, lambda s, half=half: r2.at[s, half])
        r2_lines.append(line)
        for t in (1, 3, 2):
            line.send(t, r2.at[m, half])
        for r in ((1, 2), (3,))[w]:
            es_sent += es_all.forward(r)

    for t in (1, 2, 3):
        g_line.wait(t)
    for s in range(4):
        for w in range(2):
            half = slice(w * UNIT, w * UNIT + UNIT)
            upper = unpack(gg, w, s)
            fg[s, half, :] = (modf[5, w * 4 + s : w * 4 + s + 1, :] * upper).astype(bf16)
    es_all.finish()

    p2_line = Zline(net, lambda s: p2l.at[s])
    f_line = Zline(net, lambda s: fl.at[s])

    def feed(s):
        expand = esg[:, :, 0:1536].reshape(D, 1536)
        shrink = esg[:, :, 1536:2304].reshape(D, 768)
        up = mm(r2[s], expand)
        gate = up[:, 0:768]
        upward = up[:, 768:1536]
        act_grad = mm(fg[s], shrink)
        sigma = jax.nn.sigmoid(gate)
        activated = (gate * sigma * upward).astype(bf16)
        act[s] = activated
        slope = sigma * (1.0 + gate * (1.0 - sigma))
        grads = jnp.concatenate(
            [(act_grad * upward * slope).astype(bf16), (act_grad * gate * sigma).astype(bf16)],
            axis=-1,
        )
        upg[s] = grads
        return mm(grads, expand, NT), mm(activated, shrink, NT)

    partial, fed = feed(m)
    p2o[...] = partial
    fpo[...] = fed
    for t in (1, 3, 2):
        for line in r2_lines:
            source = line.wait(t)
        partial, fed = feed(source)
        p2[source] = partial.astype(bf16)
        p2_line.send(t, p2.at[source])
        fp[source] = fed.astype(bf16)

    def put_es(left, right, at):
        for h in range(2):
            value = mm(left[:, :, 384 * h : 384 * h + 384].reshape(512, 384), right, TN)
            for i in range(4):
                part = value[96 * i : 96 * i + 96, :].astype(bf16)
                esp[i % 2, 2 * h + i // 2, :, at : at + 768] = part

    put_es(r2, upg[:, :, 0:768].reshape(512, 768), 0)
    put_es(r2, upg[:, :, 768:1536].reshape(512, 768), 768)
    put_es(fg, act[...].reshape(512, 768), 1536)
    for made in es_sent:
        net.settle(made)
    es_pair = net.sems(1)
    net.send(esp.at[1 - net.core], epl, es_pair, (net.partner, m))

    for t in (1, 3, 2):
        p2_line.wait(t)
    for t in (1, 3, 2):
        f_line.send(t, fp.at[net.z(t)])

    def norm_back(upstream, normed, spread, scale):
        inner = upstream * (1.0 + scale)
        first = jnp.mean(inner, axis=-1, keepdims=True)
        second = jnp.mean(inner * normed, axis=-1, keepdims=True)
        return spread * (inner - first - normed * second)

    def unit_sum(v):
        return jnp.sum(v, axis=0, keepdims=True)

    own_sums = [[None] * 6, [None] * 6]
    for w in range(2):
        half = slice(w * UNIT, w * UNIT + UNIT)
        upstream = p2o[half, :]
        for t in (1, 3, 2):
            upstream = upstream + p2l[net.z(t), half, :].astype(f32)
        normed = n2[half, :]
        back = norm_back(upstream, normed, sp2[half, 0:1], mod_row(4, w))
        grad = unpack(gg, w, m) + back
        p2o[half, :] = grad
        own_sums[w][2] = unit_sum(grad * att[half, :])
        own_sums[w][3] = unit_sum(upstream)
        own_sums[w][4] = unit_sum(upstream * normed)
        l2[slice(128 + w * UNIT, 128 + w * UNIT + UNIT), :] = (mod_row(2, w) * grad).astype(bf16)
        l2[half, :] = r1[own(w), :]
    merged_grad = l2[128:256, :]
    mgd[...] = jnp.concatenate(
        [mm(merged_grad, weight(s, 384, 768))[:, 192:384] for s in range(4)], axis=-1
    ).astype(bf16)

    net.wait(epl, es_pair)
    es_chip = net.sems(4)
    for r in (1, 2, 3, 0):
        total = esp[net.core, net.chips[r]].astype(f32) + epl[net.chips[r]].astype(f32)
        if r == 0:
            eso[...] = total
        else:
            esp[net.core, net.chips[r]] = total.astype(bf16)
            net.send(
                esp.at[net.core, net.chips[r]], exl.at[r - 1], es_chip + r, (net.peer(r), m)
            )

    dkf[...] = jnp.zeros_like(dkf)
    dvf[...] = jnp.zeros_like(dvf)

    def attend_back(c, carry):
        w = c // 4
        mine = pl.ds(pl.multiple_of(c * CHUNK, CHUNK), CHUNK)
        keys = pl.ds(pl.multiple_of(w * 256, 256), 256)
        wide = pl.ds(pl.multiple_of((c % 4) * CHUNK * GROUP, CHUNK * GROUP), CHUNK * GROUP)
        grad = spread_heads(mgd[mine, :])
        chance = pr[w, wide, :]
        chance_grad = mm(grad, vf[keys, :], NT)
        inner = jnp.sum(chance * chance_grad, axis=-1, keepdims=True)
        score = (chance * (chance_grad - inner)).astype(bf16)
        ds_o[w, wide, :] = score
        dqf[mine, :] = (merge_heads(mm(score, kf[keys, :])) * factor).astype(bf16)
        dvf[keys, :] += mm(chance.astype(bf16), grad, TN)
        dkf[keys, :] += mm(score, spread_heads(qf[mine, :]), TN) * factor
        return carry

    lax.fori_loop(0, 8, attend_back, 0)

    o_line = Zline(net, lambda s: opl.at[s])

    def pack(line, value, ref):
        for s in range(4):
            part = value[:, 192 * s : 192 * s + 192]
            ref[s, 0:128, :] = part[:, 0:128].astype(bf16)
            low = part[:, 128:192]
            ref[s, 128:192, :] = jnp.concatenate([low[0:64], low[64:128]], axis=-1).astype(bf16)
        for t in (1, 3, 2):
            line.send(t, ref.at[net.z(t)])

    def unpack_out(line, ref, mine, to):
        for t in (0, 1, 3, 2):
            s = net.z(t)
            block = mine if t == 0 else ref
            if t:
                line.wait(t)
            for w in range(2):
                rows = pl.ds(pl.multiple_of(w * 256 + s * UNIT, UNIT), UNIT)
                high = block[s, w * UNIT : w * UNIT + UNIT, :].astype(f32)
                low = block[s, 128:192, :].astype(f32)[:, 64 * w : 64 * w + 64]
                to[rows, :] = jnp.concatenate([high, low], axis=-1).astype(bf16)

    for t in (1, 3, 2):
        f_line.wait(t)
    done = []
    for w in range(2):
        half = slice(w * UNIT, w * UNIT + UNIT)
        fed = fpo[half, :]
        for t in (1, 3, 2):
            fed = fed + fl[net.z(t), half, :].astype(f32)
        own_sums[w][5] = unit_sum(unpack(gg, w, m) * fed)
        done.append(mid[half, :] + mod_row(5, w) * fed)
    pack(o_line, jnp.concatenate(done, axis=0), ops)

    for s in range(4):
        cols = slice(192 * s, 192 * s + 192)
        dkv[s] = jnp.concatenate([dkf[:, cols], dvf[:, cols]], axis=-1).astype(bf16)
        rhs2[s, 0:128, :] = jnp.concatenate([dqf[:, cols], blank], axis=-1)
        rhs2[s, 128:256, :] = jnp.concatenate([blank, mix[:, cols]], axis=-1)
    am_pair = net.sems(4)

    def apl(t):
        return esg.at[pl.ds(4 * (t // 3), 4), :, 768 * (t % 3) : 768 * (t % 3) + 768]

    for t in (1, 3, 2, 0):
        s = net.z(t)
        for h in range(2):
            cols = slice(384 * h, 384 * h + 384)
            for left, right, at in ((r1, dkv, 0), (l2, rhs2, 384)):
                value = mm(left[:, cols], right[s], TN)
                for i in range(4):
                    part = value[96 * i : 96 * i + 96, :].astype(bf16)
                    amp[s, i % 2, 2 * h + i // 2, :, at : at + 384] = part
        net.send(amp.at[s, 1 - net.core], apl(t), am_pair + t, (net.partner, m))

    for w in range(2):
        rows = slice(w * 256, w * 256 + 256)
        total = mm(dkv[0, rows, :], weight(0, 0, 384), NT)
        for s in range(1, 4):
            total = total + mm(dkv[s, rows, :], weight(s, 0, 384), NT)
        dkf[rows, :] = total
    total = mm(rhs2[0, 0:128, :], weight(0, 384, 768), NT)
    for s in range(1, 4):
        total = total + mm(rhs2[s, 0:128, :], weight(s, 384, 768), NT)
    for w in range(2):
        dkf[own(w), :] += total[w * UNIT : w * UNIT + UNIT, :]
    p1_line = Zline(net, lambda s: p1l.at[s])
    for t in (1, 3, 2):
        s = net.z(t)
        for w in range(2):
            rows = pl.ds(pl.multiple_of(w * 256 + s * UNIT, UNIT), UNIT)
            p1[s, w * UNIT : w * UNIT + UNIT, :] = dkf[rows, :].astype(bf16)
        p1_line.send(t, p1.at[s])

    sums = [[], []]
    for u in range(8):
        rows = slice(u * UNIT, u * UNIT + UNIT)
        sums[0].append(unit_sum(dkf[rows, :]))
        sums[1].append(unit_sum(dkf[rows, :] * n1[rows, :]))
    row = lax.broadcasted_iota(jnp.int32, (8, D), 0)
    table = [jnp.concatenate(sums[0], axis=0), jnp.concatenate(sums[1], axis=0)]
    for j in range(2, 6):
        first = jnp.broadcast_to(own_sums[0][j], (8, D))
        second = jnp.broadcast_to(own_sums[1][j], (8, D))
        table.append(jnp.where(row == m, first, jnp.where(row == m + 4, second, 0.0)))
    mod_sum = Zline(net, lambda s: mpl.at[s])
    for s in range(4):
        mps[s] = jnp.concatenate([v[:, 192 * s : 192 * s + 192] for v in table], axis=-1)
    for t in (1, 3, 2):
        mod_sum.send(t, mps.at[net.z(t)])

    def pair_chunk(step, acc):
        slot = step % slots
        pair_copy(step).wait()

        def one(i, acc):
            at = pl.multiple_of((step % 8) * PAIRS * GROUP + i * GROUP, GROUP)
            return acc + mm(ds_o[(step - 16) // 8, pl.ds(at, GROUP), :], pb[slot, i])

        acc = lax.fori_loop(0, PAIRS, one, acc, unroll=4)
        if step + slots < 2 * chunks:
            pair_copy(step + slots).start()
        return acc

    pairwise = jnp.zeros((GROUP, 256), f32)
    am_chip = net.sems(16)
    step = 16
    for t in (1, 3, 2, 0):
        s = net.z(t)
        net.wait(apl(t), am_pair + t)
        base, cols = 4 * (t // 3), slice(768 * (t % 3), 768 * (t % 3) + 768)
        for r in (1, 2, 3, 0):
            total = amp[s, net.core, net.chips[r]].astype(f32)
            total = total + esg[base + net.chips[r], :, cols].astype(f32)
            if r == 0:
                aso[s] = total
            else:
                amp[s, net.core, net.chips[r]] = total.astype(bf16)
                net.send(
                    amp.at[s, net.core, net.chips[r]],
                    axl.at[s, r - 1],
                    am_chip + 4 * t + r,
                    (net.peer(r), m),
                )
        for _ in range(4):
            pairwise = pair_chunk(step, pairwise)
            step += 1

    for r in (1, 2, 3):
        bp_all.forward(r)
    bp_all.finish()

    wide = jnp.concatenate([pairwise, jnp.zeros((112, 256), f32)], axis=0).T
    for i in range(8):
        pws[i % 2, i // 2] = wide[32 * i : 32 * i + 32, :]
    pw_pair = net.sems(1)
    net.send(pws.at[1 - net.core], pwl, pw_pair, (net.partner, m))

    for t in (1, 3, 2):
        mod_sum.wait(t)
    mod_grad = mps[m]
    for t in (1, 3, 2):
        mod_grad = mod_grad + mpl[net.z(t)]
    mrg[d] = mod_grad
    mr_all = Spread(net, lambda i: mrg.at[i])
    mr_all.start()

    am_z = Zline(net, lambda s: azl.at[s])

    def am_arrive(t):
        s = net.z(t)
        total = aso[s]
        for r in (1, 2, 3):
            net.wait(axl.at[s, r - 1], am_chip + 4 * t + r)
            total = total + axl[s, r - 1].astype(f32)
        if t:
            azs[s] = total.astype(bf16)
            am_z.send(t, azs.at[s])
        else:
            aso[s] = total

    am_arrive(1)

    for t in (1, 3, 2):
        p1_line.wait(t)
    r_line = Zline(net, lambda s: rpl.at[s])
    done = []
    for w in range(2):
        half = slice(w * UNIT, w * UNIT + UNIT)
        upstream = dkf[own(w), :]
        for t in (1, 3, 2):
            upstream = upstream + p1l[net.z(t), half, :].astype(f32)
        back = norm_back(upstream, n1[own(w), :], sp1[own(w), :][:, 0:1], mod_row(1, w))
        done.append(p2o[half, :] + back)
    pack(r_line, jnp.concatenate(done, axis=0), rps)

    am_arrive(3)
    am_arrive(2)

    total = eso[...]
    for r in (1, 2, 3):
        net.wait(exl.at[r - 1], es_chip + r)
        total = total + exl[r - 1].astype(f32)
    for k in range(2):
        ex_o[:, k, :] = total[:, 768 * k : 768 * k + 768]
    sh_o[...] = total[:, 1536:2304]

    net.wait(pwl, pw_pair)
    pw_chip = net.sems(4)
    for r in (1, 2, 3):
        pwx[r] = pws[net.core, net.chips[r]] + pwl[net.chips[r]]
        net.send(pwx.at[r], pwy.at[r], pw_chip + r, (net.peer(r), m))
    pair_sum = pws[net.core, net.chip] + pwl[net.chip]

    for r in (1, 2, 3):
        mr_all.forward(r)
    am_arrive(0)

    mr_all.finish()
    before = bpg[:, :, 0:256].reshape(64, 256)
    sig = jax.nn.sigmoid(before)
    condition = (before * sig).astype(bf16).astype(f32)
    picks = bpg[:, :, 256:384].reshape(64, 128)
    grads = mrg[...].reshape(64, 1152)
    ctf[...] = condition.T
    mod_sums = mm(ctf[pl.ds(pl.multiple_of(d * 32, 32), 32), :], grads, NN, HIGH)
    for j in range(6):
        mod_o[j] = mod_sums[:, 192 * j : 192 * j + 192]
    cond_grad = mm(grads, msg[:, :, 128:1280].reshape(256, 1152).astype(f32), NT, HIGH)
    before_grad = cond_grad * (sig * (1.0 + before * (1.0 - sig)))
    cfull[...] = mm(before_grad, picks, TN, HIGH)
    for r in (1, 2, 3):
        net.wait(pwy.at[r], pw_chip + r)
        pair_sum = pair_sum + pwy[r]
    pco[...] = jnp.concatenate(
        [pair_sum, cfull[pl.ds(pl.multiple_of(d * 32, 32), 32), :]], axis=-1
    )
    pc_line = Zline(net, lambda s: pcl.at[s])
    for t in (1, 3, 2):
        pc_line.send(t, pco)

    unpack_out(o_line, opl, ops, out_o)
    unpack_out(r_line, rpl, rps, res_o)
    total = aso[m]
    for t in (1, 3, 2):
        total = total + azl[am_z.wait(t)].astype(f32)
    at_o[0] = total[:, 384:576]
    at_o[1] = total[:, 0:192]
    at_o[2] = total[:, 192:384]
    tall = jnp.concatenate([total[:, 512:768], jnp.zeros((32, 256), f32)], axis=0).T
    mg_o[...] = tall[64:256, 0:96]
    total = pco[...]
    for t in (1, 3, 2):
        total = total + pcl[pc_line.wait(t)]
    tall = jnp.concatenate([total[:, 0:128], jnp.zeros((96, 128), f32)], axis=0).T
    pair_o[...] = tall[0:HEADS, 0:32]
    class_o[...] = total[:, 128 : 128 + class_o.shape[1]]
    net.drain()


def layer_call(classes, *args):
    V = pltpu.VMEM
    scratch = [
        V((8, 32, 1280), bf16), V((4, 8, 96, 768), bf16), V((8, 96, 2304), bf16),
        V((4, 768, 128), bf16), V((4, 768, 128), bf16),
        V((8, 1152), f32), V((4, 8, 1152), f32), V((6, 8, 768), f32), V((8, 8, 384), f32),
        V((2, PAIRS, 256, 256), bf16), V((2, 1024, 256), bf16),
        V((512, 768), f32), V((512, 128), f32), V((512, 768), bf16),
        V((512, 768), bf16), V((512, 768), bf16), V((128, 768), bf16), V((2, 1024, 256), f32),
        V((128, 768), bf16), V((128, 768), f32), V((128, 768), f32), V((128, 768), f32),
        V((128, 128), f32),
        V((4, 128, 768), bf16), V((4, 128, 768), bf16), V((4, 128, 768), bf16),
        V((4, 128, 1536), bf16), V((4, 128, 768), bf16), V((4, 128, 768), bf16),
        V((4, 128, 768), bf16), V((4, 128, 768), bf16), V((128, 768), f32), V((128, 768), f32),
        V((2, 4, 96, 2304), bf16), V((4, 96, 2304), bf16), V((3, 96, 2304), bf16),
        V((96, 2304), f32),
        V((4, 512, 384), bf16), V((512, 768), f32), V((512, 768), f32), V((128, 768), bf16),
        V((128, 768), bf16), V((256, 768), bf16), V((4, 256, 384), bf16),
        V((4, 128, 768), bf16), V((4, 128, 768), bf16),
        V((4, 2, 4, 96, 768), bf16), V((4, 3, 96, 768), bf16),
        V((4, 96, 768), f32), V((4, 96, 768), bf16), V((4, 96, 768), bf16),
        V((4, 8, 1152), f32), V((4, 8, 1152), f32), V((8, 8, 1152), f32),
        V((2, 4, 32, 128), f32), V((4, 32, 128), f32), V((4, 32, 128), f32), V((4, 32, 128), f32),
        V((32, 256), f32), V((4, 32, 256), f32),
        V((4, 192, 128), bf16), V((4, 192, 128), bf16), V((4, 192, 128), bf16),
        V((4, 192, 128), bf16), V((256, 64), f32), V((256, 128), f32),
        pltpu.SemaphoreType.DMA((160,)), pltpu.SemaphoreType.DMA((160,)),
        pltpu.SemaphoreType.DMA((2,)),
    ]
    whole = pl.BlockSpec(memory_space=pltpu.VMEM)
    outs = (
        ((512, 192), bf16), ((512, 192), bf16), ((2, 1024, 256), bf16), ((16, 256), bf16),
        ((3, 96, 192), f32), ((192, 96), f32), ((96, 2, 768), f32), ((96, 768), f32),
        ((6, 32, 192), f32), ((HEADS, 32), f32), ((32, classes), f32),
    )
    return pl.pallas_call(
        layer_kernel,
        out_shape=tuple(jax.ShapeDtypeStruct(s, t) for s, t in outs),
        in_specs=[pl.BlockSpec(memory_space=pl.ANY) if i == 5 else whole for i in range(9)],
        out_specs=(whole,) * len(outs),
        scratch_shapes=scratch,
        compiler_params=pltpu.CompilerParams(
            collective_id=0, has_side_effects=True, vmem_limit_bytes=67043328
        ),
        name="layer",
    )(*args)


def finish_kernel(*refs):
    ds, pw, out, res = refs[0:4]
    groups = [refs[4 + 3 * i : 7 + 3 * i] for i in range(7)]
    out_t, res_t, pair = refs[25:28]
    results = [refs[28 + 2 * i : 30 + 2 * i] for i in range(7)]
    block, sems = refs[42:44]
    step = pl.program_id(0)

    def put(c, at):
        rows = pl.ds((at % 2) * 32 + 8 * c, 8)
        return pltpu.make_async_copy(block.at[c], pair.at[at // 2, rows], sems.at[c])

    def update(index):
        (master, state, grad), (fresh, kept) = groups[index], results[index]
        old, slope = master[...], grad[...]
        first = BETA_ONE * state[0] + (1.0 - BETA_ONE) * slope
        second = BETA_TWO * state[1] + (1.0 - BETA_TWO) * slope * slope
        first_hat = first / (1.0 - BETA_ONE**STEP)
        second_hat = second / (1.0 - BETA_TWO**STEP)
        new = old - RATES[index] * (first_hat / (jnp.sqrt(second_hat) + ADAM_EPS) + DECAY * old)
        average = AVERAGE * state[2] + (1.0 - AVERAGE) * new
        for ref, values in ((fresh, (new, average)), (kept, (first, second))):
            for i in range(2):
                if index == 5:
                    ref[:, i, :] = values[i]
                else:
                    ref[i] = values[i]

    def turn(source, target):
        wide = jnp.concatenate([source[...].astype(f32), jnp.zeros((128, 64), f32)], axis=-1)
        target[...] = wide.T[0:192, :].astype(bf16)

    for c in range(4):

        @pl.when(step > 0)
        def _(c=c):
            put(c, step - 1).wait()

        for i in range(8):
            at = GROUP * (8 * c + i)
            block[c, i] = mm(ds[0, at : at + GROUP, :], pw[...], TN).astype(bf16)
        if c == 0:
            update(0)
            update(1)
            turn(out, out_t)
        elif c == 1:
            update(2)
        elif c == 2:
            update(3)
            turn(res, res_t)
        else:
            for index in (4, 5, 6):
                update(index)
        put(c, step).start()

    @pl.when(step == 3)
    def _():
        for c in range(4):
            put(c, step).wait()


def finish_call(ds, pw, out, res, *groups):
    def rows(shape, axis=-2):
        at = len(shape) + axis
        block = (*shape[:at], shape[at] // 4, *shape[at + 1 :])
        return pl.BlockSpec(block, lambda i: (0,) * at + (i,) + (0,) * (-1 - axis))

    def whole(shape):
        return pl.BlockSpec(tuple(shape), lambda i: (0,) * len(shape))

    in_specs = [
        pl.BlockSpec((1, 512, 256), lambda i: (i // 2, i % 2, 0)), whole((16, 256)),
        rows((512, 192)), rows((512, 192)),
    ]
    turned = pl.BlockSpec((192, 128), lambda i: (0, i))
    out_specs = [turned, turned, pl.BlockSpec(memory_space=pl.ANY)]
    outs = [
        jax.ShapeDtypeStruct((192, 512), bf16), jax.ShapeDtypeStruct((192, 512), bf16),
        jax.ShapeDtypeStruct((2, 64, 256, 256), bf16),
    ]
    for index in range(7):
        master, state, grad = groups[3 * index : 3 * index + 3]
        make = rows if index < 5 else whole
        if index == 2:
            make = lambda shape: rows(shape, -3)
        in_specs += [make(master.shape), make(state.shape), make(grad.shape)]
        shape = (2, *master.shape)
        if index == 5:
            shape = (master.shape[0], 2, master.shape[1])
        out_specs += [make(shape)] * 2
        outs += [jax.ShapeDtypeStruct(shape, f32)] * 2
    return pl.pallas_call(
        finish_kernel,
        grid=(4,),
        out_shape=tuple(outs),
        in_specs=in_specs,
        out_specs=tuple(out_specs),
        scratch_shapes=[pltpu.VMEM((4, 8, 256, 256), bf16), pltpu.SemaphoreType.DMA((4,))],
        compiler_params=pltpu.CompilerParams(vmem_limit_bytes=67043328),
        name="finish",
    )(ds, pw, out, res, *groups)


def fast_local(
    residues, pair_input, out_grad, bucket_layout, time_bins, fold_class,
    attend_weight, attend_state, merge_weight, merge_state, expand_weight, expand_state,
    shrink_weight, shrink_state, modulate_weight, modulate_state, pair_weight, pair_state,
    class_weight, class_state,
):
    m = lax.axis_index("mp")
    classes = class_weight.shape[0]
    am = jnp.concatenate(
        [attend_weight[:, 1], attend_weight[:, 2], attend_weight[:, 0], merge_weight.T], axis=1
    ).astype(bf16)
    es = jnp.concatenate(
        [expand_weight[:, 0], expand_weight[:, 1], shrink_weight.T], axis=1
    ).astype(bf16)
    ms = jnp.concatenate(
        [
            jnp.pad(class_weight.T, ((0, 0), (0, 64 - classes))),
            jnp.pad(pair_weight, ((0, 0), (0, 52))),
            modulate_weight.reshape(32, 1152),
        ],
        axis=1,
    ).astype(bf16)

    def packed(v):
        low = v[:, 128:]
        return jnp.concatenate([v[:, :128], jnp.concatenate([low[:256], low[256:]], axis=1)], axis=0)

    table = jnp.asarray(PATTERNS)
    layout = (bucket_layout[:, None] == jnp.arange(5, dtype=jnp.int32)).astype(jnp.int32)
    unit_slot = jnp.sum(layout[:, :, None] * table[None], axis=1)
    pick_slot = (unit_slot[..., None] == jnp.arange(4, dtype=jnp.int32)).astype(jnp.int32)
    unit_bin = jnp.sum(pick_slot * time_bins[:, None, :], axis=-1).reshape(8)
    unit_class = jnp.sum(pick_slot * fold_class[:, None, :], axis=-1).reshape(8)
    sinus = time_features(unit_bin, 256)
    pick = (unit_class[:, None] == jnp.arange(128, dtype=jnp.int32)).astype(bf16)
    mine = jnp.sum(
        unit_slot * (jnp.arange(4, dtype=jnp.int32)[None] == m).astype(jnp.int32),
        axis=1,
        keepdims=True,
    )
    seen = jnp.where(unit_slot == mine, 0.0, MASKED)
    mask = jnp.broadcast_to(seen[:, :, None], (2, 4, UNIT)).reshape(2, 256)

    out, res, ds, pw, *grads = layer_call(
        classes, ms, am, es, packed(residues), packed(out_grad), pair_input, sinus, pick, mask
    )

    def thirds(v):
        return jnp.swapaxes(v, -3, -2).reshape(*v.shape[:-3], -1, v.shape[-1])

    def turned(v):
        return jnp.swapaxes(v, -2, -1)

    def same(v):
        return v

    views = (thirds, same, same, turned, thirds, turned, turned)
    masters = (
        attend_weight, merge_weight, expand_weight, shrink_weight, modulate_weight, pair_weight,
        class_weight,
    )
    states = (
        attend_state, merge_state, expand_state, shrink_state, modulate_state, pair_state,
        class_state,
    )
    groups = []
    for view, master, state, grad in zip(views, masters, states, grads):
        master = view(master)
        groups += [master, view(state), grad.reshape(master.shape)]
    out, res, pair_grad, *results = finish_call(ds, pw, out, res, *groups)

    def back(index, v):
        if index in (0, 4):
            count = masters[index].shape[1]
            return jnp.swapaxes(v.reshape(2, count, -1, v.shape[-1]), 1, 2)
        if index == 5:
            return jnp.transpose(v, (1, 2, 0))
        return v if index in (1, 2) else turned(v)

    return (out.T, res.T, pair_grad, *(back(i // 2, v) for i, v in enumerate(results)))


def solution(mesh):
    quick = mesh.shape["dp"] == 8 and mesh.shape["mp"] == 4
    placed = (
        P("dp", "mp"),
        P("dp", "mp", None, None),
        P("dp", "mp"),
        P("dp"),
        P("dp", None),
        P("dp", None),
        P("dp", None, "mp"),
        P(None, "dp", None, "mp"),
        P("mp", "dp"),
        P(None, "mp", "dp"),
        P("dp", None, "mp"),
        P(None, "dp", None, "mp"),
        P("mp", "dp"),
        P(None, "mp", "dp"),
        P("dp", None, "mp"),
        P(None, "dp", None, "mp"),
        P("dp", None),
        P(None, "dp", None),
        P(None, "dp"),
        P(None, None, "dp"),
    )
    return jax.shard_map(
        fast_local if quick else local,
        mesh=mesh,
        in_specs=placed,
        out_specs=(
            P("dp", "mp"),
            P("dp", "mp"),
            P("dp", "mp", None, None),
            P(None, "dp", None, "mp"),
            P(None, "dp", None, "mp"),
            P(None, "mp", "dp"),
            P(None, "mp", "dp"),
            P(None, "dp", None, "mp"),
            P(None, "dp", None, "mp"),
            P(None, "mp", "dp"),
            P(None, "mp", "dp"),
            P(None, "dp", None, "mp"),
            P(None, "dp", None, "mp"),
            P(None, "dp", None),
            P(None, "dp", None),
            P(None, None, "dp"),
            P(None, None, "dp"),
        ),
        check_vma=False,
    )
```

```python
import math

import jax
import jax.numpy as jnp
import numpy as np
from jax import lax
from jax.experimental import pallas as pl
from jax.experimental.pallas import tpu as pltpu
from jax.sharding import PartitionSpec as P

D = 768
HD = 64
FF = 3072
PAIR = 256
CDIM = 256
TBINS = 64
STEP = 10


PATTERNS = np.array(
    [[0, 0, 0, 0], [0, 0, 1, 1], [0, 0, 1, 2], [0, 1, 2, 2], [0, 1, 2, 3]], dtype=np.int32
)
NORM_EPS = 1e-06
BETA_ONE = 0.9
BETA_TWO = 0.999
ADAM_EPS = 1e-08
DECAY = 0.01
AVERAGE = 0.999
MASKED = -1e30
HIGH = lax.Precision.HIGHEST


def time_features(bins, width):
    half = width // 2
    moment = (bins.astype(jnp.float32) + 0.5) / TBINS
    freq = jnp.exp(-math.log(10000.0) * jnp.arange(half, dtype=jnp.float32) / half)
    angle = 1000.0 * moment[..., None] * freq
    return jnp.concatenate([jnp.sin(angle), jnp.cos(angle)], axis=-1)


def slot_ids(layout, window):
    unit = np.arange(window) // (window // 4)
    table = jnp.asarray(PATTERNS[:, unit])
    select = (layout[:, None] == jnp.arange(5, dtype=jnp.int32)[None, :]).astype(jnp.int32)
    return jnp.dot(select, table)


def adamw(master, state, grad, rate):
    first = BETA_ONE * state[0] + (1.0 - BETA_ONE) * grad
    second = BETA_TWO * state[1] + (1.0 - BETA_TWO) * grad * grad
    first_hat = first / (1.0 - BETA_ONE**STEP)
    second_hat = second / (1.0 - BETA_TWO**STEP)
    updated = master - rate * (first_hat / (jnp.sqrt(second_hat) + ADAM_EPS) + DECAY * master)
    average = AVERAGE * state[2] + (1.0 - AVERAGE) * updated
    return (jnp.stack([updated, average]), jnp.stack([first, second]))


def normalize(hidden, shift, scale, width):
    totals = lax.psum((jnp.sum(hidden, axis=1), jnp.sum(hidden * hidden, axis=1)), "mp")
    center = totals[0] / width
    spread = lax.rsqrt(totals[1] / width - center * center + NORM_EPS)
    normed = (hidden - center[:, None]) * spread[:, None]
    rows = (normed * (1.0 + scale) + shift).astype(jnp.bfloat16)
    return (normed, spread, lax.all_gather(rows, "mp", axis=1, tiled=True))


def normalize_back(partial_value, normed, spread, scale, width):
    upstream = lax.psum_scatter(partial_value, "mp", scatter_dimension=1, tiled=True)
    inner = upstream * (1.0 + scale)
    totals = lax.psum((jnp.sum(inner, axis=1), jnp.sum(inner * normed, axis=1)), "mp")
    result = spread[:, None] * (
        inner - totals[0][:, None] / width - normed * (totals[1][:, None] / width)
    )
    return (upstream, result)


def branch_total(partial_value):
    return lax.psum_scatter(partial_value, "mp", scatter_dimension=1, tiled=True)


def gather_grad(value):
    return lax.all_gather(value, "mp", axis=1, tiled=True)


def attention_scores(query, keys, bias, same, factor):
    scores = jnp.einsum(
        "wihe,wjhe->whij", query, keys, preferred_element_type=jnp.float32
    ) * factor + bias.astype(jnp.float32)
    return jnp.where(same[:, None], scores, MASKED)


def local(
    residues,
    pair_input,
    out_grad,
    bucket_layout,
    time_bins,
    fold_class,
    attend_weight,
    attend_state,
    merge_weight,
    merge_state,
    expand_weight,
    expand_state,
    shrink_weight,
    shrink_state,
    modulate_weight,
    modulate_state,
    pair_weight,
    pair_state,
    class_weight,
    class_state,
):
    parts = lax.axis_size("mp")
    gathered = (
        lax.all_gather(attend_weight.astype(jnp.bfloat16), "dp", axis=0, tiled=True),
        lax.all_gather(merge_weight.astype(jnp.bfloat16), "dp", axis=1, tiled=True),
        lax.all_gather(expand_weight.astype(jnp.bfloat16), "dp", axis=0, tiled=True),
        lax.all_gather(shrink_weight.astype(jnp.bfloat16), "dp", axis=1, tiled=True),
        lax.all_gather(modulate_weight.astype(jnp.bfloat16), "dp", axis=0, tiled=True),
        lax.all_gather(pair_weight.astype(jnp.bfloat16), "dp", axis=0, tiled=True),
        lax.all_gather(class_weight.astype(jnp.bfloat16), "dp", axis=1, tiled=True),
    )
    attend_full, merge_full, expand_full, shrink_full, modulate_full, pair_full, class_full = (
        gathered
    )
    tokens, local_width = residues.shape
    windows = bucket_layout.shape[0]
    window = tokens // windows
    slots = time_bins.shape[1]
    classes_count = class_full.shape[0]
    heads_local = local_width // HD
    width = local_width * parts
    factor = HD ** (-0.5)
    slot = slot_ids(bucket_layout, window)
    pick = (slot[..., None] == jnp.arange(slots, dtype=jnp.int32)).astype(jnp.float32)
    same = slot[:, :, None] == slot[:, None, :]
    class_pick = (fold_class[..., None] == jnp.arange(classes_count, dtype=jnp.int32)).astype(
        jnp.float32
    )
    before = time_features(time_bins, class_full.shape[1]) + jnp.einsum(
        "wsn,nc->wsc", class_pick, class_full.astype(jnp.float32), precision=HIGH
    )
    condition = jax.nn.silu(before).astype(jnp.bfloat16)
    modulation = jnp.einsum(
        "wsc,cjd->wsjd", condition, modulate_full, preferred_element_type=jnp.float32
    )
    per_token = jnp.einsum("wts,wsjd->wtjd", pick, modulation, precision=HIGH).reshape(
        tokens, 6, local_width
    )
    hidden_in = residues.astype(jnp.float32)
    normed_one, spread_one, rows_one = normalize(hidden_in, per_token[:, 0], per_token[:, 1], width)
    triple = jnp.einsum(
        "td,dje->tje", rows_one, attend_full, preferred_element_type=jnp.float32
    ).astype(jnp.bfloat16)
    query = triple[:, 0].reshape(windows, window, heads_local, HD)
    keys = triple[:, 1].reshape(windows, window, heads_local, HD)
    values = triple[:, 2].reshape(windows, window, heads_local, HD)
    local_bias = jnp.einsum(
        "wijc,ch->whij", pair_input, pair_full, preferred_element_type=jnp.float32
    ).astype(jnp.bfloat16)
    bias = lax.all_to_all(local_bias, "mp", split_axis=1, concat_axis=2, tiled=True)
    scores = attention_scores(query, keys, bias, same, factor)
    peak = jnp.max(scores, axis=-1, keepdims=True)
    logsum = peak + jnp.log(jnp.sum(jnp.exp(scores - peak), axis=-1, keepdims=True))
    chance = jnp.exp(scores - logsum).astype(jnp.bfloat16)
    mixed = (
        jnp.einsum("whij,wjhe->wihe", chance, values, preferred_element_type=jnp.float32)
        .astype(jnp.bfloat16)
        .reshape(tokens, local_width)
    )
    attended = branch_total(jnp.dot(mixed, merge_full, preferred_element_type=jnp.float32))
    middle = hidden_in + per_token[:, 2] * attended
    normed_two, spread_two, rows_two = normalize(middle, per_token[:, 3], per_token[:, 4], width)
    pair_up = jnp.einsum("td,dje->tje", rows_two, expand_full, preferred_element_type=jnp.float32)
    gate = pair_up[:, 0]
    upward = pair_up[:, 1]
    sigma = jax.nn.sigmoid(gate)
    activated = (gate * sigma * upward).astype(jnp.bfloat16)
    fed = branch_total(jnp.dot(activated, shrink_full, preferred_element_type=jnp.float32))
    output = (middle + per_token[:, 5] * fed).astype(jnp.bfloat16)
    upper = out_grad.astype(jnp.float32)
    fed_grad = gather_grad((per_token[:, 5] * upper).astype(jnp.bfloat16))
    act_grad = lax.dot_general(
        fed_grad, shrink_full, (((1,), (1,)), ((), ())), preferred_element_type=jnp.float32
    )
    shrink_grad = lax.dot_general(
        activated, fed_grad, (((0,), (0,)), ((), ())), preferred_element_type=jnp.float32
    )
    slope = sigma * (1.0 + gate * (1.0 - sigma))
    up_grads = jnp.stack([act_grad * upward * slope, act_grad * gate * sigma], axis=1).astype(
        jnp.bfloat16
    )
    expand_grad = jnp.einsum("td,tje->dje", rows_two, up_grads, preferred_element_type=jnp.float32)
    partial_two = jnp.einsum(
        "tje,dje->td", up_grads, expand_full, preferred_element_type=jnp.float32
    )
    upstream_two, norm_two = normalize_back(
        partial_two, normed_two, spread_two, per_token[:, 4], width
    )
    middle_grad = upper + norm_two
    merged_grad = gather_grad((per_token[:, 2] * middle_grad).astype(jnp.bfloat16))
    mixed_grad = (
        lax.dot_general(
            merged_grad, merge_full, (((1,), (1,)), ((), ())), preferred_element_type=jnp.float32
        )
        .astype(jnp.bfloat16)
        .reshape(windows, window, heads_local, HD)
    )
    merge_grad = lax.dot_general(
        mixed, merged_grad, (((0,), (0,)), ((), ())), preferred_element_type=jnp.float32
    )
    again = attention_scores(query, keys, bias, same, factor)
    exact = jnp.exp(again - logsum)
    chance_grad = jnp.einsum(
        "wihe,wjhe->whij", mixed_grad, values, preferred_element_type=jnp.float32
    )
    score_grad = (
        exact * (chance_grad - jnp.sum(exact * chance_grad, axis=-1, keepdims=True))
    ).astype(jnp.bfloat16)
    value_grad = jnp.einsum(
        "whij,wihe->wjhe",
        exact.astype(jnp.bfloat16),
        mixed_grad,
        preferred_element_type=jnp.float32,
    )
    query_grad = (
        jnp.einsum("whij,wjhe->wihe", score_grad, keys, preferred_element_type=jnp.float32) * factor
    )
    keys_grad = (
        jnp.einsum("whij,wihe->wjhe", score_grad, query, preferred_element_type=jnp.float32)
        * factor
    )
    triple_grad = jnp.stack(
        [
            query_grad.reshape(tokens, local_width),
            keys_grad.reshape(tokens, local_width),
            value_grad.reshape(tokens, local_width),
        ],
        axis=1,
    ).astype(jnp.bfloat16)
    bias_grad = lax.all_to_all(score_grad, "mp", split_axis=2, concat_axis=1, tiled=True)
    pair_grad = jnp.einsum(
        "whij,ch->wijc", bias_grad, pair_full, preferred_element_type=jnp.float32
    ).astype(jnp.bfloat16)
    pairwise_grad = jnp.einsum(
        "wijc,whij->ch", pair_input, bias_grad, preferred_element_type=jnp.float32
    )
    attend_grad = jnp.einsum(
        "td,tje->dje", rows_one, triple_grad, preferred_element_type=jnp.float32
    )
    partial_one = jnp.einsum(
        "tje,dje->td", triple_grad, attend_full, preferred_element_type=jnp.float32
    )
    upstream_one, norm_one = normalize_back(
        partial_one, normed_one, spread_one, per_token[:, 1], width
    )
    residue_grad = (middle_grad + norm_one).astype(jnp.bfloat16)
    token_mod_grad = jnp.stack(
        [
            upstream_one,
            upstream_one * normed_one,
            middle_grad * attended,
            upstream_two,
            upstream_two * normed_two,
            upper * fed,
        ],
        axis=1,
    ).reshape(windows, window, 6, local_width)
    mod_grad = jnp.einsum("wts,wtjd->wsjd", pick, token_mod_grad, precision=HIGH)
    modulate_grad = jnp.einsum(
        "wsc,wsjd->cjd", condition.astype(jnp.float32), mod_grad, precision=HIGH
    )
    cond_grad = jnp.einsum(
        "wsjd,cjd->wsc", mod_grad, modulate_full.astype(jnp.float32), precision=HIGH
    )
    sig_before = jax.nn.sigmoid(before)
    before_grad = cond_grad * (sig_before * (1.0 + before * (1.0 - sig_before)))
    class_grad = jnp.einsum("wsn,wsc->nc", class_pick, before_grad, precision=HIGH)
    shared = lax.psum((pairwise_grad, class_grad), "mp")
    sums = (
        lax.psum_scatter(attend_grad, "dp", scatter_dimension=0, tiled=True),
        lax.psum_scatter(merge_grad, "dp", scatter_dimension=1, tiled=True),
        lax.psum_scatter(expand_grad, "dp", scatter_dimension=0, tiled=True),
        lax.psum_scatter(shrink_grad, "dp", scatter_dimension=1, tiled=True),
        lax.psum_scatter(modulate_grad, "dp", scatter_dimension=0, tiled=True),
        lax.psum_scatter(shared[0], "dp", scatter_dimension=0, tiled=True),
        lax.psum_scatter(shared[1], "dp", scatter_dimension=1, tiled=True),
    )
    rates = (
        2.0 / math.sqrt(D),
        2.0 / math.sqrt(D // 8),
        2.0 / math.sqrt(D),
        2.0 / math.sqrt(FF),
        2.0 / math.sqrt(CDIM),
        2.0 / math.sqrt(PAIR),
        2.0,
    )
    masters = (
        attend_weight,
        merge_weight,
        expand_weight,
        shrink_weight,
        modulate_weight,
        pair_weight,
        class_weight,
    )
    states = (
        attend_state,
        merge_state,
        expand_state,
        shrink_state,
        modulate_state,
        pair_state,
        class_state,
    )
    results = []
    for index in range(7):
        updated, tracked = adamw(masters[index], states[index], sums[index], rates[index])
        results.append(updated)
        results.append(tracked)
    return (
        output,
        residue_grad,
        pair_grad,
        results[0],
        results[1],
        results[2],
        results[3],
        results[4],
        results[5],
        results[6],
        results[7],
        results[8],
        results[9],
        results[10],
        results[11],
        results[12],
        results[13],
    )


RATES = (
    2.0 / math.sqrt(D),
    2.0 / math.sqrt(D // 8),
    2.0 / math.sqrt(D),
    2.0 / math.sqrt(FF),
    2.0 / math.sqrt(CDIM),
    2.0 / math.sqrt(PAIR),
    2.0,
)
f32 = jnp.float32
bf16 = jnp.bfloat16
NT = (((1,), (1,)), ((), ()))
NN = (((1,), (0,)), ((), ()))
TN = (((0,), (0,)), ((), ()))
HEADS = 12
GROUP = 16
UNIT = 64
CHUNK = 16
PAIRS = 8


def mm(a, b, dims=NN, precision=None):
    return lax.dot_general(a, b, dims, precision=precision, preferred_element_type=f32)


def head_mask(count):
    row = lax.broadcasted_iota(jnp.int32, (count, GROUP, D), 1)
    col = lax.broadcasted_iota(jnp.int32, (count, GROUP, D), 2) // HD
    return row == col


def spread_heads(rows):
    count = rows.shape[0]
    wide = jnp.broadcast_to(rows.astype(f32)[:, None, :], (count, GROUP, D))
    return jnp.where(head_mask(count), wide, 0.0).astype(bf16).reshape(count * GROUP, D)


def merge_heads(wide):
    count = wide.shape[0] // GROUP
    return jnp.sum(jnp.where(head_mask(count), wide.reshape(count, GROUP, D), 0.0), axis=1)


class Net:
    def __init__(self, send_sems, recv_sems):
        self.d = lax.axis_index("dp")
        self.m = lax.axis_index("mp")
        core = self.d % 2
        x = (self.d // 2) % 2
        y = self.d // 4
        self.core = core
        self.chip = self.d // 2
        self.chips = [self.chip, y * 2 + 1 - x, (1 - y) * 2 + x, (1 - y) * 2 + 1 - x]
        self.partner = self.chip * 2 + 1 - core
        self.send_sems = send_sems
        self.recv_sems = recv_sems
        self.sent = []
        self.open = []
        self.base = 0

    def z(self, t):
        return (self.m + t) % 4

    def peer(self, r):
        return self.chips[r] * 2 + self.core

    def sems(self, count):
        base = self.base
        self.base = base + count
        return base

    def barrier(self):
        sem = pltpu.get_barrier_semaphore()
        targets = [(self.d, self.z(t)) for t in (1, 2, 3)]
        targets += [(self.peer(r), self.m) for r in (1, 2, 3)] + [(self.partner, self.m)]
        for target in targets:
            pl.semaphore_signal(
                sem, inc=1, device_id=target, device_id_type=pl.DeviceIdType.MESH
            )
        pl.semaphore_wait(sem, len(targets))

    def copy(self, src, dst, recv, target, send=None):
        send = len(self.sent) if send is None else send
        return pltpu.make_async_remote_copy(
            src_ref=src,
            dst_ref=dst,
            send_sem=self.send_sems.at[send],
            recv_sem=self.recv_sems.at[recv],
            device_id=target,
            device_id_type=pl.DeviceIdType.MESH,
        )

    def send(self, src, dst, recv, target):
        made = self.copy(src, dst, recv, target)
        made.start()
        self.sent.append(made)
        self.open.append(made)
        return made

    def wait(self, dst, recv):
        self.copy(dst, dst, recv, (self.partner, self.m), 0).wait_recv()

    def drain(self):
        for made in self.open:
            made.wait_send()

    def settle(self, made):
        made.wait_send()
        self.open = [other for other in self.open if other is not made]


class Spread:
    def __init__(self, net, slot):
        self.net, self.slot, self.base = net, slot, net.sems(7)

    def start(self, src=None):
        net = self.net
        own = self.slot(net.d)
        src = own if src is None else src
        made = [net.send(src, own, self.base + r, (net.peer(r), net.m)) for r in (1, 2, 3)]
        return made + [net.send(src, own, self.base, (net.partner, net.m))]

    def forward(self, r):
        net = self.net
        slot = self.slot(net.peer(r))
        net.wait(slot, self.base + r)
        return [net.send(slot, slot, self.base + 3 + r, (net.partner, net.m))]

    def finish(self):
        net = self.net
        net.wait(self.slot(net.partner), self.base)
        for r in (1, 2, 3):
            net.wait(self.slot(net.chips[r] * 2 + 1 - net.core), self.base + 3 + r)


class Zline:
    def __init__(self, net, slot):
        self.net, self.slot, self.base = net, slot, net.sems(4)

    def send(self, t, src):
        net = self.net
        net.send(src, self.slot(net.m), self.base + net.m, (net.d, net.z(t)))

    def wait(self, t):
        net = self.net
        source = net.z(t)
        net.wait(self.slot(source), self.base + source)
        return source


def layer_kernel(
    aw, mw, ew, sw, ow, pwt, cwt, xt, gt, pair, waves, layout, bins, kinds,
    out_o, res_o, ds_o, pw_o, at_o, mg_o, ex_o, sh_o, mod_o, pair_o, class_o,
    msg, amg, esg, xg, gg, modu, modg, modf, bpg, pb, n1, sp1, r1,
    kf, vf, qf, pr, mix, att, mid, n2, sp2, r2, fg, act, upg, fp, fl, p2, p2l, p2o, fpo,
    esp, epl, exl, dkv, dkf, dvf, dqf, mgd, l2, rhs2, p1, p1l,
    amp, axl, aso, azs, azl, mps, mpl, mrg, pws, pwl, pwx, pwy, pco, pcl,
    ops, opl, rps, rpl, ctf, cfull,
    mask, send_sems, recv_sems, pair_sems,
):
    net = Net(send_sems, recv_sems)
    d, m = net.d, net.m

    chunks = 16
    slots = pb.shape[0]

    def pair_copy(step):
        c = step % chunks
        return pltpu.make_async_copy(
            pair.at[c // 8, pl.ds((c % 8) * PAIRS, PAIRS)],
            pb.at[step % slots],
            pair_sems.at[step % slots],
        )

    for step in range(slots):
        pair_copy(step).start()

    dkf[0:256, 0:128] = jnp.zeros((256, 128), f32)
    dkf[0:192, 0:96] = mw[...]
    tall = dkf[0:256, 0:128].T
    amg[m, d] = jnp.concatenate([aw[1], aw[2], aw[0], tall[0:96, 0:192]], axis=-1).astype(bf16)
    cfull[...] = jnp.zeros_like(cfull)
    cfull[0:HEADS, 0:32] = pwt[...]
    cfull[128:160, 0 : cwt.shape[1]] = cwt[...]
    narrow = [cfull[128:160, 0:64], cfull[0:128, :].T[0:32, 0:64]]
    msg[d] = jnp.concatenate(narrow + [ow[j] for j in range(6)], axis=-1).astype(bf16)
    net.barrier()

    row8 = lax.broadcasted_iota(jnp.int32, (8, 128), 0)
    lane8 = lax.broadcasted_iota(jnp.int32, (8, 128), 1)
    bin8 = jnp.zeros((8, 128), jnp.int32)
    kind8 = jnp.zeros((8, 128), jnp.int32)
    mask_row = lax.broadcasted_iota(jnp.int32, (8, 256), 0)
    mask_unit = lax.broadcasted_iota(jnp.int32, (8, 256), 1) // UNIT
    seen = jnp.zeros((8, 256), f32)
    for w in range(2):
        at = layout[w]
        held = []
        for u in range(4):
            slot = jnp.int32(0)
            for k in range(5):
                slot = jnp.where(at == k, jnp.int32(int(PATTERNS[k, u])), slot)
            held.append(slot)
        mine = jnp.int32(0)
        for u in range(4):
            mine = jnp.where(m == u, held[u], mine)
        for u in range(4):
            time, kind = jnp.int32(0), jnp.int32(0)
            for i in range(4):
                time = jnp.where(held[u] == i, bins[w, i], time)
                kind = jnp.where(held[u] == i, kinds[w, i], kind)
            bin8 = jnp.where(row8 == 4 * w + u, time, bin8)
            kind8 = jnp.where(row8 == 4 * w + u, kind, kind8)
            value = jnp.where(held[u] == mine, 0.0, MASKED)
            seen = jnp.where((mask_row == w) & (mask_unit == u), value, seen)
    mask[...] = seen
    pick = jnp.where(lane8 == kind8, 1.0, 0.0).astype(bf16)
    sinus = mm(jnp.where(lane8 == bin8, 1.0, 0.0), waves[...], NN, HIGH)

    cp_all = Spread(net, lambda i: msg.at[i, :, 0:128])
    ms_all = Spread(net, lambda i: msg.at[i, :, 128:1280])
    am_line = Zline(net, lambda s: amg.at[s, d])
    am_all = [Spread(net, lambda i, t=t: amg.at[net.z(t), i]) for t in range(4)]
    x_line = Zline(net, lambda s: xg.at[s])
    g_line = Zline(net, lambda s: gg.at[s])
    mod_line = Zline(net, lambda s: modg.at[s])
    bp_all = Spread(net, lambda i: bpg.at[i])
    es_all = Spread(net, lambda i: esg.at[i])

    cp_all.start()
    for t in (1, 3, 2):
        am_line.send(t, amg.at[m, d])
    ms_all.start()
    am_all[0].start()
    esg[d] = jnp.concatenate([ew[:, 0, :], ew[:, 1, :], sw[...]], axis=-1).astype(bf16)

    def pack_rows(source, ref):
        wide = jnp.concatenate([source[...], jnp.zeros((64, 512), bf16)], axis=0).T
        ref[m, 0:512, :] = wide[:, 0:128]
        low = wide[:, 128:192]
        ref[m, 512:768, :] = jnp.concatenate([low[0:256], low[256:512]], axis=-1)

    pack_rows(xt, xg)
    pack_rows(gt, gg)
    for r in (1, 2, 3):
        cp_all.forward(r)
    cp_all.finish()

    slab = msg[:, :, 0:128].reshape(256, 128)
    select = (
        lax.broadcasted_iota(jnp.int32, (GROUP, 128), 1)
        == lax.broadcasted_iota(jnp.int32, (GROUP, 128), 0) + 64
    ) & (lax.broadcasted_iota(jnp.int32, (GROUP, 128), 0) < HEADS)
    pw_o[...] = mm(jnp.where(select, 1.0, 0.0).astype(bf16), slab, NT).astype(bf16)
    before = sinus + mm(pick, slab, NT)
    condition = (before * jax.nn.sigmoid(before)).astype(bf16)
    bpg[d] = jnp.concatenate([before, pick.astype(f32)], axis=-1)

    def bias_chunk(step):
        slot = step % slots
        pair_copy(step).wait()

        def one(i, carry):
            part = mm(pw_o[...], pb[slot, i], NT)
            at = pl.multiple_of((step % 8) * PAIRS * GROUP + i * GROUP, GROUP)
            ds_o[step // 8, pl.ds(at, GROUP), :] = part.astype(bf16)
            return carry

        lax.fori_loop(0, PAIRS, one, 0, unroll=4)
        pair_copy(step + slots).start()

    bias_chunk(0)
    bias_chunk(1)
    for r in (1, 2, 3):
        ms_all.forward(r)
    bias_chunk(2)
    am_line.wait(1)
    am_all[1].start()
    bias_chunk(3)
    ms_all.finish()
    modu[...] = mm(condition, msg[:, :, 128:1280].reshape(256, 1152))
    modg[m] = modu[...]
    am_line.wait(3)
    am_all[3].start()
    bias_chunk(4)
    for r in (1, 2):
        am_all[0].forward(r)
    bias_chunk(5)
    am_line.wait(2)
    am_all[2].start()
    for t in (1, 2, 3):
        x_line.send(t, xg.at[m])
    for t in (1, 2, 3):
        mod_line.send(t, modu)
    bias_chunk(6)
    am_all[0].forward(3)
    bias_chunk(7)
    for r in (1, 2):
        am_all[1].forward(r)
    for step in (8, 9, 10):
        bias_chunk(step)
    am_all[1].forward(3)
    for r in (1, 2):
        am_all[3].forward(r)
    for step in (11, 12, 13):
        bias_chunk(step)
    am_all[3].forward(3)
    for r in (1, 2):
        am_all[2].forward(r)
    bias_chunk(14)
    bias_chunk(15)

    for t in (1, 2, 3):
        mod_line.wait(t)
    for j in range(6):
        modf[j] = jnp.concatenate([modg[s, :, 192 * j : 192 * j + 192] for s in range(4)], axis=-1)
    for t in (1, 2, 3):
        x_line.wait(t)

    def unpack(ref, w, unit):
        parts = []
        for s in range(4):
            parts.append(ref[s, pl.ds(w * 256 + unit * UNIT, UNIT), :].astype(f32))
            low = ref[s, pl.ds(512 + unit * UNIT, UNIT), :].astype(f32)
            parts.append(low[:, 64 * w : 64 * w + 64])
        return jnp.concatenate(parts, axis=-1)

    def norm(v):
        center = jnp.mean(v, axis=-1, keepdims=True)
        spread = lax.rsqrt(jnp.mean(v * v, axis=-1, keepdims=True) - center * center + NORM_EPS)
        return (v - center) * spread, spread

    for w in range(2):

        def first_norm(unit, carry, w=w):
            v = unpack(xg, w, unit)
            rows = pl.ds(pl.multiple_of(w * 256 + unit * UNIT, UNIT), UNIT)
            normed, spread = norm(v)
            n1[rows, :] = normed
            sp1[rows, :] = jnp.broadcast_to(spread, (UNIT, 128))
            shift = modf[0, pl.ds(w * 4 + unit, 1), :]
            scale = modf[1, pl.ds(w * 4 + unit, 1), :]
            r1[rows, :] = (normed * (1.0 + scale) + shift).astype(bf16)
            return carry

        lax.fori_loop(0, 4, first_norm, 0)

    am_all[2].forward(3)
    es_sent = es_all.start()
    for t in (1, 2, 3):
        g_line.send(t, gg.at[m])
    bp_all.start()
    for t in (0, 1, 3, 2):
        am_all[t].finish()

    def own(w):
        return pl.ds(pl.multiple_of(w * 256 + m * UNIT, UNIT), UNIT)

    def weight(s, lo, hi):
        return amg[s, :, :, lo:hi].reshape(D, hi - lo)

    r1_own = jnp.concatenate([r1[own(0), :], r1[own(1), :]], axis=0)
    qf[...] = jnp.concatenate(
        [mm(r1_own, weight(s, 384, 768))[:, 0:192] for s in range(4)], axis=-1
    ).astype(bf16)
    for w in range(2):
        rows = slice(w * 256, w * 256 + 256)
        both = [mm(r1[rows, :], weight(s, 0, 384)) for s in range(4)]
        kf[rows, :] = jnp.concatenate([v[:, 0:192] for v in both], axis=-1).astype(bf16)
        vf[rows, :] = jnp.concatenate([v[:, 192:384] for v in both], axis=-1).astype(bf16)

    factor = HD ** (-0.5)

    def attend(c, carry):
        w = c // 4
        mine = pl.ds(pl.multiple_of(c * CHUNK, CHUNK), CHUNK)
        keys = pl.ds(pl.multiple_of(w * 256, 256), 256)
        wide = pl.ds(pl.multiple_of((c % 4) * CHUNK * GROUP, CHUNK * GROUP), CHUNK * GROUP)
        scores = mm(spread_heads(qf[mine, :]), kf[keys, :], NT) * factor
        scores = scores + ds_o[w, wide, :].astype(f32) + mask[pl.ds(w, 1), :]
        peak = jnp.max(scores, axis=-1, keepdims=True)
        expo = jnp.exp(scores - peak)
        chance = expo / jnp.sum(expo, axis=-1, keepdims=True)
        pr[w, wide, :] = chance
        mix[mine, :] = merge_heads(mm(chance.astype(bf16), vf[keys, :])).astype(bf16)
        return carry

    def mod_row(j, w):
        return modf[j, pl.ds(w * 4 + m, 1), :]

    blank = jnp.zeros((128, 192), bf16)
    r2_lines = []
    for w in range(2):
        half = slice(w * UNIT, w * UNIT + UNIT)
        lax.fori_loop(4 * w, 4 * w + 4, attend, 0)
        mixed = mix[half, :]
        attended = 0.0
        for s in range(4):
            part = jnp.concatenate([blank[:UNIT], mixed[:, 192 * s : 192 * s + 192]], axis=-1)
            attended = attended + mm(part, weight(s, 384, 768), NT)
        att[half, :] = attended
        middle = unpack(xg, w, m) + mod_row(2, w) * attended
        mid[half, :] = middle
        normed, spread = norm(middle)
        n2[half, :] = normed
        sp2[half, :] = jnp.broadcast_to(spread, (UNIT, 128))
        r2[m, half, :] = (normed * (1.0 + mod_row(4, w)) + mod_row(3, w)).astype(bf16)
        line = Zline(net, lambda s, half=half: r2.at[s, half])
        r2_lines.append(line)
        for t in (1, 3, 2):
            line.send(t, r2.at[m, half])
        for r in ((1, 2), (3,))[w]:
            es_sent += es_all.forward(r)

    for t in (1, 2, 3):
        g_line.wait(t)
    for s in range(4):
        for w in range(2):
            half = slice(w * UNIT, w * UNIT + UNIT)
            upper = unpack(gg, w, s)
            fg[s, half, :] = (modf[5, w * 4 + s : w * 4 + s + 1, :] * upper).astype(bf16)
    es_all.finish()

    p2_line = Zline(net, lambda s: p2l.at[s])
    f_line = Zline(net, lambda s: fl.at[s])

    def feed(s):
        expand = esg[:, :, 0:1536].reshape(D, 1536)
        shrink = esg[:, :, 1536:2304].reshape(D, 768)
        up = mm(r2[s], expand)
        gate = up[:, 0:768]
        upward = up[:, 768:1536]
        act_grad = mm(fg[s], shrink)
        sigma = jax.nn.sigmoid(gate)
        activated = (gate * sigma * upward).astype(bf16)
        act[s] = activated
        slope = sigma * (1.0 + gate * (1.0 - sigma))
        grads = jnp.concatenate(
            [(act_grad * upward * slope).astype(bf16), (act_grad * gate * sigma).astype(bf16)],
            axis=-1,
        )
        upg[s] = grads
        return mm(grads, expand, NT), mm(activated, shrink, NT)

    partial, fed = feed(m)
    p2o[...] = partial
    fpo[...] = fed
    for t in (1, 3, 2):
        for line in r2_lines:
            source = line.wait(t)
        partial, fed = feed(source)
        p2[source] = partial.astype(bf16)
        p2_line.send(t, p2.at[source])
        fp[source] = fed.astype(bf16)

    def put_es(left, right, at):
        for h in range(2):
            value = mm(left[:, :, 384 * h : 384 * h + 384].reshape(512, 384), right, TN)
            for i in range(4):
                part = value[96 * i : 96 * i + 96, :].astype(bf16)
                esp[i % 2, 2 * h + i // 2, :, at : at + 768] = part

    put_es(r2, upg[:, :, 0:768].reshape(512, 768), 0)
    put_es(r2, upg[:, :, 768:1536].reshape(512, 768), 768)
    put_es(fg, act[...].reshape(512, 768), 1536)
    for made in es_sent:
        net.settle(made)
    es_pair = net.sems(1)
    net.send(esp.at[1 - net.core], epl, es_pair, (net.partner, m))

    for t in (1, 3, 2):
        p2_line.wait(t)
    for t in (1, 3, 2):
        f_line.send(t, fp.at[net.z(t)])

    def norm_back(upstream, normed, spread, scale):
        inner = upstream * (1.0 + scale)
        first = jnp.mean(inner, axis=-1, keepdims=True)
        second = jnp.mean(inner * normed, axis=-1, keepdims=True)
        return spread * (inner - first - normed * second)

    def unit_sum(v):
        return jnp.sum(v, axis=0, keepdims=True)

    own_sums = [[None] * 6, [None] * 6]
    for w in range(2):
        half = slice(w * UNIT, w * UNIT + UNIT)
        upstream = p2o[half, :]
        for t in (1, 3, 2):
            upstream = upstream + p2l[net.z(t), half, :].astype(f32)
        normed = n2[half, :]
        back = norm_back(upstream, normed, sp2[half, 0:1], mod_row(4, w))
        grad = unpack(gg, w, m) + back
        p2o[half, :] = grad
        own_sums[w][2] = unit_sum(grad * att[half, :])
        own_sums[w][3] = unit_sum(upstream)
        own_sums[w][4] = unit_sum(upstream * normed)
        l2[slice(128 + w * UNIT, 128 + w * UNIT + UNIT), :] = (mod_row(2, w) * grad).astype(bf16)
        l2[half, :] = r1[own(w), :]
    merged_grad = l2[128:256, :]
    mgd[...] = jnp.concatenate(
        [mm(merged_grad, weight(s, 384, 768))[:, 192:384] for s in range(4)], axis=-1
    ).astype(bf16)

    net.wait(epl, es_pair)
    es_chip = net.sems(4)
    for r in (1, 2, 3):
        total = esp[net.core, net.chips[r]].astype(f32) + epl[net.chips[r]].astype(f32)
        esp[net.core, net.chips[r]] = total.astype(bf16)
        net.send(esp.at[net.core, net.chips[r]], exl.at[r - 1], es_chip + r, (net.peer(r), m))

    dkf[...] = jnp.zeros_like(dkf)
    dvf[...] = jnp.zeros_like(dvf)

    def attend_back(c, carry):
        w = c // 4
        mine = pl.ds(pl.multiple_of(c * CHUNK, CHUNK), CHUNK)
        keys = pl.ds(pl.multiple_of(w * 256, 256), 256)
        wide = pl.ds(pl.multiple_of((c % 4) * CHUNK * GROUP, CHUNK * GROUP), CHUNK * GROUP)
        grad = spread_heads(mgd[mine, :])
        chance = pr[w, wide, :]
        chance_grad = mm(grad, vf[keys, :], NT)
        inner = jnp.sum(chance * chance_grad, axis=-1, keepdims=True)
        score = (chance * (chance_grad - inner)).astype(bf16)
        ds_o[w, wide, :] = score
        dqf[mine, :] = (merge_heads(mm(score, kf[keys, :])) * factor).astype(bf16)
        dvf[keys, :] += mm(chance.astype(bf16), grad, TN)
        dkf[keys, :] += mm(score, spread_heads(qf[mine, :]), TN) * factor
        return carry

    lax.fori_loop(0, 8, attend_back, 0)

    o_line = Zline(net, lambda s: opl.at[s])

    def pack(line, value, ref):
        for s in range(4):
            part = value[:, 192 * s : 192 * s + 192]
            ref[s, 0:128, :] = part[:, 0:128].astype(bf16)
            low = part[:, 128:192]
            ref[s, 128:192, :] = jnp.concatenate([low[0:64], low[64:128]], axis=-1).astype(bf16)
        for t in (1, 3, 2):
            line.send(t, ref.at[net.z(t)])

    def unpack_out(line, ref, mine, to):
        for t in (0, 1, 3, 2):
            s = net.z(t)
            block = mine if t == 0 else ref
            if t:
                line.wait(t)
            for w in range(2):
                rows = pl.ds(pl.multiple_of(w * 256 + s * UNIT, UNIT), UNIT)
                high = block[s, w * UNIT : w * UNIT + UNIT, :].astype(f32)
                low = block[s, 128:192, :].astype(f32)[:, 64 * w : 64 * w + 64]
                to[rows, :] = jnp.concatenate([high, low], axis=-1).astype(bf16)

    for t in (1, 3, 2):
        f_line.wait(t)
    done = []
    for w in range(2):
        half = slice(w * UNIT, w * UNIT + UNIT)
        fed = fpo[half, :]
        for t in (1, 3, 2):
            fed = fed + fl[net.z(t), half, :].astype(f32)
        own_sums[w][5] = unit_sum(unpack(gg, w, m) * fed)
        done.append(mid[half, :] + mod_row(5, w) * fed)
    pack(o_line, jnp.concatenate(done, axis=0), ops)

    for s in range(4):
        cols = slice(192 * s, 192 * s + 192)
        dkv[s] = jnp.concatenate([dkf[:, cols], dvf[:, cols]], axis=-1).astype(bf16)
        rhs2[s, 0:128, :] = jnp.concatenate([dqf[:, cols], blank], axis=-1)
        rhs2[s, 128:256, :] = jnp.concatenate([blank, mix[:, cols]], axis=-1)
    am_pair = net.sems(4)

    def apl(t):
        return esg.at[pl.ds(4 * (t // 3), 4), :, 768 * (t % 3) : 768 * (t % 3) + 768]

    for t in (1, 3, 2, 0):
        s = net.z(t)
        for h in range(2):
            cols = slice(384 * h, 384 * h + 384)
            for left, right, at in ((r1, dkv, 0), (l2, rhs2, 384)):
                value = mm(left[:, cols], right[s], TN)
                for i in range(4):
                    part = value[96 * i : 96 * i + 96, :].astype(bf16)
                    amp[s, i % 2, 2 * h + i // 2, :, at : at + 384] = part
        net.send(amp.at[s, 1 - net.core], apl(t), am_pair + t, (net.partner, m))

    for w in range(2):
        rows = slice(w * 256, w * 256 + 256)
        total = mm(dkv[0, rows, :], weight(0, 0, 384), NT)
        for s in range(1, 4):
            total = total + mm(dkv[s, rows, :], weight(s, 0, 384), NT)
        dkf[rows, :] = total
    total = mm(rhs2[0, 0:128, :], weight(0, 384, 768), NT)
    for s in range(1, 4):
        total = total + mm(rhs2[s, 0:128, :], weight(s, 384, 768), NT)
    for w in range(2):
        dkf[own(w), :] += total[w * UNIT : w * UNIT + UNIT, :]
    p1_line = Zline(net, lambda s: p1l.at[s])
    for t in (1, 3, 2):
        s = net.z(t)
        for w in range(2):
            rows = pl.ds(pl.multiple_of(w * 256 + s * UNIT, UNIT), UNIT)
            p1[s, w * UNIT : w * UNIT + UNIT, :] = dkf[rows, :].astype(bf16)
        p1_line.send(t, p1.at[s])

    sums = [[], []]
    for u in range(8):
        rows = slice(u * UNIT, u * UNIT + UNIT)
        sums[0].append(unit_sum(dkf[rows, :]))
        sums[1].append(unit_sum(dkf[rows, :] * n1[rows, :]))
    row = lax.broadcasted_iota(jnp.int32, (8, D), 0)
    table = [jnp.concatenate(sums[0], axis=0), jnp.concatenate(sums[1], axis=0)]
    for j in range(2, 6):
        first = jnp.broadcast_to(own_sums[0][j], (8, D))
        second = jnp.broadcast_to(own_sums[1][j], (8, D))
        table.append(jnp.where(row == m, first, jnp.where(row == m + 4, second, 0.0)))
    mod_sum = Zline(net, lambda s: mpl.at[s])
    for s in range(4):
        mps[s] = jnp.concatenate([v[:, 192 * s : 192 * s + 192] for v in table], axis=-1)
    for t in (1, 3, 2):
        mod_sum.send(t, mps.at[net.z(t)])

    def pair_chunk(step, acc):
        slot = step % slots
        pair_copy(step).wait()

        def one(i, acc):
            at = pl.multiple_of((step % 8) * PAIRS * GROUP + i * GROUP, GROUP)
            return acc + mm(ds_o[(step - 16) // 8, pl.ds(at, GROUP), :], pb[slot, i])

        acc = lax.fori_loop(0, PAIRS, one, acc, unroll=4)
        if step + slots < 2 * chunks:
            pair_copy(step + slots).start()
        return acc

    pairwise = jnp.zeros((GROUP, 256), f32)
    am_chip = net.sems(16)

    def am_total(t, r):
        base, cols = 4 * (t // 3), slice(768 * (t % 3), 768 * (t % 3) + 768)
        total = amp[net.z(t), net.core, net.chips[r]].astype(f32)
        return total + esg[base + net.chips[r], :, cols].astype(f32)

    step = 16
    for t in (1, 3, 2, 0):
        s = net.z(t)
        net.wait(apl(t), am_pair + t)
        for r in (1, 2, 3):
            part = amp.at[s, net.core, net.chips[r]]
            part[...] = am_total(t, r).astype(bf16)
            net.send(part, axl.at[s, r - 1], am_chip + 4 * t + r, (net.peer(r), m))
        for _ in range(4):
            pairwise = pair_chunk(step, pairwise)
            step += 1

    for r in (1, 2, 3):
        bp_all.forward(r)
    bp_all.finish()

    wide = jnp.concatenate([pairwise, jnp.zeros((112, 256), f32)], axis=0).T
    for i in range(8):
        pws[i % 2, i // 2] = wide[32 * i : 32 * i + 32, :]
    pw_pair = net.sems(1)
    net.send(pws.at[1 - net.core], pwl, pw_pair, (net.partner, m))

    for t in (1, 3, 2):
        mod_sum.wait(t)
    mod_grad = mps[m]
    for t in (1, 3, 2):
        mod_grad = mod_grad + mpl[net.z(t)]
    mrg[d] = mod_grad
    mr_all = Spread(net, lambda i: mrg.at[i])
    mr_all.start()

    am_z = Zline(net, lambda s: azl.at[s])

    def am_arrive(t):
        s = net.z(t)
        total = am_total(t, 0)
        for r in (1, 2, 3):
            net.wait(axl.at[s, r - 1], am_chip + 4 * t + r)
            total = total + axl[s, r - 1].astype(f32)
        if t:
            azs[s] = total.astype(bf16)
            am_z.send(t, azs.at[s])
        else:
            aso[...] = total

    am_arrive(1)

    for t in (1, 3, 2):
        p1_line.wait(t)
    r_line = Zline(net, lambda s: rpl.at[s])
    done = []
    for w in range(2):
        half = slice(w * UNIT, w * UNIT + UNIT)
        upstream = dkf[own(w), :]
        for t in (1, 3, 2):
            upstream = upstream + p1l[net.z(t), half, :].astype(f32)
        back = norm_back(upstream, n1[own(w), :], sp1[own(w), :][:, 0:1], mod_row(1, w))
        done.append(p2o[half, :] + back)
    pack(r_line, jnp.concatenate(done, axis=0), rps)

    am_arrive(3)
    am_arrive(2)

    total = esp[net.core, net.chip].astype(f32) + epl[net.chip].astype(f32)
    for r in (1, 2, 3):
        net.wait(exl.at[r - 1], es_chip + r)
        total = total + exl[r - 1].astype(f32)
    for k in range(2):
        ex_o[:, k, :] = total[:, 768 * k : 768 * k + 768]
    sh_o[...] = total[:, 1536:2304]

    net.wait(pwl, pw_pair)
    pw_chip = net.sems(4)
    for r in (1, 2, 3):
        pwx[r] = pws[net.core, net.chips[r]] + pwl[net.chips[r]]
        net.send(pwx.at[r], pwy.at[r], pw_chip + r, (net.peer(r), m))
    pair_sum = pws[net.core, net.chip] + pwl[net.chip]

    for r in (1, 2, 3):
        mr_all.forward(r)
    am_arrive(0)

    mr_all.finish()
    before = bpg[:, :, 0:256].reshape(64, 256)
    sig = jax.nn.sigmoid(before)
    condition = (before * sig).astype(bf16).astype(f32)
    picks = bpg[:, :, 256:384].reshape(64, 128)
    grads = mrg[...].reshape(64, 1152)
    ctf[...] = condition.T
    mod_sums = mm(ctf[pl.ds(pl.multiple_of(d * 32, 32), 32), :], grads, NN, HIGH)
    for j in range(6):
        mod_o[j] = mod_sums[:, 192 * j : 192 * j + 192]
    cond_grad = mm(grads, msg[:, :, 128:1280].reshape(256, 1152).astype(f32), NT, HIGH)
    before_grad = cond_grad * (sig * (1.0 + before * (1.0 - sig)))
    cfull[...] = mm(before_grad, picks, TN, HIGH)
    for r in (1, 2, 3):
        net.wait(pwy.at[r], pw_chip + r)
        pair_sum = pair_sum + pwy[r]
    pco[...] = jnp.concatenate(
        [pair_sum, cfull[pl.ds(pl.multiple_of(d * 32, 32), 32), :]], axis=-1
    )
    pc_line = Zline(net, lambda s: pcl.at[s])
    for t in (1, 3, 2):
        pc_line.send(t, pco)

    unpack_out(o_line, opl, ops, out_o)
    unpack_out(r_line, rpl, rps, res_o)
    total = aso[...]
    for t in (1, 3, 2):
        total = total + azl[am_z.wait(t)].astype(f32)
    at_o[0] = total[:, 384:576]
    at_o[1] = total[:, 0:192]
    at_o[2] = total[:, 192:384]
    tall = jnp.concatenate([total[:, 512:768], jnp.zeros((32, 256), f32)], axis=0).T
    mg_o[...] = tall[64:256, 0:96]
    total = pco[...]
    for t in (1, 3, 2):
        total = total + pcl[pc_line.wait(t)]
    tall = jnp.concatenate([total[:, 0:128], jnp.zeros((96, 128), f32)], axis=0).T
    pair_o[...] = tall[0:HEADS, 0:32]
    class_o[...] = total[:, 128 : 128 + class_o.shape[1]]
    net.drain()


def layer_call(classes, *args):
    V = pltpu.VMEM
    scratch = [
        V((8, 32, 1280), bf16), V((4, 8, 96, 768), bf16), V((8, 96, 2304), bf16),
        V((4, 768, 128), bf16), V((4, 768, 128), bf16),
        V((8, 1152), f32), V((4, 8, 1152), f32), V((6, 8, 768), f32), V((8, 8, 384), f32),
        V((2, PAIRS, 256, 256), bf16),
        V((512, 768), f32), V((512, 128), f32), V((512, 768), bf16),
        V((512, 768), bf16), V((512, 768), bf16), V((128, 768), bf16), V((2, 1024, 256), f32),
        V((128, 768), bf16), V((128, 768), f32), V((128, 768), f32), V((128, 768), f32),
        V((128, 128), f32),
        V((4, 128, 768), bf16), V((4, 128, 768), bf16), V((4, 128, 768), bf16),
        V((4, 128, 1536), bf16), V((4, 128, 768), bf16), V((4, 128, 768), bf16),
        V((4, 128, 768), bf16), V((4, 128, 768), bf16), V((128, 768), f32), V((128, 768), f32),
        V((2, 4, 96, 2304), bf16), V((4, 96, 2304), bf16), V((3, 96, 2304), bf16),
        V((4, 512, 384), bf16), V((512, 768), f32), V((512, 768), f32), V((128, 768), bf16),
        V((128, 768), bf16), V((256, 768), bf16), V((4, 256, 384), bf16),
        V((4, 128, 768), bf16), V((4, 128, 768), bf16),
        V((4, 2, 4, 96, 768), bf16), V((4, 3, 96, 768), bf16),
        V((96, 768), f32), V((4, 96, 768), bf16), V((4, 96, 768), bf16),
        V((4, 8, 1152), f32), V((4, 8, 1152), f32), V((8, 8, 1152), f32),
        V((2, 4, 32, 128), f32), V((4, 32, 128), f32), V((4, 32, 128), f32), V((4, 32, 128), f32),
        V((32, 256), f32), V((4, 32, 256), f32),
        V((4, 192, 128), bf16), V((4, 192, 128), bf16), V((4, 192, 128), bf16),
        V((4, 192, 128), bf16), V((256, 64), f32), V((256, 128), f32),
        V((8, 256), f32),
        pltpu.SemaphoreType.DMA((160,)), pltpu.SemaphoreType.DMA((160,)),
        pltpu.SemaphoreType.DMA((2,)),
    ]
    whole = pl.BlockSpec(memory_space=pltpu.VMEM)
    outs = (
        ((512, 192), bf16), ((512, 192), bf16), ((2, 1024, 256), bf16), ((16, 256), bf16),
        ((3, 96, 192), f32), ((192, 96), f32), ((96, 2, 768), f32), ((96, 768), f32),
        ((6, 32, 192), f32), ((HEADS, 32), f32), ((32, classes), f32),
    )
    return pl.pallas_call(
        layer_kernel,
        out_shape=tuple(jax.ShapeDtypeStruct(s, t) for s, t in outs),
        in_specs=[whole] * 9
        + [pl.BlockSpec(memory_space=pl.ANY), whole]
        + [pl.BlockSpec(memory_space=pltpu.SMEM)] * 3,
        out_specs=(whole,) * len(outs),
        scratch_shapes=scratch,
        compiler_params=pltpu.CompilerParams(
            collective_id=0, has_side_effects=True, vmem_limit_bytes=67043328
        ),
        name="layer",
    )(*args)


def finish_kernel(*refs):
    ds, pw, out, res = refs[0:4]
    groups = [refs[4 + 3 * i : 7 + 3 * i] for i in range(7)]
    out_t, res_t, pair = refs[25:28]
    results = [refs[28 + 2 * i : 30 + 2 * i] for i in range(7)]
    block, sems = refs[42:44]
    step = pl.program_id(0)

    def put(c, at):
        rows = pl.ds((at % 2) * 32 + 8 * c, 8)
        return pltpu.make_async_copy(block.at[c], pair.at[at // 2, rows], sems.at[c])

    def update(index):
        (master, state, grad), (fresh, kept) = groups[index], results[index]
        old, slope = master[...], grad[...]
        first = BETA_ONE * state[0] + (1.0 - BETA_ONE) * slope
        second = BETA_TWO * state[1] + (1.0 - BETA_TWO) * slope * slope
        first_hat = first / (1.0 - BETA_ONE**STEP)
        second_hat = second / (1.0 - BETA_TWO**STEP)
        new = old - RATES[index] * (first_hat / (jnp.sqrt(second_hat) + ADAM_EPS) + DECAY * old)
        average = AVERAGE * state[2] + (1.0 - AVERAGE) * new
        for ref, values in ((fresh, (new, average)), (kept, (first, second))):
            for i in range(2):
                if index == 5:
                    ref[:, i, :] = values[i]
                else:
                    ref[i] = values[i]

    def turn(source, target):
        wide = jnp.concatenate([source[...].astype(f32), jnp.zeros((128, 64), f32)], axis=-1)
        target[...] = wide.T[0:192, :].astype(bf16)

    for c in range(4):

        @pl.when(step > 0)
        def _(c=c):
            put(c, step - 1).wait()

        for i in range(8):
            at = GROUP * (8 * c + i)
            block[c, i] = mm(ds[0, at : at + GROUP, :], pw[...], TN).astype(bf16)
        if c == 0:
            update(0)
            update(1)
            turn(out, out_t)
        elif c == 1:
            update(2)
        elif c == 2:
            update(3)
            turn(res, res_t)
        else:
            for index in (4, 5, 6):
                update(index)
        put(c, step).start()

    @pl.when(step == 3)
    def _():
        for c in range(4):
            put(c, step).wait()


def finish_call(ds, pw, out, res, *groups):
    def rows(shape, axis=-2):
        at = len(shape) + axis
        block = (*shape[:at], shape[at] // 4, *shape[at + 1 :])
        return pl.BlockSpec(block, lambda i: (0,) * at + (i,) + (0,) * (-1 - axis))

    def whole(shape):
        return pl.BlockSpec(tuple(shape), lambda i: (0,) * len(shape))

    in_specs = [
        pl.BlockSpec((1, 512, 256), lambda i: (i // 2, i % 2, 0)), whole((16, 256)),
        rows((512, 192)), rows((512, 192)),
    ]
    turned = pl.BlockSpec((192, 128), lambda i: (0, i))
    out_specs = [turned, turned, pl.BlockSpec(memory_space=pl.ANY)]
    outs = [
        jax.ShapeDtypeStruct((192, 512), bf16), jax.ShapeDtypeStruct((192, 512), bf16),
        jax.ShapeDtypeStruct((2, 64, 256, 256), bf16),
    ]
    for index in range(7):
        master, state, grad = groups[3 * index : 3 * index + 3]
        make = rows if index < 5 else whole
        if index == 2:
            make = lambda shape: rows(shape, -3)
        in_specs += [make(master.shape), make(state.shape), make(grad.shape)]
        shape = (2, *master.shape)
        if index == 5:
            shape = (master.shape[0], 2, master.shape[1])
        out_specs += [make(shape)] * 2
        outs += [jax.ShapeDtypeStruct(shape, f32)] * 2
    return pl.pallas_call(
        finish_kernel,
        grid=(4,),
        out_shape=tuple(outs),
        in_specs=in_specs,
        out_specs=tuple(out_specs),
        scratch_shapes=[pltpu.VMEM((4, 8, 256, 256), bf16), pltpu.SemaphoreType.DMA((4,))],
        compiler_params=pltpu.CompilerParams(vmem_limit_bytes=67043328),
        name="finish",
    )(ds, pw, out, res, *groups)


def fast_local(
    residues, pair_input, out_grad, bucket_layout, time_bins, fold_class,
    attend_weight, attend_state, merge_weight, merge_state, expand_weight, expand_state,
    shrink_weight, shrink_state, modulate_weight, modulate_state, pair_weight, pair_state,
    class_weight, class_state,
):
    classes = class_weight.shape[0]

    def thirds(v):
        return jnp.swapaxes(v, -3, -2).reshape(*v.shape[:-3], -1, v.shape[-1])

    def turned(v):
        return jnp.swapaxes(v, -2, -1)

    def same(v):
        return v

    views = (thirds, same, same, turned, thirds, turned, turned)
    masters = (
        attend_weight, merge_weight, expand_weight, shrink_weight, modulate_weight, pair_weight,
        class_weight,
    )
    states = (
        attend_state, merge_state, expand_state, shrink_state, modulate_state, pair_state,
        class_state,
    )
    flat = [view(master) for view, master in zip(views, masters)]
    out, res, ds, pw, *grads = layer_call(
        classes, flat[0].reshape(3, 96, 192), *flat[1:4], flat[4].reshape(6, 32, 192), *flat[5:],
        residues.T, out_grad.T, pair_input, time_features(jnp.arange(128), 256), bucket_layout,
        time_bins, fold_class,
    )
    groups = []
    for view, master, state, grad in zip(views, flat, states, grads):
        groups += [master, view(state), grad.reshape(master.shape)]
    out, res, pair_grad, *results = finish_call(ds, pw, out, res, *groups)

    def back(index, v):
        if index in (0, 4):
            count = masters[index].shape[1]
            return jnp.swapaxes(v.reshape(2, count, -1, v.shape[-1]), 1, 2)
        if index == 5:
            return jnp.transpose(v, (1, 2, 0))
        return v if index in (1, 2) else turned(v)

    return (out.T, res.T, pair_grad, *(back(i // 2, v) for i, v in enumerate(results)))


def solution(mesh):
    quick = mesh.shape["dp"] == 8 and mesh.shape["mp"] == 4
    placed = (
        P("dp", "mp"),
        P("dp", "mp", None, None),
        P("dp", "mp"),
        P("dp"),
        P("dp", None),
        P("dp", None),
        P("dp", None, "mp"),
        P(None, "dp", None, "mp"),
        P("mp", "dp"),
        P(None, "mp", "dp"),
        P("dp", None, "mp"),
        P(None, "dp", None, "mp"),
        P("mp", "dp"),
        P(None, "mp", "dp"),
        P("dp", None, "mp"),
        P(None, "dp", None, "mp"),
        P("dp", None),
        P(None, "dp", None),
        P(None, "dp"),
        P(None, None, "dp"),
    )
    return jax.shard_map(
        fast_local if quick else local,
        mesh=mesh,
        in_specs=placed,
        out_specs=(
            P("dp", "mp"),
            P("dp", "mp"),
            P("dp", "mp", None, None),
            P(None, "dp", None, "mp"),
            P(None, "dp", None, "mp"),
            P(None, "mp", "dp"),
            P(None, "mp", "dp"),
            P(None, "dp", None, "mp"),
            P(None, "dp", None, "mp"),
            P(None, "mp", "dp"),
            P(None, "mp", "dp"),
            P(None, "dp", None, "mp"),
            P(None, "dp", None, "mp"),
            P(None, "dp", None),
            P(None, "dp", None),
            P(None, None, "dp"),
            P(None, None, "dp"),
        ),
        check_vma=False,
    )
```

```python
import math

import jax
import jax.numpy as jnp
import numpy as np
from jax import lax
from jax.experimental import pallas as pl
from jax.experimental.pallas import tpu as pltpu
from jax.sharding import PartitionSpec as P

D = 768
HD = 64
FF = 3072
PAIR = 256
CDIM = 256
TBINS = 64
STEP = 10


PATTERNS = np.array(
    [[0, 0, 0, 0], [0, 0, 1, 1], [0, 0, 1, 2], [0, 1, 2, 2], [0, 1, 2, 3]], dtype=np.int32
)
NORM_EPS = 1e-06
BETA_ONE = 0.9
BETA_TWO = 0.999
ADAM_EPS = 1e-08
DECAY = 0.01
AVERAGE = 0.999
MASKED = -1e30
HIGH = lax.Precision.HIGHEST


def time_features(bins, width):
    half = width // 2
    moment = (bins.astype(jnp.float32) + 0.5) / TBINS
    freq = jnp.exp(-math.log(10000.0) * jnp.arange(half, dtype=jnp.float32) / half)
    angle = 1000.0 * moment[..., None] * freq
    return jnp.concatenate([jnp.sin(angle), jnp.cos(angle)], axis=-1)


def slot_ids(layout, window):
    unit = np.arange(window) // (window // 4)
    table = jnp.asarray(PATTERNS[:, unit])
    select = (layout[:, None] == jnp.arange(5, dtype=jnp.int32)[None, :]).astype(jnp.int32)
    return jnp.dot(select, table)


def adamw(master, state, grad, rate):
    first = BETA_ONE * state[0] + (1.0 - BETA_ONE) * grad
    second = BETA_TWO * state[1] + (1.0 - BETA_TWO) * grad * grad
    first_hat = first / (1.0 - BETA_ONE**STEP)
    second_hat = second / (1.0 - BETA_TWO**STEP)
    updated = master - rate * (first_hat / (jnp.sqrt(second_hat) + ADAM_EPS) + DECAY * master)
    average = AVERAGE * state[2] + (1.0 - AVERAGE) * updated
    return (jnp.stack([updated, average]), jnp.stack([first, second]))


def normalize(hidden, shift, scale, width):
    totals = lax.psum((jnp.sum(hidden, axis=1), jnp.sum(hidden * hidden, axis=1)), "mp")
    center = totals[0] / width
    spread = lax.rsqrt(totals[1] / width - center * center + NORM_EPS)
    normed = (hidden - center[:, None]) * spread[:, None]
    rows = (normed * (1.0 + scale) + shift).astype(jnp.bfloat16)
    return (normed, spread, lax.all_gather(rows, "mp", axis=1, tiled=True))


def normalize_back(partial_value, normed, spread, scale, width):
    upstream = lax.psum_scatter(partial_value, "mp", scatter_dimension=1, tiled=True)
    inner = upstream * (1.0 + scale)
    totals = lax.psum((jnp.sum(inner, axis=1), jnp.sum(inner * normed, axis=1)), "mp")
    result = spread[:, None] * (
        inner - totals[0][:, None] / width - normed * (totals[1][:, None] / width)
    )
    return (upstream, result)


def branch_total(partial_value):
    return lax.psum_scatter(partial_value, "mp", scatter_dimension=1, tiled=True)


def gather_grad(value):
    return lax.all_gather(value, "mp", axis=1, tiled=True)


def attention_scores(query, keys, bias, same, factor):
    scores = jnp.einsum(
        "wihe,wjhe->whij", query, keys, preferred_element_type=jnp.float32
    ) * factor + bias.astype(jnp.float32)
    return jnp.where(same[:, None], scores, MASKED)


def local(
    residues,
    pair_input,
    out_grad,
    bucket_layout,
    time_bins,
    fold_class,
    attend_weight,
    attend_state,
    merge_weight,
    merge_state,
    expand_weight,
    expand_state,
    shrink_weight,
    shrink_state,
    modulate_weight,
    modulate_state,
    pair_weight,
    pair_state,
    class_weight,
    class_state,
):
    parts = lax.axis_size("mp")
    gathered = (
        lax.all_gather(attend_weight.astype(jnp.bfloat16), "dp", axis=0, tiled=True),
        lax.all_gather(merge_weight.astype(jnp.bfloat16), "dp", axis=1, tiled=True),
        lax.all_gather(expand_weight.astype(jnp.bfloat16), "dp", axis=0, tiled=True),
        lax.all_gather(shrink_weight.astype(jnp.bfloat16), "dp", axis=1, tiled=True),
        lax.all_gather(modulate_weight.astype(jnp.bfloat16), "dp", axis=0, tiled=True),
        lax.all_gather(pair_weight.astype(jnp.bfloat16), "dp", axis=0, tiled=True),
        lax.all_gather(class_weight.astype(jnp.bfloat16), "dp", axis=1, tiled=True),
    )
    attend_full, merge_full, expand_full, shrink_full, modulate_full, pair_full, class_full = (
        gathered
    )
    tokens, local_width = residues.shape
    windows = bucket_layout.shape[0]
    window = tokens // windows
    slots = time_bins.shape[1]
    classes_count = class_full.shape[0]
    heads_local = local_width // HD
    width = local_width * parts
    factor = HD ** (-0.5)
    slot = slot_ids(bucket_layout, window)
    pick = (slot[..., None] == jnp.arange(slots, dtype=jnp.int32)).astype(jnp.float32)
    same = slot[:, :, None] == slot[:, None, :]
    class_pick = (fold_class[..., None] == jnp.arange(classes_count, dtype=jnp.int32)).astype(
        jnp.float32
    )
    before = time_features(time_bins, class_full.shape[1]) + jnp.einsum(
        "wsn,nc->wsc", class_pick, class_full.astype(jnp.float32), precision=HIGH
    )
    condition = jax.nn.silu(before).astype(jnp.bfloat16)
    modulation = jnp.einsum(
        "wsc,cjd->wsjd", condition, modulate_full, preferred_element_type=jnp.float32
    )
    per_token = jnp.einsum("wts,wsjd->wtjd", pick, modulation, precision=HIGH).reshape(
        tokens, 6, local_width
    )
    hidden_in = residues.astype(jnp.float32)
    normed_one, spread_one, rows_one = normalize(hidden_in, per_token[:, 0], per_token[:, 1], width)
    triple = jnp.einsum(
        "td,dje->tje", rows_one, attend_full, preferred_element_type=jnp.float32
    ).astype(jnp.bfloat16)
    query = triple[:, 0].reshape(windows, window, heads_local, HD)
    keys = triple[:, 1].reshape(windows, window, heads_local, HD)
    values = triple[:, 2].reshape(windows, window, heads_local, HD)
    local_bias = jnp.einsum(
        "wijc,ch->whij", pair_input, pair_full, preferred_element_type=jnp.float32
    ).astype(jnp.bfloat16)
    bias = lax.all_to_all(local_bias, "mp", split_axis=1, concat_axis=2, tiled=True)
    scores = attention_scores(query, keys, bias, same, factor)
    peak = jnp.max(scores, axis=-1, keepdims=True)
    logsum = peak + jnp.log(jnp.sum(jnp.exp(scores - peak), axis=-1, keepdims=True))
    chance = jnp.exp(scores - logsum).astype(jnp.bfloat16)
    mixed = (
        jnp.einsum("whij,wjhe->wihe", chance, values, preferred_element_type=jnp.float32)
        .astype(jnp.bfloat16)
        .reshape(tokens, local_width)
    )
    attended = branch_total(jnp.dot(mixed, merge_full, preferred_element_type=jnp.float32))
    middle = hidden_in + per_token[:, 2] * attended
    normed_two, spread_two, rows_two = normalize(middle, per_token[:, 3], per_token[:, 4], width)
    pair_up = jnp.einsum("td,dje->tje", rows_two, expand_full, preferred_element_type=jnp.float32)
    gate = pair_up[:, 0]
    upward = pair_up[:, 1]
    sigma = jax.nn.sigmoid(gate)
    activated = (gate * sigma * upward).astype(jnp.bfloat16)
    fed = branch_total(jnp.dot(activated, shrink_full, preferred_element_type=jnp.float32))
    output = (middle + per_token[:, 5] * fed).astype(jnp.bfloat16)
    upper = out_grad.astype(jnp.float32)
    fed_grad = gather_grad((per_token[:, 5] * upper).astype(jnp.bfloat16))
    act_grad = lax.dot_general(
        fed_grad, shrink_full, (((1,), (1,)), ((), ())), preferred_element_type=jnp.float32
    )
    shrink_grad = lax.dot_general(
        activated, fed_grad, (((0,), (0,)), ((), ())), preferred_element_type=jnp.float32
    )
    slope = sigma * (1.0 + gate * (1.0 - sigma))
    up_grads = jnp.stack([act_grad * upward * slope, act_grad * gate * sigma], axis=1).astype(
        jnp.bfloat16
    )
    expand_grad = jnp.einsum("td,tje->dje", rows_two, up_grads, preferred_element_type=jnp.float32)
    partial_two = jnp.einsum(
        "tje,dje->td", up_grads, expand_full, preferred_element_type=jnp.float32
    )
    upstream_two, norm_two = normalize_back(
        partial_two, normed_two, spread_two, per_token[:, 4], width
    )
    middle_grad = upper + norm_two
    merged_grad = gather_grad((per_token[:, 2] * middle_grad).astype(jnp.bfloat16))
    mixed_grad = (
        lax.dot_general(
            merged_grad, merge_full, (((1,), (1,)), ((), ())), preferred_element_type=jnp.float32
        )
        .astype(jnp.bfloat16)
        .reshape(windows, window, heads_local, HD)
    )
    merge_grad = lax.dot_general(
        mixed, merged_grad, (((0,), (0,)), ((), ())), preferred_element_type=jnp.float32
    )
    again = attention_scores(query, keys, bias, same, factor)
    exact = jnp.exp(again - logsum)
    chance_grad = jnp.einsum(
        "wihe,wjhe->whij", mixed_grad, values, preferred_element_type=jnp.float32
    )
    score_grad = (
        exact * (chance_grad - jnp.sum(exact * chance_grad, axis=-1, keepdims=True))
    ).astype(jnp.bfloat16)
    value_grad = jnp.einsum(
        "whij,wihe->wjhe",
        exact.astype(jnp.bfloat16),
        mixed_grad,
        preferred_element_type=jnp.float32,
    )
    query_grad = (
        jnp.einsum("whij,wjhe->wihe", score_grad, keys, preferred_element_type=jnp.float32) * factor
    )
    keys_grad = (
        jnp.einsum("whij,wihe->wjhe", score_grad, query, preferred_element_type=jnp.float32)
        * factor
    )
    triple_grad = jnp.stack(
        [
            query_grad.reshape(tokens, local_width),
            keys_grad.reshape(tokens, local_width),
            value_grad.reshape(tokens, local_width),
        ],
        axis=1,
    ).astype(jnp.bfloat16)
    bias_grad = lax.all_to_all(score_grad, "mp", split_axis=2, concat_axis=1, tiled=True)
    pair_grad = jnp.einsum(
        "whij,ch->wijc", bias_grad, pair_full, preferred_element_type=jnp.float32
    ).astype(jnp.bfloat16)
    pairwise_grad = jnp.einsum(
        "wijc,whij->ch", pair_input, bias_grad, preferred_element_type=jnp.float32
    )
    attend_grad = jnp.einsum(
        "td,tje->dje", rows_one, triple_grad, preferred_element_type=jnp.float32
    )
    partial_one = jnp.einsum(
        "tje,dje->td", triple_grad, attend_full, preferred_element_type=jnp.float32
    )
    upstream_one, norm_one = normalize_back(
        partial_one, normed_one, spread_one, per_token[:, 1], width
    )
    residue_grad = (middle_grad + norm_one).astype(jnp.bfloat16)
    token_mod_grad = jnp.stack(
        [
            upstream_one,
            upstream_one * normed_one,
            middle_grad * attended,
            upstream_two,
            upstream_two * normed_two,
            upper * fed,
        ],
        axis=1,
    ).reshape(windows, window, 6, local_width)
    mod_grad = jnp.einsum("wts,wtjd->wsjd", pick, token_mod_grad, precision=HIGH)
    modulate_grad = jnp.einsum(
        "wsc,wsjd->cjd", condition.astype(jnp.float32), mod_grad, precision=HIGH
    )
    cond_grad = jnp.einsum(
        "wsjd,cjd->wsc", mod_grad, modulate_full.astype(jnp.float32), precision=HIGH
    )
    sig_before = jax.nn.sigmoid(before)
    before_grad = cond_grad * (sig_before * (1.0 + before * (1.0 - sig_before)))
    class_grad = jnp.einsum("wsn,wsc->nc", class_pick, before_grad, precision=HIGH)
    shared = lax.psum((pairwise_grad, class_grad), "mp")
    sums = (
        lax.psum_scatter(attend_grad, "dp", scatter_dimension=0, tiled=True),
        lax.psum_scatter(merge_grad, "dp", scatter_dimension=1, tiled=True),
        lax.psum_scatter(expand_grad, "dp", scatter_dimension=0, tiled=True),
        lax.psum_scatter(shrink_grad, "dp", scatter_dimension=1, tiled=True),
        lax.psum_scatter(modulate_grad, "dp", scatter_dimension=0, tiled=True),
        lax.psum_scatter(shared[0], "dp", scatter_dimension=0, tiled=True),
        lax.psum_scatter(shared[1], "dp", scatter_dimension=1, tiled=True),
    )
    rates = (
        2.0 / math.sqrt(D),
        2.0 / math.sqrt(D // 8),
        2.0 / math.sqrt(D),
        2.0 / math.sqrt(FF),
        2.0 / math.sqrt(CDIM),
        2.0 / math.sqrt(PAIR),
        2.0,
    )
    masters = (
        attend_weight,
        merge_weight,
        expand_weight,
        shrink_weight,
        modulate_weight,
        pair_weight,
        class_weight,
    )
    states = (
        attend_state,
        merge_state,
        expand_state,
        shrink_state,
        modulate_state,
        pair_state,
        class_state,
    )
    results = []
    for index in range(7):
        updated, tracked = adamw(masters[index], states[index], sums[index], rates[index])
        results.append(updated)
        results.append(tracked)
    return (
        output,
        residue_grad,
        pair_grad,
        results[0],
        results[1],
        results[2],
        results[3],
        results[4],
        results[5],
        results[6],
        results[7],
        results[8],
        results[9],
        results[10],
        results[11],
        results[12],
        results[13],
    )


RATES = (
    2.0 / math.sqrt(D),
    2.0 / math.sqrt(D // 8),
    2.0 / math.sqrt(D),
    2.0 / math.sqrt(FF),
    2.0 / math.sqrt(CDIM),
    2.0 / math.sqrt(PAIR),
    2.0,
)
f32 = jnp.float32
bf16 = jnp.bfloat16
NT = (((1,), (1,)), ((), ()))
NN = (((1,), (0,)), ((), ()))
TN = (((0,), (0,)), ((), ()))
HEADS = 12
GROUP = 16
UNIT = 64
CHUNK = 16
PAIRS = 8


def mm(a, b, dims=NN, precision=None):
    return lax.dot_general(a, b, dims, precision=precision, preferred_element_type=f32)


def head_mask(count):
    row = lax.broadcasted_iota(jnp.int32, (count, GROUP, D), 1)
    col = lax.broadcasted_iota(jnp.int32, (count, GROUP, D), 2) // HD
    return row == col


def spread_heads(rows):
    count = rows.shape[0]
    wide = jnp.broadcast_to(rows.astype(f32)[:, None, :], (count, GROUP, D))
    return jnp.where(head_mask(count), wide, 0.0).astype(bf16).reshape(count * GROUP, D)


def merge_heads(wide):
    count = wide.shape[0] // GROUP
    return jnp.sum(jnp.where(head_mask(count), wide.reshape(count, GROUP, D), 0.0), axis=1)


class Net:
    def __init__(self, send_sems, recv_sems):
        self.d = lax.axis_index("dp")
        self.m = lax.axis_index("mp")
        core = self.d % 2
        x = (self.d // 2) % 2
        y = self.d // 4
        self.core = core
        self.chip = self.d // 2
        self.chips = [self.chip, y * 2 + 1 - x, (1 - y) * 2 + x, (1 - y) * 2 + 1 - x]
        self.partner = self.chip * 2 + 1 - core
        self.send_sems = send_sems
        self.recv_sems = recv_sems
        self.sent = []
        self.open = []
        self.base = 0

    def z(self, t):
        return (self.m + t) % 4

    def peer(self, r):
        return self.chips[r] * 2 + self.core

    def sems(self, count):
        base = self.base
        self.base = base + count
        return base

    def barrier(self):
        sem = pltpu.get_barrier_semaphore()
        targets = [(self.d, self.z(t)) for t in (1, 2, 3)]
        targets += [(self.peer(r), self.m) for r in (1, 2, 3)] + [(self.partner, self.m)]
        for target in targets:
            pl.semaphore_signal(
                sem, inc=1, device_id=target, device_id_type=pl.DeviceIdType.MESH
            )
        pl.semaphore_wait(sem, len(targets))

    def copy(self, src, dst, recv, target, send=None):
        send = len(self.sent) if send is None else send
        return pltpu.make_async_remote_copy(
            src_ref=src,
            dst_ref=dst,
            send_sem=self.send_sems.at[send],
            recv_sem=self.recv_sems.at[recv],
            device_id=target,
            device_id_type=pl.DeviceIdType.MESH,
        )

    def send(self, src, dst, recv, target):
        made = self.copy(src, dst, recv, target)
        made.start()
        self.sent.append(made)
        self.open.append(made)
        return made

    def wait(self, dst, recv):
        self.copy(dst, dst, recv, (self.partner, self.m), 0).wait_recv()

    def drain(self):
        for made in self.open:
            made.wait_send()

    def settle(self, made):
        made.wait_send()
        self.open = [other for other in self.open if other is not made]


class Spread:
    def __init__(self, net, slot):
        self.net, self.slot, self.base = net, slot, net.sems(7)

    def start(self, src=None):
        net = self.net
        own = self.slot(net.d)
        src = own if src is None else src
        made = [net.send(src, own, self.base + r, (net.peer(r), net.m)) for r in (1, 2, 3)]
        return made + [net.send(src, own, self.base, (net.partner, net.m))]

    def forward(self, r):
        net = self.net
        slot = self.slot(net.peer(r))
        net.wait(slot, self.base + r)
        return [net.send(slot, slot, self.base + 3 + r, (net.partner, net.m))]

    def finish(self):
        net = self.net
        net.wait(self.slot(net.partner), self.base)
        for r in (1, 2, 3):
            net.wait(self.slot(net.chips[r] * 2 + 1 - net.core), self.base + 3 + r)


class Zline:
    def __init__(self, net, slot):
        self.net, self.slot, self.base = net, slot, net.sems(4)

    def send(self, t, src):
        net = self.net
        net.send(src, self.slot(net.m), self.base + net.m, (net.d, net.z(t)))

    def wait(self, t):
        net = self.net
        source = net.z(t)
        net.wait(self.slot(source), self.base + source)
        return source


def layer_kernel(
    aw, mw, ew, sw, ow, pwt, cwt, xt, gt, pair, waves, layout, bins, kinds,
    out_o, res_o, ds_o, pw_o, at_o, mg_o, ex_o, sh_o, mod_o, pair_o, class_o,
    msg, amg, esg, xg, gg, modu, modg, modf, bpg, pb, n1, sp1, r1,
    kf, vf, qf, pr, mix, att, mid, n2, sp2, r2, fg, act, upg, fp, fl, p2, p2l, p2o, fpo,
    esp, epl, exl, dkv, dkf, dvf, dqf, mgd, l2, rhs2, p1, p1l,
    amp, axl, aso, azs, azl, mps, mpl, mrg, pws, pwl, pwx, pwy, pco, pcl,
    ops, opl, rps, rpl, ctf, cfull,
    mask, send_sems, recv_sems, pair_sems,
):
    net = Net(send_sems, recv_sems)
    d, m = net.d, net.m

    chunks = 16
    slots = pb.shape[0]

    def pair_copy(step):
        c = step % chunks
        return pltpu.make_async_copy(
            pair.at[c // 8, pl.ds((c % 8) * PAIRS, PAIRS)],
            pb.at[step % slots],
            pair_sems.at[step % slots],
        )

    for step in range(slots):
        pair_copy(step).start()

    dkf[0:256, 0:128] = jnp.zeros((256, 128), f32)
    dkf[0:192, 0:96] = mw[...]
    tall = dkf[0:256, 0:128].T
    amg[m, d] = jnp.concatenate([aw[1], aw[2], aw[0], tall[0:96, 0:192]], axis=-1).astype(bf16)
    cfull[...] = jnp.zeros_like(cfull)
    cfull[0:HEADS, 0:32] = pwt[...]
    cfull[128:160, 0 : cwt.shape[1]] = cwt[...]
    narrow = [cfull[128:160, 0:64], cfull[0:128, :].T[0:32, 0:64]]
    msg[d] = jnp.concatenate(narrow + [ow[j] for j in range(6)], axis=-1).astype(bf16)
    net.barrier()

    row8 = lax.broadcasted_iota(jnp.int32, (8, 128), 0)
    lane8 = lax.broadcasted_iota(jnp.int32, (8, 128), 1)
    bin8 = jnp.zeros((8, 128), jnp.int32)
    kind8 = jnp.zeros((8, 128), jnp.int32)
    mask_row = lax.broadcasted_iota(jnp.int32, (8, 256), 0)
    mask_unit = lax.broadcasted_iota(jnp.int32, (8, 256), 1) // UNIT
    seen = jnp.zeros((8, 256), f32)
    for w in range(2):
        at = layout[w]
        held = []
        for u in range(4):
            slot = jnp.int32(0)
            for k in range(5):
                slot = jnp.where(at == k, jnp.int32(int(PATTERNS[k, u])), slot)
            held.append(slot)
        mine = jnp.int32(0)
        for u in range(4):
            mine = jnp.where(m == u, held[u], mine)
        for u in range(4):
            time, kind = jnp.int32(0), jnp.int32(0)
            for i in range(4):
                time = jnp.where(held[u] == i, bins[w, i], time)
                kind = jnp.where(held[u] == i, kinds[w, i], kind)
            bin8 = jnp.where(row8 == 4 * w + u, time, bin8)
            kind8 = jnp.where(row8 == 4 * w + u, kind, kind8)
            value = jnp.where(held[u] == mine, 0.0, MASKED)
            seen = jnp.where((mask_row == w) & (mask_unit == u), value, seen)
    mask[...] = seen
    pick = jnp.where(lane8 == kind8, 1.0, 0.0).astype(bf16)
    sinus = mm(jnp.where(lane8 == bin8, 1.0, 0.0), waves[...], NN, HIGH)

    cp_all = Spread(net, lambda i: msg.at[i, :, 0:128])
    ms_all = Spread(net, lambda i: msg.at[i, :, 128:1280])
    am_line = Zline(net, lambda s: amg.at[s, d])
    am_all = [Spread(net, lambda i, t=t: amg.at[net.z(t), i]) for t in range(4)]
    x_line = Zline(net, lambda s: xg.at[s])
    g_line = Zline(net, lambda s: gg.at[s])
    mod_line = Zline(net, lambda s: modg.at[s])
    bp_all = Spread(net, lambda i: bpg.at[i])
    es_all = Spread(net, lambda i: esg.at[i])

    cp_all.start()
    for t in (1, 3, 2):
        am_line.send(t, amg.at[m, d])
    ms_all.start()
    am_all[0].start()
    esg[d] = jnp.concatenate([ew[:, 0, :], ew[:, 1, :], sw[...]], axis=-1).astype(bf16)

    def pack_rows(source, ref):
        wide = jnp.concatenate([source[...], jnp.zeros((64, 512), bf16)], axis=0).T
        ref[m, 0:512, :] = wide[:, 0:128]
        low = wide[:, 128:192]
        ref[m, 512:768, :] = jnp.concatenate([low[0:256], low[256:512]], axis=-1)

    pack_rows(xt, xg)
    pack_rows(gt, gg)
    for r in (1, 2, 3):
        cp_all.forward(r)
    cp_all.finish()

    slab = msg[:, :, 0:128].reshape(256, 128)
    select = (
        lax.broadcasted_iota(jnp.int32, (GROUP, 128), 1)
        == lax.broadcasted_iota(jnp.int32, (GROUP, 128), 0) + 64
    ) & (lax.broadcasted_iota(jnp.int32, (GROUP, 128), 0) < HEADS)
    pw_o[...] = mm(jnp.where(select, 1.0, 0.0).astype(bf16), slab, NT).astype(bf16)
    before = sinus + mm(pick, slab, NT)
    condition = (before * jax.nn.sigmoid(before)).astype(bf16)
    bpg[d] = jnp.concatenate([before, pick.astype(f32)], axis=-1)

    def bias_chunk(step):
        slot = step % slots
        pair_copy(step).wait()

        def one(i, carry):
            part = mm(pw_o[...], pb[slot, i], NT)
            at = pl.multiple_of((step % 8) * PAIRS * GROUP + i * GROUP, GROUP)
            ds_o[step // 8, pl.ds(at, GROUP), :] = part.astype(bf16)
            return carry

        lax.fori_loop(0, PAIRS, one, 0, unroll=4)
        pair_copy(step + slots).start()

    bias_chunk(0)
    bias_chunk(1)
    for r in (1, 2, 3):
        ms_all.forward(r)
    bias_chunk(2)
    am_line.wait(1)
    am_all[1].start()
    bias_chunk(3)
    ms_all.finish()
    modu[...] = mm(condition, msg[:, :, 128:1280].reshape(256, 1152))
    modg[m] = modu[...]
    am_line.wait(3)
    am_all[3].start()
    bias_chunk(4)
    for r in (1, 2):
        am_all[0].forward(r)
    bias_chunk(5)
    am_line.wait(2)
    am_all[2].start()
    for t in (1, 2, 3):
        x_line.send(t, xg.at[m])
    for t in (1, 2, 3):
        mod_line.send(t, modu)
    bias_chunk(6)
    am_all[0].forward(3)
    bias_chunk(7)
    for r in (1, 2):
        am_all[1].forward(r)
    for step in (8, 9, 10):
        bias_chunk(step)
    am_all[1].forward(3)
    for r in (1, 2):
        am_all[3].forward(r)
    for step in (11, 12, 13):
        bias_chunk(step)
    am_all[3].forward(3)
    for r in (1, 2):
        am_all[2].forward(r)
    bias_chunk(14)
    bias_chunk(15)

    for t in (1, 2, 3):
        mod_line.wait(t)
    for j in range(6):
        modf[j] = jnp.concatenate([modg[s, :, 192 * j : 192 * j + 192] for s in range(4)], axis=-1)
    for t in (1, 2, 3):
        x_line.wait(t)

    def unpack(ref, w, unit):
        parts = []
        for s in range(4):
            parts.append(ref[s, pl.ds(w * 256 + unit * UNIT, UNIT), :].astype(f32))
            low = ref[s, pl.ds(512 + unit * UNIT, UNIT), :].astype(f32)
            parts.append(low[:, 64 * w : 64 * w + 64])
        return jnp.concatenate(parts, axis=-1)

    def norm(v):
        center = jnp.mean(v, axis=-1, keepdims=True)
        spread = lax.rsqrt(jnp.mean(v * v, axis=-1, keepdims=True) - center * center + NORM_EPS)
        return (v - center) * spread, spread

    for w in range(2):

        def first_norm(unit, carry, w=w):
            v = unpack(xg, w, unit)
            rows = pl.ds(pl.multiple_of(w * 256 + unit * UNIT, UNIT), UNIT)
            normed, spread = norm(v)
            n1[rows, :] = normed
            sp1[rows, :] = jnp.broadcast_to(spread, (UNIT, 128))
            shift = modf[0, pl.ds(w * 4 + unit, 1), :]
            scale = modf[1, pl.ds(w * 4 + unit, 1), :]
            r1[rows, :] = (normed * (1.0 + scale) + shift).astype(bf16)
            return carry

        lax.fori_loop(0, 4, first_norm, 0)

    am_all[2].forward(3)
    es_sent = es_all.start()
    for t in (1, 2, 3):
        g_line.send(t, gg.at[m])
    bp_all.start()
    for t in (0, 1, 3, 2):
        am_all[t].finish()

    def own(w):
        return pl.ds(pl.multiple_of(w * 256 + m * UNIT, UNIT), UNIT)

    def weight(s, lo, hi):
        return amg[s, :, :, lo:hi].reshape(D, hi - lo)

    r1_own = jnp.concatenate([r1[own(0), :], r1[own(1), :]], axis=0)
    qf[...] = jnp.concatenate(
        [mm(r1_own, weight(s, 384, 768))[:, 0:192] for s in range(4)], axis=-1
    ).astype(bf16)
    for w in range(2):
        rows = slice(w * 256, w * 256 + 256)
        both = [mm(r1[rows, :], weight(s, 0, 384)) for s in range(4)]
        kf[rows, :] = jnp.concatenate([v[:, 0:192] for v in both], axis=-1).astype(bf16)
        vf[rows, :] = jnp.concatenate([v[:, 192:384] for v in both], axis=-1).astype(bf16)

    factor = HD ** (-0.5)

    def attend(c, carry):
        w = c // 4
        mine = pl.ds(pl.multiple_of(c * CHUNK, CHUNK), CHUNK)
        keys = pl.ds(pl.multiple_of(w * 256, 256), 256)
        wide = pl.ds(pl.multiple_of((c % 4) * CHUNK * GROUP, CHUNK * GROUP), CHUNK * GROUP)
        scores = mm(spread_heads(qf[mine, :]), kf[keys, :], NT) * factor
        scores = scores + ds_o[w, wide, :].astype(f32) + mask[pl.ds(w, 1), :]
        peak = jnp.max(scores, axis=-1, keepdims=True)
        expo = jnp.exp(scores - peak)
        chance = expo / jnp.sum(expo, axis=-1, keepdims=True)
        pr[w, wide, :] = chance
        mix[mine, :] = merge_heads(mm(chance.astype(bf16), vf[keys, :])).astype(bf16)
        return carry

    def mod_row(j, w):
        return modf[j, pl.ds(w * 4 + m, 1), :]

    blank = jnp.zeros((128, 192), bf16)
    r2_lines = []
    for w in range(2):
        half = slice(w * UNIT, w * UNIT + UNIT)
        lax.fori_loop(4 * w, 4 * w + 4, attend, 0)
        mixed = mix[half, :]
        attended = 0.0
        for s in range(4):
            part = jnp.concatenate([blank[:UNIT], mixed[:, 192 * s : 192 * s + 192]], axis=-1)
            attended = attended + mm(part, weight(s, 384, 768), NT)
        att[half, :] = attended
        middle = unpack(xg, w, m) + mod_row(2, w) * attended
        mid[half, :] = middle
        normed, spread = norm(middle)
        n2[half, :] = normed
        sp2[half, :] = jnp.broadcast_to(spread, (UNIT, 128))
        r2[m, half, :] = (normed * (1.0 + mod_row(4, w)) + mod_row(3, w)).astype(bf16)
        line = Zline(net, lambda s, half=half: r2.at[s, half])
        r2_lines.append(line)
        for t in (1, 3, 2):
            line.send(t, r2.at[m, half])
        for r in ((1, 2), (3,))[w]:
            es_sent += es_all.forward(r)

    for t in (1, 2, 3):
        g_line.wait(t)
    for s in range(4):
        for w in range(2):
            half = slice(w * UNIT, w * UNIT + UNIT)
            upper = unpack(gg, w, s)
            fg[s, half, :] = (modf[5, w * 4 + s : w * 4 + s + 1, :] * upper).astype(bf16)
    es_all.finish()

    p2_line = Zline(net, lambda s: p2l.at[s])
    f_line = Zline(net, lambda s: fl.at[s])

    def feed(s):
        expand = esg[:, :, 0:1536].reshape(D, 1536)
        shrink = esg[:, :, 1536:2304].reshape(D, 768)
        up = mm(r2[s], expand)
        gate = up[:, 0:768]
        upward = up[:, 768:1536]
        act_grad = mm(fg[s], shrink)
        sigma = jax.nn.sigmoid(gate)
        activated = (gate * sigma * upward).astype(bf16)
        act[s] = activated
        slope = sigma * (1.0 + gate * (1.0 - sigma))
        grads = jnp.concatenate(
            [(act_grad * upward * slope).astype(bf16), (act_grad * gate * sigma).astype(bf16)],
            axis=-1,
        )
        upg[s] = grads
        return mm(grads, expand, NT), mm(activated, shrink, NT)

    partial, fed = feed(m)
    p2o[...] = partial
    fpo[...] = fed
    for t in (1, 3, 2):
        for line in r2_lines:
            source = line.wait(t)
        partial, fed = feed(source)
        p2[source] = partial.astype(bf16)
        p2_line.send(t, p2.at[source])
        fp[source] = fed.astype(bf16)

    def put_es(left, right, at):
        for h in range(2):
            value = mm(left[:, :, 384 * h : 384 * h + 384].reshape(512, 384), right, TN)
            for i in range(4):
                part = value[96 * i : 96 * i + 96, :].astype(bf16)
                esp[i % 2, 2 * h + i // 2, :, at : at + 768] = part

    put_es(r2, upg[:, :, 0:768].reshape(512, 768), 0)
    put_es(r2, upg[:, :, 768:1536].reshape(512, 768), 768)
    put_es(fg, act[...].reshape(512, 768), 1536)
    for made in es_sent:
        net.settle(made)
    es_pair = net.sems(1)
    net.send(esp.at[1 - net.core], epl, es_pair, (net.partner, m))

    for t in (1, 3, 2):
        p2_line.wait(t)
    for t in (1, 3, 2):
        f_line.send(t, fp.at[net.z(t)])

    def norm_back(upstream, normed, spread, scale):
        inner = upstream * (1.0 + scale)
        first = jnp.mean(inner, axis=-1, keepdims=True)
        second = jnp.mean(inner * normed, axis=-1, keepdims=True)
        return spread * (inner - first - normed * second)

    def unit_sum(v):
        return jnp.sum(v, axis=0, keepdims=True)

    own_sums = [[None] * 6, [None] * 6]
    for w in range(2):
        half = slice(w * UNIT, w * UNIT + UNIT)
        upstream = p2o[half, :]
        for t in (1, 3, 2):
            upstream = upstream + p2l[net.z(t), half, :].astype(f32)
        normed = n2[half, :]
        back = norm_back(upstream, normed, sp2[half, 0:1], mod_row(4, w))
        grad = unpack(gg, w, m) + back
        p2o[half, :] = grad
        own_sums[w][2] = unit_sum(grad * att[half, :])
        own_sums[w][3] = unit_sum(upstream)
        own_sums[w][4] = unit_sum(upstream * normed)
        l2[slice(128 + w * UNIT, 128 + w * UNIT + UNIT), :] = (mod_row(2, w) * grad).astype(bf16)
        l2[half, :] = r1[own(w), :]
    merged_grad = l2[128:256, :]
    mgd[...] = jnp.concatenate(
        [mm(merged_grad, weight(s, 384, 768))[:, 192:384] for s in range(4)], axis=-1
    ).astype(bf16)

    net.wait(epl, es_pair)
    es_chip = net.sems(4)
    for r in (1, 2, 3):
        total = esp[net.core, net.chips[r]].astype(f32) + epl[net.chips[r]].astype(f32)
        esp[net.core, net.chips[r]] = total.astype(bf16)
        net.send(esp.at[net.core, net.chips[r]], exl.at[r - 1], es_chip + r, (net.peer(r), m))

    dkf[...] = jnp.zeros_like(dkf)
    dvf[...] = jnp.zeros_like(dvf)

    def attend_back(c, carry):
        w = c // 4
        mine = pl.ds(pl.multiple_of(c * CHUNK, CHUNK), CHUNK)
        keys = pl.ds(pl.multiple_of(w * 256, 256), 256)
        wide = pl.ds(pl.multiple_of((c % 4) * CHUNK * GROUP, CHUNK * GROUP), CHUNK * GROUP)
        grad = spread_heads(mgd[mine, :])
        chance = pr[w, wide, :]
        chance_grad = mm(grad, vf[keys, :], NT)
        inner = jnp.sum(chance * chance_grad, axis=-1, keepdims=True)
        score = (chance * (chance_grad - inner)).astype(bf16)
        ds_o[w, wide, :] = score
        dqf[mine, :] = (merge_heads(mm(score, kf[keys, :])) * factor).astype(bf16)
        dvf[keys, :] += mm(chance.astype(bf16), grad, TN)
        dkf[keys, :] += mm(score, spread_heads(qf[mine, :]), TN) * factor
        return carry

    lax.fori_loop(0, 8, attend_back, 0)

    o_line = Zline(net, lambda s: opl.at[s])

    def pack(line, value, ref):
        for s in range(4):
            part = value[:, 192 * s : 192 * s + 192]
            ref[s, 0:128, :] = part[:, 0:128].astype(bf16)
            low = part[:, 128:192]
            ref[s, 128:192, :] = jnp.concatenate([low[0:64], low[64:128]], axis=-1).astype(bf16)
        for t in (1, 3, 2):
            line.send(t, ref.at[net.z(t)])

    def unpack_out(line, ref, mine, to):
        for t in (0, 1, 3, 2):
            s = net.z(t)
            block = mine if t == 0 else ref
            if t:
                line.wait(t)
            for w in range(2):
                rows = pl.ds(pl.multiple_of(w * 256 + s * UNIT, UNIT), UNIT)
                high = block[s, w * UNIT : w * UNIT + UNIT, :].astype(f32)
                low = block[s, 128:192, :].astype(f32)[:, 64 * w : 64 * w + 64]
                to[rows, :] = jnp.concatenate([high, low], axis=-1).astype(bf16)

    for s in range(4):
        cols = slice(192 * s, 192 * s + 192)
        dkv[s] = jnp.concatenate([dkf[:, cols], dvf[:, cols]], axis=-1).astype(bf16)
        rhs2[s, 0:128, :] = jnp.concatenate([dqf[:, cols], blank], axis=-1)
        rhs2[s, 128:256, :] = jnp.concatenate([blank, mix[:, cols]], axis=-1)
    am_pair = net.sems(4)

    def apl(t):
        return esg.at[pl.ds(4 * (t // 3), 4), :, 768 * (t % 3) : 768 * (t % 3) + 768]

    am_chip = net.sems(16)

    def am_total(t, r):
        base, cols = 4 * (t // 3), slice(768 * (t % 3), 768 * (t % 3) + 768)
        total = amp[net.z(t), net.core, net.chips[r]].astype(f32)
        return total + esg[base + net.chips[r], :, cols].astype(f32)

    def am_grads(t):
        s = net.z(t)
        for h in range(2):
            cols = slice(384 * h, 384 * h + 384)
            for left, right, at in ((r1, dkv, 0), (l2, rhs2, 384)):
                value = mm(left[:, cols], right[s], TN)
                for i in range(4):
                    part = value[96 * i : 96 * i + 96, :].astype(bf16)
                    amp[s, i % 2, 2 * h + i // 2, :, at : at + 384] = part
        net.send(amp.at[s, 1 - net.core], apl(t), am_pair + t, (net.partner, m))

    def am_out(t):
        s = net.z(t)
        net.wait(apl(t), am_pair + t)
        for r in (1, 2, 3):
            part = amp.at[s, net.core, net.chips[r]]
            part[...] = am_total(t, r).astype(bf16)
            net.send(part, axl.at[s, r - 1], am_chip + 4 * t + r, (net.peer(r), m))

    am_grads(1)
    am_grads(3)
    am_out(1)
    am_grads(2)
    am_out(3)
    am_grads(0)
    am_out(2)

    for t in (1, 3, 2):
        f_line.wait(t)
    fed_done = []
    for w in range(2):
        half = slice(w * UNIT, w * UNIT + UNIT)
        fed = fpo[half, :]
        for t in (1, 3, 2):
            fed = fed + fl[net.z(t), half, :].astype(f32)
        own_sums[w][5] = unit_sum(unpack(gg, w, m) * fed)
        fed_done.append(mid[half, :] + mod_row(5, w) * fed)

    for w in range(2):
        rows = slice(w * 256, w * 256 + 256)
        total = mm(dkv[0, rows, :], weight(0, 0, 384), NT)
        for s in range(1, 4):
            total = total + mm(dkv[s, rows, :], weight(s, 0, 384), NT)
        dkf[rows, :] = total
    total = mm(rhs2[0, 0:128, :], weight(0, 384, 768), NT)
    for s in range(1, 4):
        total = total + mm(rhs2[s, 0:128, :], weight(s, 384, 768), NT)
    for w in range(2):
        dkf[own(w), :] += total[w * UNIT : w * UNIT + UNIT, :]

    sums = [[], []]
    for u in range(8):
        rows = slice(u * UNIT, u * UNIT + UNIT)
        sums[0].append(unit_sum(dkf[rows, :]))
        sums[1].append(unit_sum(dkf[rows, :] * n1[rows, :]))
    row = lax.broadcasted_iota(jnp.int32, (8, D), 0)
    table = [jnp.concatenate(sums[0], axis=0), jnp.concatenate(sums[1], axis=0)]
    for j in range(2, 6):
        first = jnp.broadcast_to(own_sums[0][j], (8, D))
        second = jnp.broadcast_to(own_sums[1][j], (8, D))
        table.append(jnp.where(row == m, first, jnp.where(row == m + 4, second, 0.0)))
    mod_sum = Zline(net, lambda s: mpl.at[s])
    for s in range(4):
        mps[s] = jnp.concatenate([v[:, 192 * s : 192 * s + 192] for v in table], axis=-1)
    for t in (1, 3, 2):
        mod_sum.send(t, mps.at[net.z(t)])
    p1_line = Zline(net, lambda s: p1l.at[s])
    for t in (1, 3, 2):
        s = net.z(t)
        for w in range(2):
            rows = pl.ds(pl.multiple_of(w * 256 + s * UNIT, UNIT), UNIT)
            p1[s, w * UNIT : w * UNIT + UNIT, :] = dkf[rows, :].astype(bf16)
        p1_line.send(t, p1.at[s])
    pack(o_line, jnp.concatenate(fed_done, axis=0), ops)

    def pair_chunk(step, acc):
        slot = step % slots
        pair_copy(step).wait()

        def one(i, acc):
            at = pl.multiple_of((step % 8) * PAIRS * GROUP + i * GROUP, GROUP)
            return acc + mm(ds_o[(step - 16) // 8, pl.ds(at, GROUP), :], pb[slot, i])

        acc = lax.fori_loop(0, PAIRS, one, acc, unroll=4)
        if step + slots < 2 * chunks:
            pair_copy(step + slots).start()
        return acc

    pairwise = jnp.zeros((GROUP, 256), f32)
    for step in range(16, 32):
        pairwise = pair_chunk(step, pairwise)

    for r in (1, 2, 3):
        bp_all.forward(r)
    bp_all.finish()

    wide = jnp.concatenate([pairwise, jnp.zeros((112, 256), f32)], axis=0).T
    for i in range(8):
        pws[i % 2, i // 2] = wide[32 * i : 32 * i + 32, :]
    pw_pair = net.sems(1)
    net.send(pws.at[1 - net.core], pwl, pw_pair, (net.partner, m))

    for t in (1, 3, 2):
        mod_sum.wait(t)
    mod_grad = mps[m]
    for t in (1, 3, 2):
        mod_grad = mod_grad + mpl[net.z(t)]
    mrg[d] = mod_grad
    mr_all = Spread(net, lambda i: mrg.at[i])
    mr_all.start()

    am_z = Zline(net, lambda s: azl.at[s])

    def am_arrive(t):
        s = net.z(t)
        total = am_total(t, 0)
        for r in (1, 2, 3):
            net.wait(axl.at[s, r - 1], am_chip + 4 * t + r)
            total = total + axl[s, r - 1].astype(f32)
        if t:
            azs[s] = total.astype(bf16)
            am_z.send(t, azs.at[s])
        else:
            aso[...] = total

    net.wait(pwl, pw_pair)
    pw_chip = net.sems(4)
    for r in (1, 2, 3):
        pwx[r] = pws[net.core, net.chips[r]] + pwl[net.chips[r]]
        net.send(pwx.at[r], pwy.at[r], pw_chip + r, (net.peer(r), m))
    pair_sum = pws[net.core, net.chip] + pwl[net.chip]

    am_out(0)
    am_arrive(1)
    am_arrive(3)

    total = esp[net.core, net.chip].astype(f32) + epl[net.chip].astype(f32)
    for r in (1, 2, 3):
        net.wait(exl.at[r - 1], es_chip + r)
        total = total + exl[r - 1].astype(f32)
    for k in range(2):
        ex_o[:, k, :] = total[:, 768 * k : 768 * k + 768]
    sh_o[...] = total[:, 1536:2304]

    am_arrive(2)

    for t in (1, 3, 2):
        p1_line.wait(t)
    r_line = Zline(net, lambda s: rpl.at[s])
    done = []
    for w in range(2):
        half = slice(w * UNIT, w * UNIT + UNIT)
        upstream = dkf[own(w), :]
        for t in (1, 3, 2):
            upstream = upstream + p1l[net.z(t), half, :].astype(f32)
        back = norm_back(upstream, n1[own(w), :], sp1[own(w), :][:, 0:1], mod_row(1, w))
        done.append(p2o[half, :] + back)
    pack(r_line, jnp.concatenate(done, axis=0), rps)

    for r in (1, 2, 3):
        mr_all.forward(r)
    am_arrive(0)

    mr_all.finish()
    before = bpg[:, :, 0:256].reshape(64, 256)
    sig = jax.nn.sigmoid(before)
    condition = (before * sig).astype(bf16).astype(f32)
    picks = bpg[:, :, 256:384].reshape(64, 128)
    grads = mrg[...].reshape(64, 1152)
    ctf[...] = condition.T
    mod_sums = mm(ctf[pl.ds(pl.multiple_of(d * 32, 32), 32), :], grads, NN, HIGH)
    for j in range(6):
        mod_o[j] = mod_sums[:, 192 * j : 192 * j + 192]
    cond_grad = mm(grads, msg[:, :, 128:1280].reshape(256, 1152).astype(f32), NT, HIGH)
    before_grad = cond_grad * (sig * (1.0 + before * (1.0 - sig)))
    cfull[...] = mm(before_grad, picks, TN, HIGH)
    for r in (1, 2, 3):
        net.wait(pwy.at[r], pw_chip + r)
        pair_sum = pair_sum + pwy[r]
    pco[...] = jnp.concatenate(
        [pair_sum, cfull[pl.ds(pl.multiple_of(d * 32, 32), 32), :]], axis=-1
    )
    pc_line = Zline(net, lambda s: pcl.at[s])
    for t in (1, 3, 2):
        pc_line.send(t, pco)

    unpack_out(o_line, opl, ops, out_o)
    unpack_out(r_line, rpl, rps, res_o)
    total = aso[...]
    for t in (1, 3, 2):
        total = total + azl[am_z.wait(t)].astype(f32)
    at_o[0] = total[:, 384:576]
    at_o[1] = total[:, 0:192]
    at_o[2] = total[:, 192:384]
    tall = jnp.concatenate([total[:, 512:768], jnp.zeros((32, 256), f32)], axis=0).T
    mg_o[...] = tall[64:256, 0:96]
    total = pco[...]
    for t in (1, 3, 2):
        total = total + pcl[pc_line.wait(t)]
    tall = jnp.concatenate([total[:, 0:128], jnp.zeros((96, 128), f32)], axis=0).T
    pair_o[...] = tall[0:HEADS, 0:32]
    class_o[...] = total[:, 128 : 128 + class_o.shape[1]]
    net.drain()


def layer_call(classes, *args):
    V = pltpu.VMEM
    scratch = [
        V((8, 32, 1280), bf16), V((4, 8, 96, 768), bf16), V((8, 96, 2304), bf16),
        V((4, 768, 128), bf16), V((4, 768, 128), bf16),
        V((8, 1152), f32), V((4, 8, 1152), f32), V((6, 8, 768), f32), V((8, 8, 384), f32),
        V((2, PAIRS, 256, 256), bf16),
        V((512, 768), f32), V((512, 128), f32), V((512, 768), bf16),
        V((512, 768), bf16), V((512, 768), bf16), V((128, 768), bf16), V((2, 1024, 256), f32),
        V((128, 768), bf16), V((128, 768), f32), V((128, 768), f32), V((128, 768), f32),
        V((128, 128), f32),
        V((4, 128, 768), bf16), V((4, 128, 768), bf16), V((4, 128, 768), bf16),
        V((4, 128, 1536), bf16), V((4, 128, 768), bf16), V((4, 128, 768), bf16),
        V((4, 128, 768), bf16), V((4, 128, 768), bf16), V((128, 768), f32), V((128, 768), f32),
        V((2, 4, 96, 2304), bf16), V((4, 96, 2304), bf16), V((3, 96, 2304), bf16),
        V((4, 512, 384), bf16), V((512, 768), f32), V((512, 768), f32), V((128, 768), bf16),
        V((128, 768), bf16), V((256, 768), bf16), V((4, 256, 384), bf16),
        V((4, 128, 768), bf16), V((4, 128, 768), bf16),
        V((4, 2, 4, 96, 768), bf16), V((4, 3, 96, 768), bf16),
        V((96, 768), f32), V((4, 96, 768), bf16), V((4, 96, 768), bf16),
        V((4, 8, 1152), f32), V((4, 8, 1152), f32), V((8, 8, 1152), f32),
        V((2, 4, 32, 128), f32), V((4, 32, 128), f32), V((4, 32, 128), f32), V((4, 32, 128), f32),
        V((32, 256), f32), V((4, 32, 256), f32),
        V((4, 192, 128), bf16), V((4, 192, 128), bf16), V((4, 192, 128), bf16),
        V((4, 192, 128), bf16), V((256, 64), f32), V((256, 128), f32),
        V((8, 256), f32),
        pltpu.SemaphoreType.DMA((160,)), pltpu.SemaphoreType.DMA((160,)),
        pltpu.SemaphoreType.DMA((2,)),
    ]
    whole = pl.BlockSpec(memory_space=pltpu.VMEM)
    outs = (
        ((512, 192), bf16), ((512, 192), bf16), ((2, 1024, 256), bf16), ((16, 256), bf16),
        ((3, 96, 192), f32), ((192, 96), f32), ((96, 2, 768), f32), ((96, 768), f32),
        ((6, 32, 192), f32), ((HEADS, 32), f32), ((32, classes), f32),
    )
    return pl.pallas_call(
        layer_kernel,
        out_shape=tuple(jax.ShapeDtypeStruct(s, t) for s, t in outs),
        in_specs=[whole] * 9
        + [pl.BlockSpec(memory_space=pl.ANY), whole]
        + [pl.BlockSpec(memory_space=pltpu.SMEM)] * 3,
        out_specs=(whole,) * len(outs),
        scratch_shapes=scratch,
        compiler_params=pltpu.CompilerParams(
            collective_id=0, has_side_effects=True, vmem_limit_bytes=67043328
        ),
        name="layer",
    )(*args)


def finish_kernel(*refs):
    ds, pw, out, res = refs[0:4]
    groups = [refs[4 + 3 * i : 7 + 3 * i] for i in range(7)]
    out_t, res_t, pair = refs[25:28]
    results = [refs[28 + 2 * i : 30 + 2 * i] for i in range(7)]
    block, sems = refs[42:44]
    step = pl.program_id(0)

    def put(c, at):
        rows = pl.ds((at % 2) * 32 + 8 * c, 8)
        return pltpu.make_async_copy(block.at[c], pair.at[at // 2, rows], sems.at[c])

    def update(index):
        (master, state, grad), (fresh, kept) = groups[index], results[index]
        old, slope = master[...], grad[...]
        first = BETA_ONE * state[0] + (1.0 - BETA_ONE) * slope
        second = BETA_TWO * state[1] + (1.0 - BETA_TWO) * slope * slope
        first_hat = first / (1.0 - BETA_ONE**STEP)
        second_hat = second / (1.0 - BETA_TWO**STEP)
        new = old - RATES[index] * (first_hat / (jnp.sqrt(second_hat) + ADAM_EPS) + DECAY * old)
        average = AVERAGE * state[2] + (1.0 - AVERAGE) * new
        for ref, values in ((fresh, (new, average)), (kept, (first, second))):
            for i in range(2):
                if index == 5:
                    ref[:, i, :] = values[i]
                else:
                    ref[i] = values[i]

    def turn(source, target):
        wide = jnp.concatenate([source[...].astype(f32), jnp.zeros((128, 64), f32)], axis=-1)
        target[...] = wide.T[0:192, :].astype(bf16)

    for c in range(4):

        @pl.when(step > 0)
        def _(c=c):
            put(c, step - 1).wait()

        for i in range(8):
            at = GROUP * (8 * c + i)
            block[c, i] = mm(ds[0, at : at + GROUP, :], pw[...], TN).astype(bf16)
        if c == 0:
            update(0)
            update(1)
            turn(out, out_t)
        elif c == 1:
            update(2)
        elif c == 2:
            update(3)
            turn(res, res_t)
        else:
            for index in (4, 5, 6):
                update(index)
        put(c, step).start()

    @pl.when(step == 3)
    def _():
        for c in range(4):
            put(c, step).wait()


def finish_call(ds, pw, out, res, *groups):
    def rows(shape, axis=-2):
        at = len(shape) + axis
        block = (*shape[:at], shape[at] // 4, *shape[at + 1 :])
        return pl.BlockSpec(block, lambda i: (0,) * at + (i,) + (0,) * (-1 - axis))

    def whole(shape):
        return pl.BlockSpec(tuple(shape), lambda i: (0,) * len(shape))

    in_specs = [
        pl.BlockSpec((1, 512, 256), lambda i: (i // 2, i % 2, 0)), whole((16, 256)),
        rows((512, 192)), rows((512, 192)),
    ]
    turned = pl.BlockSpec((192, 128), lambda i: (0, i))
    out_specs = [turned, turned, pl.BlockSpec(memory_space=pl.ANY)]
    outs = [
        jax.ShapeDtypeStruct((192, 512), bf16), jax.ShapeDtypeStruct((192, 512), bf16),
        jax.ShapeDtypeStruct((2, 64, 256, 256), bf16),
    ]
    for index in range(7):
        master, state, grad = groups[3 * index : 3 * index + 3]
        make = rows if index < 5 else whole
        if index == 2:
            make = lambda shape: rows(shape, -3)
        in_specs += [make(master.shape), make(state.shape), make(grad.shape)]
        shape = (2, *master.shape)
        if index == 5:
            shape = (master.shape[0], 2, master.shape[1])
        out_specs += [make(shape)] * 2
        outs += [jax.ShapeDtypeStruct(shape, f32)] * 2
    return pl.pallas_call(
        finish_kernel,
        grid=(4,),
        out_shape=tuple(outs),
        in_specs=in_specs,
        out_specs=tuple(out_specs),
        scratch_shapes=[pltpu.VMEM((4, 8, 256, 256), bf16), pltpu.SemaphoreType.DMA((4,))],
        compiler_params=pltpu.CompilerParams(vmem_limit_bytes=67043328),
        name="finish",
    )(ds, pw, out, res, *groups)


def fast_local(
    residues, pair_input, out_grad, bucket_layout, time_bins, fold_class,
    attend_weight, attend_state, merge_weight, merge_state, expand_weight, expand_state,
    shrink_weight, shrink_state, modulate_weight, modulate_state, pair_weight, pair_state,
    class_weight, class_state,
):
    classes = class_weight.shape[0]

    def thirds(v):
        return jnp.swapaxes(v, -3, -2).reshape(*v.shape[:-3], -1, v.shape[-1])

    def turned(v):
        return jnp.swapaxes(v, -2, -1)

    def same(v):
        return v

    views = (thirds, same, same, turned, thirds, turned, turned)
    masters = (
        attend_weight, merge_weight, expand_weight, shrink_weight, modulate_weight, pair_weight,
        class_weight,
    )
    states = (
        attend_state, merge_state, expand_state, shrink_state, modulate_state, pair_state,
        class_state,
    )
    flat = [view(master) for view, master in zip(views, masters)]
    out, res, ds, pw, *grads = layer_call(
        classes, flat[0].reshape(3, 96, 192), *flat[1:4], flat[4].reshape(6, 32, 192), *flat[5:],
        residues.T, out_grad.T, pair_input, time_features(jnp.arange(128), 256), bucket_layout,
        time_bins, fold_class,
    )
    groups = []
    for view, master, state, grad in zip(views, flat, states, grads):
        groups += [master, view(state), grad.reshape(master.shape)]
    out, res, pair_grad, *results = finish_call(ds, pw, out, res, *groups)

    def back(index, v):
        if index in (0, 4):
            count = masters[index].shape[1]
            return jnp.swapaxes(v.reshape(2, count, -1, v.shape[-1]), 1, 2)
        if index == 5:
            return jnp.transpose(v, (1, 2, 0))
        return v if index in (1, 2) else turned(v)

    return (out.T, res.T, pair_grad, *(back(i // 2, v) for i, v in enumerate(results)))


def solution(mesh):
    quick = mesh.shape["dp"] == 8 and mesh.shape["mp"] == 4
    placed = (
        P("dp", "mp"),
        P("dp", "mp", None, None),
        P("dp", "mp"),
        P("dp"),
        P("dp", None),
        P("dp", None),
        P("dp", None, "mp"),
        P(None, "dp", None, "mp"),
        P("mp", "dp"),
        P(None, "mp", "dp"),
        P("dp", None, "mp"),
        P(None, "dp", None, "mp"),
        P("mp", "dp"),
        P(None, "mp", "dp"),
        P("dp", None, "mp"),
        P(None, "dp", None, "mp"),
        P("dp", None),
        P(None, "dp", None),
        P(None, "dp"),
        P(None, None, "dp"),
    )
    return jax.shard_map(
        fast_local if quick else local,
        mesh=mesh,
        in_specs=placed,
        out_specs=(
            P("dp", "mp"),
            P("dp", "mp"),
            P("dp", "mp", None, None),
            P(None, "dp", None, "mp"),
            P(None, "dp", None, "mp"),
            P(None, "mp", "dp"),
            P(None, "mp", "dp"),
            P(None, "dp", None, "mp"),
            P(None, "dp", None, "mp"),
            P(None, "mp", "dp"),
            P(None, "mp", "dp"),
            P(None, "dp", None, "mp"),
            P(None, "dp", None, "mp"),
            P(None, "dp", None),
            P(None, "dp", None),
            P(None, None, "dp"),
            P(None, None, "dp"),
        ),
        check_vma=False,
    )
```

```python
import math

import jax
import jax.numpy as jnp
import numpy as np
from jax import lax
from jax.experimental import pallas as pl
from jax.experimental.pallas import tpu as pltpu
from jax.sharding import PartitionSpec as P

D = 768
HD = 64
FF = 3072
PAIR = 256
CDIM = 256
TBINS = 64
STEP = 10


PATTERNS = np.array(
    [[0, 0, 0, 0], [0, 0, 1, 1], [0, 0, 1, 2], [0, 1, 2, 2], [0, 1, 2, 3]], dtype=np.int32
)
NORM_EPS = 1e-06
BETA_ONE = 0.9
BETA_TWO = 0.999
ADAM_EPS = 1e-08
DECAY = 0.01
AVERAGE = 0.999
MASKED = -1e30
HIGH = lax.Precision.HIGHEST


def time_features(bins, width):
    half = width // 2
    moment = (bins.astype(jnp.float32) + 0.5) / TBINS
    freq = jnp.exp(-math.log(10000.0) * jnp.arange(half, dtype=jnp.float32) / half)
    angle = 1000.0 * moment[..., None] * freq
    return jnp.concatenate([jnp.sin(angle), jnp.cos(angle)], axis=-1)


def slot_ids(layout, window):
    unit = np.arange(window) // (window // 4)
    table = jnp.asarray(PATTERNS[:, unit])
    select = (layout[:, None] == jnp.arange(5, dtype=jnp.int32)[None, :]).astype(jnp.int32)
    return jnp.dot(select, table)


def adamw(master, state, grad, rate):
    first = BETA_ONE * state[0] + (1.0 - BETA_ONE) * grad
    second = BETA_TWO * state[1] + (1.0 - BETA_TWO) * grad * grad
    first_hat = first / (1.0 - BETA_ONE**STEP)
    second_hat = second / (1.0 - BETA_TWO**STEP)
    updated = master - rate * (first_hat / (jnp.sqrt(second_hat) + ADAM_EPS) + DECAY * master)
    average = AVERAGE * state[2] + (1.0 - AVERAGE) * updated
    return (jnp.stack([updated, average]), jnp.stack([first, second]))


def normalize(hidden, shift, scale, width):
    totals = lax.psum((jnp.sum(hidden, axis=1), jnp.sum(hidden * hidden, axis=1)), "mp")
    center = totals[0] / width
    spread = lax.rsqrt(totals[1] / width - center * center + NORM_EPS)
    normed = (hidden - center[:, None]) * spread[:, None]
    rows = (normed * (1.0 + scale) + shift).astype(jnp.bfloat16)
    return (normed, spread, lax.all_gather(rows, "mp", axis=1, tiled=True))


def normalize_back(partial_value, normed, spread, scale, width):
    upstream = lax.psum_scatter(partial_value, "mp", scatter_dimension=1, tiled=True)
    inner = upstream * (1.0 + scale)
    totals = lax.psum((jnp.sum(inner, axis=1), jnp.sum(inner * normed, axis=1)), "mp")
    result = spread[:, None] * (
        inner - totals[0][:, None] / width - normed * (totals[1][:, None] / width)
    )
    return (upstream, result)


def branch_total(partial_value):
    return lax.psum_scatter(partial_value, "mp", scatter_dimension=1, tiled=True)


def gather_grad(value):
    return lax.all_gather(value, "mp", axis=1, tiled=True)


def attention_scores(query, keys, bias, same, factor):
    scores = jnp.einsum(
        "wihe,wjhe->whij", query, keys, preferred_element_type=jnp.float32
    ) * factor + bias.astype(jnp.float32)
    return jnp.where(same[:, None], scores, MASKED)


def local(
    residues,
    pair_input,
    out_grad,
    bucket_layout,
    time_bins,
    fold_class,
    attend_weight,
    attend_state,
    merge_weight,
    merge_state,
    expand_weight,
    expand_state,
    shrink_weight,
    shrink_state,
    modulate_weight,
    modulate_state,
    pair_weight,
    pair_state,
    class_weight,
    class_state,
):
    parts = lax.axis_size("mp")
    gathered = (
        lax.all_gather(attend_weight.astype(jnp.bfloat16), "dp", axis=0, tiled=True),
        lax.all_gather(merge_weight.astype(jnp.bfloat16), "dp", axis=1, tiled=True),
        lax.all_gather(expand_weight.astype(jnp.bfloat16), "dp", axis=0, tiled=True),
        lax.all_gather(shrink_weight.astype(jnp.bfloat16), "dp", axis=1, tiled=True),
        lax.all_gather(modulate_weight.astype(jnp.bfloat16), "dp", axis=0, tiled=True),
        lax.all_gather(pair_weight.astype(jnp.bfloat16), "dp", axis=0, tiled=True),
        lax.all_gather(class_weight.astype(jnp.bfloat16), "dp", axis=1, tiled=True),
    )
    attend_full, merge_full, expand_full, shrink_full, modulate_full, pair_full, class_full = (
        gathered
    )
    tokens, local_width = residues.shape
    windows = bucket_layout.shape[0]
    window = tokens // windows
    slots = time_bins.shape[1]
    classes_count = class_full.shape[0]
    heads_local = local_width // HD
    width = local_width * parts
    factor = HD ** (-0.5)
    slot = slot_ids(bucket_layout, window)
    pick = (slot[..., None] == jnp.arange(slots, dtype=jnp.int32)).astype(jnp.float32)
    same = slot[:, :, None] == slot[:, None, :]
    class_pick = (fold_class[..., None] == jnp.arange(classes_count, dtype=jnp.int32)).astype(
        jnp.float32
    )
    before = time_features(time_bins, class_full.shape[1]) + jnp.einsum(
        "wsn,nc->wsc", class_pick, class_full.astype(jnp.float32), precision=HIGH
    )
    condition = jax.nn.silu(before).astype(jnp.bfloat16)
    modulation = jnp.einsum(
        "wsc,cjd->wsjd", condition, modulate_full, preferred_element_type=jnp.float32
    )
    per_token = jnp.einsum("wts,wsjd->wtjd", pick, modulation, precision=HIGH).reshape(
        tokens, 6, local_width
    )
    hidden_in = residues.astype(jnp.float32)
    normed_one, spread_one, rows_one = normalize(hidden_in, per_token[:, 0], per_token[:, 1], width)
    triple = jnp.einsum(
        "td,dje->tje", rows_one, attend_full, preferred_element_type=jnp.float32
    ).astype(jnp.bfloat16)
    query = triple[:, 0].reshape(windows, window, heads_local, HD)
    keys = triple[:, 1].reshape(windows, window, heads_local, HD)
    values = triple[:, 2].reshape(windows, window, heads_local, HD)
    local_bias = jnp.einsum(
        "wijc,ch->whij", pair_input, pair_full, preferred_element_type=jnp.float32
    ).astype(jnp.bfloat16)
    bias = lax.all_to_all(local_bias, "mp", split_axis=1, concat_axis=2, tiled=True)
    scores = attention_scores(query, keys, bias, same, factor)
    peak = jnp.max(scores, axis=-1, keepdims=True)
    logsum = peak + jnp.log(jnp.sum(jnp.exp(scores - peak), axis=-1, keepdims=True))
    chance = jnp.exp(scores - logsum).astype(jnp.bfloat16)
    mixed = (
        jnp.einsum("whij,wjhe->wihe", chance, values, preferred_element_type=jnp.float32)
        .astype(jnp.bfloat16)
        .reshape(tokens, local_width)
    )
    attended = branch_total(jnp.dot(mixed, merge_full, preferred_element_type=jnp.float32))
    middle = hidden_in + per_token[:, 2] * attended
    normed_two, spread_two, rows_two = normalize(middle, per_token[:, 3], per_token[:, 4], width)
    pair_up = jnp.einsum("td,dje->tje", rows_two, expand_full, preferred_element_type=jnp.float32)
    gate = pair_up[:, 0]
    upward = pair_up[:, 1]
    sigma = jax.nn.sigmoid(gate)
    activated = (gate * sigma * upward).astype(jnp.bfloat16)
    fed = branch_total(jnp.dot(activated, shrink_full, preferred_element_type=jnp.float32))
    output = (middle + per_token[:, 5] * fed).astype(jnp.bfloat16)
    upper = out_grad.astype(jnp.float32)
    fed_grad = gather_grad((per_token[:, 5] * upper).astype(jnp.bfloat16))
    act_grad = lax.dot_general(
        fed_grad, shrink_full, (((1,), (1,)), ((), ())), preferred_element_type=jnp.float32
    )
    shrink_grad = lax.dot_general(
        activated, fed_grad, (((0,), (0,)), ((), ())), preferred_element_type=jnp.float32
    )
    slope = sigma * (1.0 + gate * (1.0 - sigma))
    up_grads = jnp.stack([act_grad * upward * slope, act_grad * gate * sigma], axis=1).astype(
        jnp.bfloat16
    )
    expand_grad = jnp.einsum("td,tje->dje", rows_two, up_grads, preferred_element_type=jnp.float32)
    partial_two = jnp.einsum(
        "tje,dje->td", up_grads, expand_full, preferred_element_type=jnp.float32
    )
    upstream_two, norm_two = normalize_back(
        partial_two, normed_two, spread_two, per_token[:, 4], width
    )
    middle_grad = upper + norm_two
    merged_grad = gather_grad((per_token[:, 2] * middle_grad).astype(jnp.bfloat16))
    mixed_grad = (
        lax.dot_general(
            merged_grad, merge_full, (((1,), (1,)), ((), ())), preferred_element_type=jnp.float32
        )
        .astype(jnp.bfloat16)
        .reshape(windows, window, heads_local, HD)
    )
    merge_grad = lax.dot_general(
        mixed, merged_grad, (((0,), (0,)), ((), ())), preferred_element_type=jnp.float32
    )
    again = attention_scores(query, keys, bias, same, factor)
    exact = jnp.exp(again - logsum)
    chance_grad = jnp.einsum(
        "wihe,wjhe->whij", mixed_grad, values, preferred_element_type=jnp.float32
    )
    score_grad = (
        exact * (chance_grad - jnp.sum(exact * chance_grad, axis=-1, keepdims=True))
    ).astype(jnp.bfloat16)
    value_grad = jnp.einsum(
        "whij,wihe->wjhe",
        exact.astype(jnp.bfloat16),
        mixed_grad,
        preferred_element_type=jnp.float32,
    )
    query_grad = (
        jnp.einsum("whij,wjhe->wihe", score_grad, keys, preferred_element_type=jnp.float32) * factor
    )
    keys_grad = (
        jnp.einsum("whij,wihe->wjhe", score_grad, query, preferred_element_type=jnp.float32)
        * factor
    )
    triple_grad = jnp.stack(
        [
            query_grad.reshape(tokens, local_width),
            keys_grad.reshape(tokens, local_width),
            value_grad.reshape(tokens, local_width),
        ],
        axis=1,
    ).astype(jnp.bfloat16)
    bias_grad = lax.all_to_all(score_grad, "mp", split_axis=2, concat_axis=1, tiled=True)
    pair_grad = jnp.einsum(
        "whij,ch->wijc", bias_grad, pair_full, preferred_element_type=jnp.float32
    ).astype(jnp.bfloat16)
    pairwise_grad = jnp.einsum(
        "wijc,whij->ch", pair_input, bias_grad, preferred_element_type=jnp.float32
    )
    attend_grad = jnp.einsum(
        "td,tje->dje", rows_one, triple_grad, preferred_element_type=jnp.float32
    )
    partial_one = jnp.einsum(
        "tje,dje->td", triple_grad, attend_full, preferred_element_type=jnp.float32
    )
    upstream_one, norm_one = normalize_back(
        partial_one, normed_one, spread_one, per_token[:, 1], width
    )
    residue_grad = (middle_grad + norm_one).astype(jnp.bfloat16)
    token_mod_grad = jnp.stack(
        [
            upstream_one,
            upstream_one * normed_one,
            middle_grad * attended,
            upstream_two,
            upstream_two * normed_two,
            upper * fed,
        ],
        axis=1,
    ).reshape(windows, window, 6, local_width)
    mod_grad = jnp.einsum("wts,wtjd->wsjd", pick, token_mod_grad, precision=HIGH)
    modulate_grad = jnp.einsum(
        "wsc,wsjd->cjd", condition.astype(jnp.float32), mod_grad, precision=HIGH
    )
    cond_grad = jnp.einsum(
        "wsjd,cjd->wsc", mod_grad, modulate_full.astype(jnp.float32), precision=HIGH
    )
    sig_before = jax.nn.sigmoid(before)
    before_grad = cond_grad * (sig_before * (1.0 + before * (1.0 - sig_before)))
    class_grad = jnp.einsum("wsn,wsc->nc", class_pick, before_grad, precision=HIGH)
    shared = lax.psum((pairwise_grad, class_grad), "mp")
    sums = (
        lax.psum_scatter(attend_grad, "dp", scatter_dimension=0, tiled=True),
        lax.psum_scatter(merge_grad, "dp", scatter_dimension=1, tiled=True),
        lax.psum_scatter(expand_grad, "dp", scatter_dimension=0, tiled=True),
        lax.psum_scatter(shrink_grad, "dp", scatter_dimension=1, tiled=True),
        lax.psum_scatter(modulate_grad, "dp", scatter_dimension=0, tiled=True),
        lax.psum_scatter(shared[0], "dp", scatter_dimension=0, tiled=True),
        lax.psum_scatter(shared[1], "dp", scatter_dimension=1, tiled=True),
    )
    rates = (
        2.0 / math.sqrt(D),
        2.0 / math.sqrt(D // 8),
        2.0 / math.sqrt(D),
        2.0 / math.sqrt(FF),
        2.0 / math.sqrt(CDIM),
        2.0 / math.sqrt(PAIR),
        2.0,
    )
    masters = (
        attend_weight,
        merge_weight,
        expand_weight,
        shrink_weight,
        modulate_weight,
        pair_weight,
        class_weight,
    )
    states = (
        attend_state,
        merge_state,
        expand_state,
        shrink_state,
        modulate_state,
        pair_state,
        class_state,
    )
    results = []
    for index in range(7):
        updated, tracked = adamw(masters[index], states[index], sums[index], rates[index])
        results.append(updated)
        results.append(tracked)
    return (
        output,
        residue_grad,
        pair_grad,
        results[0],
        results[1],
        results[2],
        results[3],
        results[4],
        results[5],
        results[6],
        results[7],
        results[8],
        results[9],
        results[10],
        results[11],
        results[12],
        results[13],
    )


ANGLES = (1000.0 * (np.arange(128, dtype=np.float32)[:, None] + 0.5) / TBINS) * np.exp(
    -math.log(10000.0) * np.arange(128, dtype=np.float32) / 128
)
WAVES = np.concatenate([np.sin(ANGLES), np.cos(ANGLES)], axis=-1).astype(np.float32)
RATES = (
    2.0 / math.sqrt(D),
    2.0 / math.sqrt(D // 8),
    2.0 / math.sqrt(D),
    2.0 / math.sqrt(FF),
    2.0 / math.sqrt(CDIM),
    2.0 / math.sqrt(PAIR),
    2.0,
)
f32 = jnp.float32
bf16 = jnp.bfloat16
NT = (((1,), (1,)), ((), ()))
NN = (((1,), (0,)), ((), ()))
TN = (((0,), (0,)), ((), ()))
HEADS = 12
GROUP = 16
UNIT = 64
CHUNK = 16
PAIRS = 8


def mm(a, b, dims=NN, precision=None):
    return lax.dot_general(a, b, dims, precision=precision, preferred_element_type=f32)


def head_mask(count):
    row = lax.broadcasted_iota(jnp.int32, (count, GROUP, D), 1)
    col = lax.broadcasted_iota(jnp.int32, (count, GROUP, D), 2) // HD
    return row == col


def spread_heads(rows):
    count = rows.shape[0]
    wide = jnp.broadcast_to(rows.astype(f32)[:, None, :], (count, GROUP, D))
    return jnp.where(head_mask(count), wide, 0.0).astype(bf16).reshape(count * GROUP, D)


def merge_heads(wide):
    count = wide.shape[0] // GROUP
    return jnp.sum(jnp.where(head_mask(count), wide.reshape(count, GROUP, D), 0.0), axis=1)


class Net:
    def __init__(self, send_sems, recv_sems):
        self.d = lax.axis_index("dp")
        self.m = lax.axis_index("mp")
        core = self.d % 2
        x = (self.d // 2) % 2
        y = self.d // 4
        self.core = core
        self.chip = self.d // 2
        self.chips = [self.chip, y * 2 + 1 - x, (1 - y) * 2 + x, (1 - y) * 2 + 1 - x]
        self.partner = self.chip * 2 + 1 - core
        self.send_sems = send_sems
        self.recv_sems = recv_sems
        self.sent = []
        self.open = []
        self.base = 0

    def z(self, t):
        return (self.m + t) % 4

    def peer(self, r):
        return self.chips[r] * 2 + self.core

    def sems(self, count):
        base = self.base
        self.base = base + count
        return base

    def barrier(self):
        sem = pltpu.get_barrier_semaphore()
        targets = [(self.d, self.z(t)) for t in (1, 2, 3)]
        targets += [(self.peer(r), self.m) for r in (1, 2, 3)] + [(self.partner, self.m)]
        for target in targets:
            pl.semaphore_signal(
                sem, inc=1, device_id=target, device_id_type=pl.DeviceIdType.MESH
            )
        pl.semaphore_wait(sem, len(targets))

    def copy(self, src, dst, recv, target, send=None):
        send = len(self.sent) if send is None else send
        return pltpu.make_async_remote_copy(
            src_ref=src,
            dst_ref=dst,
            send_sem=self.send_sems.at[send],
            recv_sem=self.recv_sems.at[recv],
            device_id=target,
            device_id_type=pl.DeviceIdType.MESH,
        )

    def send(self, src, dst, recv, target):
        made = self.copy(src, dst, recv, target)
        made.start()
        self.sent.append(made)
        self.open.append(made)
        return made

    def wait(self, dst, recv):
        self.copy(dst, dst, recv, (self.partner, self.m), 0).wait_recv()

    def drain(self):
        for made in self.open:
            made.wait_send()

    def settle(self, made):
        made.wait_send()
        self.open = [other for other in self.open if other is not made]


class Spread:
    def __init__(self, net, slot):
        self.net, self.slot, self.base = net, slot, net.sems(7)

    def start(self, src=None):
        net = self.net
        own = self.slot(net.d)
        src = own if src is None else src
        made = [net.send(src, own, self.base + r, (net.peer(r), net.m)) for r in (1, 2, 3)]
        return made + [net.send(src, own, self.base, (net.partner, net.m))]

    def forward(self, r):
        net = self.net
        slot = self.slot(net.peer(r))
        net.wait(slot, self.base + r)
        return [net.send(slot, slot, self.base + 3 + r, (net.partner, net.m))]

    def finish(self):
        net = self.net
        net.wait(self.slot(net.partner), self.base)
        for r in (1, 2, 3):
            net.wait(self.slot(net.chips[r] * 2 + 1 - net.core), self.base + 3 + r)


class Zline:
    def __init__(self, net, slot):
        self.net, self.slot, self.base = net, slot, net.sems(4)

    def send(self, t, src):
        net = self.net
        net.send(src, self.slot(net.m), self.base + net.m, (net.d, net.z(t)))

    def wait(self, t):
        net = self.net
        source = net.z(t)
        net.wait(self.slot(source), self.base + source)
        return source


def layer_kernel(
    aw, mw, ew, sw, ow, pwt, cwt, xt, gt, pair, waves, layout, bins, kinds,
    out_o, res_o, ds_o, pw_o, at_o, mg_o, ex_o, sh_o, mod_o, pair_o, class_o,
    msg, amg, esg, xg, gg, modu, modg, modf, bpg, pb, n1, sp1, r1,
    kf, vf, qf, pr, mix, att, mid, n2, sp2, r2, fg, act, upg, fp, fl, p2, p2l, p2o, fpo,
    esp, epl, exl, dkv, dkf, dvf, dqf, mgd, l2, rhs2, p1, p1l,
    amp, axl, aso, azs, azl, mps, mpl, mrg, pws, pwl, pwx, pwy, pco, pcl,
    ops, opl, rps, rpl, ctf, cfull,
    mask, send_sems, recv_sems, pair_sems,
):
    net = Net(send_sems, recv_sems)
    d, m = net.d, net.m

    chunks = 16
    slots = pb.shape[0]

    def pair_copy(step):
        c = step % chunks
        return pltpu.make_async_copy(
            pair.at[c // 8, pl.ds((c % 8) * PAIRS, PAIRS)],
            pb.at[step % slots],
            pair_sems.at[step % slots],
        )

    for step in range(slots):
        pair_copy(step).start()

    dkf[0:256, 0:128] = jnp.zeros((256, 128), f32)
    dkf[0:192, 0:96] = mw[...]
    tall = dkf[0:256, 0:128].T
    amg[m, d] = jnp.concatenate([aw[1], aw[2], aw[0], tall[0:96, 0:192]], axis=-1).astype(bf16)
    cfull[...] = jnp.zeros_like(cfull)
    cfull[0:HEADS, 0:32] = pwt[...]
    cfull[128:160, 0 : cwt.shape[1]] = cwt[...]
    narrow = [cfull[128:160, 0:64], cfull[0:128, :].T[0:32, 0:64]]
    msg[d] = jnp.concatenate(narrow + [ow[j] for j in range(6)], axis=-1).astype(bf16)
    net.barrier()

    row8 = lax.broadcasted_iota(jnp.int32, (8, 128), 0)
    lane8 = lax.broadcasted_iota(jnp.int32, (8, 128), 1)
    bin8 = jnp.zeros((8, 128), jnp.int32)
    kind8 = jnp.zeros((8, 128), jnp.int32)
    mask_row = lax.broadcasted_iota(jnp.int32, (8, 256), 0)
    mask_unit = lax.broadcasted_iota(jnp.int32, (8, 256), 1) // UNIT
    seen = jnp.zeros((8, 256), f32)
    for w in range(2):
        at = layout[w]
        held = []
        for u in range(4):
            slot = jnp.int32(0)
            for k in range(5):
                slot = jnp.where(at == k, jnp.int32(int(PATTERNS[k, u])), slot)
            held.append(slot)
        mine = jnp.int32(0)
        for u in range(4):
            mine = jnp.where(m == u, held[u], mine)
        for u in range(4):
            time, kind = jnp.int32(0), jnp.int32(0)
            for i in range(4):
                time = jnp.where(held[u] == i, bins[w, i], time)
                kind = jnp.where(held[u] == i, kinds[w, i], kind)
            bin8 = jnp.where(row8 == 4 * w + u, time, bin8)
            kind8 = jnp.where(row8 == 4 * w + u, kind, kind8)
            value = jnp.where(held[u] == mine, 0.0, MASKED)
            seen = jnp.where((mask_row == w) & (mask_unit == u), value, seen)
    mask[...] = seen
    pick = jnp.where(lane8 == kind8, 1.0, 0.0).astype(bf16)
    sinus = mm(jnp.where(lane8 == bin8, 1.0, 0.0), waves[...], NN, HIGH)

    cp_all = Spread(net, lambda i: msg.at[i, :, 0:128])
    ms_all = Spread(net, lambda i: msg.at[i, :, 128:1280])
    am_line = Zline(net, lambda s: amg.at[s, d])
    am_all = [Spread(net, lambda i, t=t: amg.at[net.z(t), i]) for t in range(4)]
    x_line = Zline(net, lambda s: xg.at[s])
    g_line = Zline(net, lambda s: gg.at[s])
    mod_line = Zline(net, lambda s: modg.at[s])
    bp_all = Spread(net, lambda i: bpg.at[i])
    es_all = Spread(net, lambda i: esg.at[i])

    cp_all.start()
    for t in (1, 3, 2):
        am_line.send(t, amg.at[m, d])
    ms_all.start()
    am_all[0].start()
    esg[d] = jnp.concatenate([ew[:, 0, :], ew[:, 1, :], sw[...]], axis=-1).astype(bf16)

    def pack_rows(source, ref):
        wide = jnp.concatenate([source[...], jnp.zeros((64, 512), bf16)], axis=0).T
        ref[m, 0:512, :] = wide[:, 0:128]
        low = wide[:, 128:192]
        ref[m, 512:768, :] = jnp.concatenate([low[0:256], low[256:512]], axis=-1)

    pack_rows(xt, xg)
    pack_rows(gt, gg)
    for r in (1, 2, 3):
        cp_all.forward(r)
    cp_all.finish()

    slab = msg[:, :, 0:128].reshape(256, 128)
    select = (
        lax.broadcasted_iota(jnp.int32, (GROUP, 128), 1)
        == lax.broadcasted_iota(jnp.int32, (GROUP, 128), 0) + 64
    ) & (lax.broadcasted_iota(jnp.int32, (GROUP, 128), 0) < HEADS)
    pw_o[...] = mm(jnp.where(select, 1.0, 0.0).astype(bf16), slab, NT).astype(bf16)
    before = sinus + mm(pick, slab, NT)
    condition = (before * jax.nn.sigmoid(before)).astype(bf16)
    bpg[d] = jnp.concatenate([before, pick.astype(f32)], axis=-1)

    def bias_chunk(step):
        slot = step % slots
        pair_copy(step).wait()

        def one(i, carry):
            part = mm(pw_o[...], pb[slot, i], NT)
            at = pl.multiple_of((step % 8) * PAIRS * GROUP + i * GROUP, GROUP)
            ds_o[step // 8, pl.ds(at, GROUP), :] = part.astype(bf16)
            return carry

        lax.fori_loop(0, PAIRS, one, 0, unroll=4)
        pair_copy(step + slots).start()

    bias_chunk(0)
    bias_chunk(1)
    for r in (1, 2, 3):
        ms_all.forward(r)
    bias_chunk(2)
    am_line.wait(1)
    am_all[1].start()
    bias_chunk(3)
    ms_all.finish()
    modu[...] = mm(condition, msg[:, :, 128:1280].reshape(256, 1152))
    modg[m] = modu[...]
    am_line.wait(3)
    am_all[3].start()
    bias_chunk(4)
    for r in (1, 2):
        am_all[0].forward(r)
    bias_chunk(5)
    am_line.wait(2)
    am_all[2].start()
    for t in (1, 2, 3):
        x_line.send(t, xg.at[m])
    for t in (1, 2, 3):
        mod_line.send(t, modu)
    bias_chunk(6)
    am_all[0].forward(3)
    bias_chunk(7)
    for r in (1, 2):
        am_all[1].forward(r)
    for step in (8, 9, 10):
        bias_chunk(step)
    am_all[1].forward(3)
    for r in (1, 2):
        am_all[3].forward(r)
    for step in (11, 12, 13):
        bias_chunk(step)
    am_all[3].forward(3)
    for r in (1, 2):
        am_all[2].forward(r)
    bias_chunk(14)
    bias_chunk(15)

    for t in (1, 2, 3):
        mod_line.wait(t)
    for j in range(6):
        modf[j] = jnp.concatenate([modg[s, :, 192 * j : 192 * j + 192] for s in range(4)], axis=-1)
    for t in (1, 2, 3):
        x_line.wait(t)

    def unpack(ref, w, unit):
        parts = []
        for s in range(4):
            parts.append(ref[s, pl.ds(w * 256 + unit * UNIT, UNIT), :].astype(f32))
            low = ref[s, pl.ds(512 + unit * UNIT, UNIT), :].astype(f32)
            parts.append(low[:, 64 * w : 64 * w + 64])
        return jnp.concatenate(parts, axis=-1)

    def norm(v):
        center = jnp.mean(v, axis=-1, keepdims=True)
        spread = lax.rsqrt(jnp.mean(v * v, axis=-1, keepdims=True) - center * center + NORM_EPS)
        return (v - center) * spread, spread

    for w in range(2):

        def first_norm(unit, carry, w=w):
            v = unpack(xg, w, unit)
            rows = pl.ds(pl.multiple_of(w * 256 + unit * UNIT, UNIT), UNIT)
            normed, spread = norm(v)
            n1[rows, :] = normed
            sp1[rows, :] = jnp.broadcast_to(spread, (UNIT, 128))
            shift = modf[0, pl.ds(w * 4 + unit, 1), :]
            scale = modf[1, pl.ds(w * 4 + unit, 1), :]
            r1[rows, :] = (normed * (1.0 + scale) + shift).astype(bf16)
            return carry

        lax.fori_loop(0, 4, first_norm, 0)

    am_all[2].forward(3)
    es_sent = es_all.start()
    for t in (1, 2, 3):
        g_line.send(t, gg.at[m])
    bp_all.start()
    for t in (0, 1, 3, 2):
        am_all[t].finish()

    def own(w):
        return pl.ds(pl.multiple_of(w * 256 + m * UNIT, UNIT), UNIT)

    def weight(s, lo, hi):
        return amg[s, :, :, lo:hi].reshape(D, hi - lo)

    r1_own = jnp.concatenate([r1[own(0), :], r1[own(1), :]], axis=0)
    qf[...] = jnp.concatenate(
        [mm(r1_own, weight(s, 384, 768))[:, 0:192] for s in range(4)], axis=-1
    ).astype(bf16)
    for w in range(2):
        rows = slice(w * 256, w * 256 + 256)
        both = [mm(r1[rows, :], weight(s, 0, 384)) for s in range(4)]
        kf[rows, :] = jnp.concatenate([v[:, 0:192] for v in both], axis=-1).astype(bf16)
        vf[rows, :] = jnp.concatenate([v[:, 192:384] for v in both], axis=-1).astype(bf16)

    factor = HD ** (-0.5)

    def attend(c, carry):
        w = c // 4
        mine = pl.ds(pl.multiple_of(c * CHUNK, CHUNK), CHUNK)
        keys = pl.ds(pl.multiple_of(w * 256, 256), 256)
        wide = pl.ds(pl.multiple_of((c % 4) * CHUNK * GROUP, CHUNK * GROUP), CHUNK * GROUP)
        scores = mm(spread_heads(qf[mine, :]), kf[keys, :], NT) * factor
        scores = scores + ds_o[w, wide, :].astype(f32) + mask[pl.ds(w, 1), :]
        peak = jnp.max(scores, axis=-1, keepdims=True)
        expo = jnp.exp(scores - peak)
        chance = expo / jnp.sum(expo, axis=-1, keepdims=True)
        pr[w, wide, :] = chance
        mix[mine, :] = merge_heads(mm(chance.astype(bf16), vf[keys, :])).astype(bf16)
        return carry

    def mod_row(j, w):
        return modf[j, pl.ds(w * 4 + m, 1), :]

    blank = jnp.zeros((128, 192), bf16)
    r2_lines = []
    for w in range(2):
        half = slice(w * UNIT, w * UNIT + UNIT)
        lax.fori_loop(4 * w, 4 * w + 4, attend, 0)
        mixed = mix[half, :]
        attended = 0.0
        for s in range(4):
            part = jnp.concatenate([blank[:UNIT], mixed[:, 192 * s : 192 * s + 192]], axis=-1)
            attended = attended + mm(part, weight(s, 384, 768), NT)
        att[half, :] = attended
        middle = unpack(xg, w, m) + mod_row(2, w) * attended
        mid[half, :] = middle
        normed, spread = norm(middle)
        n2[half, :] = normed
        sp2[half, :] = jnp.broadcast_to(spread, (UNIT, 128))
        r2[m, half, :] = (normed * (1.0 + mod_row(4, w)) + mod_row(3, w)).astype(bf16)
        line = Zline(net, lambda s, half=half: r2.at[s, half])
        r2_lines.append(line)
        for t in (1, 3, 2):
            line.send(t, r2.at[m, half])
        for r in ((1, 2), (3,))[w]:
            es_sent += es_all.forward(r)

    for t in (1, 2, 3):
        g_line.wait(t)
    for s in range(4):
        for w in range(2):
            half = slice(w * UNIT, w * UNIT + UNIT)
            upper = unpack(gg, w, s)
            fg[s, half, :] = (modf[5, w * 4 + s : w * 4 + s + 1, :] * upper).astype(bf16)
    es_all.finish()

    p2_line = Zline(net, lambda s: p2l.at[s])
    f_line = Zline(net, lambda s: fl.at[s])

    def feed(s):
        expand = esg[:, :, 0:1536].reshape(D, 1536)
        shrink = esg[:, :, 1536:2304].reshape(D, 768)
        up = mm(r2[s], expand)
        gate = up[:, 0:768]
        upward = up[:, 768:1536]
        act_grad = mm(fg[s], shrink)
        sigma = jax.nn.sigmoid(gate)
        activated = (gate * sigma * upward).astype(bf16)
        act[s] = activated
        slope = sigma * (1.0 + gate * (1.0 - sigma))
        grads = jnp.concatenate(
            [(act_grad * upward * slope).astype(bf16), (act_grad * gate * sigma).astype(bf16)],
            axis=-1,
        )
        upg[s] = grads
        return mm(grads, expand, NT), mm(activated, shrink, NT)

    partial, fed = feed(m)
    p2o[...] = partial
    fpo[...] = fed
    for t in (1, 3, 2):
        for line in r2_lines:
            source = line.wait(t)
        partial, fed = feed(source)
        p2[source] = partial.astype(bf16)
        p2_line.send(t, p2.at[source])
        fp[source] = fed.astype(bf16)

    def put_es(left, right, at):
        for h in range(2):
            value = mm(left[:, :, 384 * h : 384 * h + 384].reshape(512, 384), right, TN)
            for i in range(4):
                part = value[96 * i : 96 * i + 96, :].astype(bf16)
                esp[i % 2, 2 * h + i // 2, :, at : at + 768] = part

    put_es(r2, upg[:, :, 0:768].reshape(512, 768), 0)
    put_es(r2, upg[:, :, 768:1536].reshape(512, 768), 768)
    put_es(fg, act[...].reshape(512, 768), 1536)
    for made in es_sent:
        net.settle(made)
    es_pair = net.sems(1)
    net.send(esp.at[1 - net.core], epl, es_pair, (net.partner, m))

    for t in (1, 3, 2):
        p2_line.wait(t)
    for t in (1, 3, 2):
        f_line.send(t, fp.at[net.z(t)])

    def norm_back(upstream, normed, spread, scale):
        inner = upstream * (1.0 + scale)
        first = jnp.mean(inner, axis=-1, keepdims=True)
        second = jnp.mean(inner * normed, axis=-1, keepdims=True)
        return spread * (inner - first - normed * second)

    def unit_sum(v):
        return jnp.sum(v, axis=0, keepdims=True)

    own_sums = [[None] * 6, [None] * 6]
    for w in range(2):
        half = slice(w * UNIT, w * UNIT + UNIT)
        upstream = p2o[half, :]
        for t in (1, 3, 2):
            upstream = upstream + p2l[net.z(t), half, :].astype(f32)
        normed = n2[half, :]
        back = norm_back(upstream, normed, sp2[half, 0:1], mod_row(4, w))
        grad = unpack(gg, w, m) + back
        p2o[half, :] = grad
        own_sums[w][2] = unit_sum(grad * att[half, :])
        own_sums[w][3] = unit_sum(upstream)
        own_sums[w][4] = unit_sum(upstream * normed)
        l2[slice(128 + w * UNIT, 128 + w * UNIT + UNIT), :] = (mod_row(2, w) * grad).astype(bf16)
        l2[half, :] = r1[own(w), :]
    merged_grad = l2[128:256, :]
    mgd[...] = jnp.concatenate(
        [mm(merged_grad, weight(s, 384, 768))[:, 192:384] for s in range(4)], axis=-1
    ).astype(bf16)

    net.wait(epl, es_pair)
    es_chip = net.sems(4)
    for r in (1, 2, 3):
        total = esp[net.core, net.chips[r]].astype(f32) + epl[net.chips[r]].astype(f32)
        esp[net.core, net.chips[r]] = total.astype(bf16)
        net.send(esp.at[net.core, net.chips[r]], exl.at[r - 1], es_chip + r, (net.peer(r), m))

    dkf[...] = jnp.zeros_like(dkf)
    dvf[...] = jnp.zeros_like(dvf)

    def attend_back(c, carry):
        w = c // 4
        mine = pl.ds(pl.multiple_of(c * CHUNK, CHUNK), CHUNK)
        keys = pl.ds(pl.multiple_of(w * 256, 256), 256)
        wide = pl.ds(pl.multiple_of((c % 4) * CHUNK * GROUP, CHUNK * GROUP), CHUNK * GROUP)
        grad = spread_heads(mgd[mine, :])
        chance = pr[w, wide, :]
        chance_grad = mm(grad, vf[keys, :], NT)
        inner = jnp.sum(chance * chance_grad, axis=-1, keepdims=True)
        score = (chance * (chance_grad - inner)).astype(bf16)
        ds_o[w, wide, :] = score
        dqf[mine, :] = (merge_heads(mm(score, kf[keys, :])) * factor).astype(bf16)
        dvf[keys, :] += mm(chance.astype(bf16), grad, TN)
        dkf[keys, :] += mm(score, spread_heads(qf[mine, :]), TN) * factor
        return carry

    lax.fori_loop(0, 8, attend_back, 0)

    o_line = Zline(net, lambda s: opl.at[s])

    def pack(line, value, ref):
        for s in range(4):
            part = value[:, 192 * s : 192 * s + 192]
            ref[s, 0:128, :] = part[:, 0:128].astype(bf16)
            low = part[:, 128:192]
            ref[s, 128:192, :] = jnp.concatenate([low[0:64], low[64:128]], axis=-1).astype(bf16)
        for t in (1, 3, 2):
            line.send(t, ref.at[net.z(t)])

    def unpack_out(line, ref, mine, to):
        for t in (0, 1, 3, 2):
            s = net.z(t)
            block = mine if t == 0 else ref
            if t:
                line.wait(t)
            for w in range(2):
                rows = pl.ds(pl.multiple_of(w * 256 + s * UNIT, UNIT), UNIT)
                high = block[s, w * UNIT : w * UNIT + UNIT, :].astype(f32)
                low = block[s, 128:192, :].astype(f32)[:, 64 * w : 64 * w + 64]
                to[rows, :] = jnp.concatenate([high, low], axis=-1).astype(bf16)

    for s in range(4):
        cols = slice(192 * s, 192 * s + 192)
        dkv[s] = jnp.concatenate([dkf[:, cols], dvf[:, cols]], axis=-1).astype(bf16)
        rhs2[s, 0:128, :] = jnp.concatenate([dqf[:, cols], blank], axis=-1)
        rhs2[s, 128:256, :] = jnp.concatenate([blank, mix[:, cols]], axis=-1)
    am_pair = net.sems(4)

    def apl(t):
        return esg.at[pl.ds(4 * (t // 3), 4), :, 768 * (t % 3) : 768 * (t % 3) + 768]

    am_chip = net.sems(16)

    def am_total(t, r):
        base, cols = 4 * (t // 3), slice(768 * (t % 3), 768 * (t % 3) + 768)
        total = amp[net.z(t), net.core, net.chips[r]].astype(f32)
        return total + esg[base + net.chips[r], :, cols].astype(f32)

    def am_grads(t):
        s = net.z(t)
        for h in range(2):
            cols = slice(384 * h, 384 * h + 384)
            for left, right, at in ((r1, dkv, 0), (l2, rhs2, 384)):
                value = mm(left[:, cols], right[s], TN)
                for i in range(4):
                    part = value[96 * i : 96 * i + 96, :].astype(bf16)
                    amp[s, i % 2, 2 * h + i // 2, :, at : at + 384] = part
        net.send(amp.at[s, 1 - net.core], apl(t), am_pair + t, (net.partner, m))

    def am_out(t):
        s = net.z(t)
        net.wait(apl(t), am_pair + t)
        for r in (1, 2, 3):
            part = amp.at[s, net.core, net.chips[r]]
            part[...] = am_total(t, r).astype(bf16)
            net.send(part, axl.at[s, r - 1], am_chip + 4 * t + r, (net.peer(r), m))

    am_grads(1)
    am_grads(3)
    am_out(1)
    am_grads(2)
    am_out(3)
    am_grads(0)
    am_out(2)

    for t in (1, 3, 2):
        f_line.wait(t)
    fed_done = []
    for w in range(2):
        half = slice(w * UNIT, w * UNIT + UNIT)
        fed = fpo[half, :]
        for t in (1, 3, 2):
            fed = fed + fl[net.z(t), half, :].astype(f32)
        own_sums[w][5] = unit_sum(unpack(gg, w, m) * fed)
        fed_done.append(mid[half, :] + mod_row(5, w) * fed)

    for w in range(2):
        rows = slice(w * 256, w * 256 + 256)
        total = mm(dkv[0, rows, :], weight(0, 0, 384), NT)
        for s in range(1, 4):
            total = total + mm(dkv[s, rows, :], weight(s, 0, 384), NT)
        dkf[rows, :] = total
    total = mm(rhs2[0, 0:128, :], weight(0, 384, 768), NT)
    for s in range(1, 4):
        total = total + mm(rhs2[s, 0:128, :], weight(s, 384, 768), NT)
    for w in range(2):
        dkf[own(w), :] += total[w * UNIT : w * UNIT + UNIT, :]

    sums = [[], []]
    for u in range(8):
        rows = slice(u * UNIT, u * UNIT + UNIT)
        sums[0].append(unit_sum(dkf[rows, :]))
        sums[1].append(unit_sum(dkf[rows, :] * n1[rows, :]))
    row = lax.broadcasted_iota(jnp.int32, (8, D), 0)
    table = [jnp.concatenate(sums[0], axis=0), jnp.concatenate(sums[1], axis=0)]
    for j in range(2, 6):
        first = jnp.broadcast_to(own_sums[0][j], (8, D))
        second = jnp.broadcast_to(own_sums[1][j], (8, D))
        table.append(jnp.where(row == m, first, jnp.where(row == m + 4, second, 0.0)))
    mod_sum = Zline(net, lambda s: mpl.at[s])
    for s in range(4):
        mps[s] = jnp.concatenate([v[:, 192 * s : 192 * s + 192] for v in table], axis=-1)
    for t in (1, 3, 2):
        mod_sum.send(t, mps.at[net.z(t)])
    p1_line = Zline(net, lambda s: p1l.at[s])
    for t in (1, 3, 2):
        s = net.z(t)
        for w in range(2):
            rows = pl.ds(pl.multiple_of(w * 256 + s * UNIT, UNIT), UNIT)
            p1[s, w * UNIT : w * UNIT + UNIT, :] = dkf[rows, :].astype(bf16)
        p1_line.send(t, p1.at[s])
    pack(o_line, jnp.concatenate(fed_done, axis=0), ops)

    def pair_chunk(step, acc):
        slot = step % slots
        pair_copy(step).wait()

        def one(i, acc):
            at = pl.multiple_of((step % 8) * PAIRS * GROUP + i * GROUP, GROUP)
            return acc + mm(ds_o[(step - 16) // 8, pl.ds(at, GROUP), :], pb[slot, i])

        acc = lax.fori_loop(0, PAIRS, one, acc, unroll=4)
        if step + slots < 2 * chunks:
            pair_copy(step + slots).start()
        return acc

    pairwise = jnp.zeros((GROUP, 256), f32)
    for step in range(16, 32):
        pairwise = pair_chunk(step, pairwise)

    for r in (1, 2, 3):
        bp_all.forward(r)
    bp_all.finish()

    wide = jnp.concatenate([pairwise, jnp.zeros((112, 256), f32)], axis=0).T
    for i in range(8):
        pws[i % 2, i // 2] = wide[32 * i : 32 * i + 32, :]
    pw_pair = net.sems(1)
    net.send(pws.at[1 - net.core], pwl, pw_pair, (net.partner, m))

    for t in (1, 3, 2):
        mod_sum.wait(t)
    mod_grad = mps[m]
    for t in (1, 3, 2):
        mod_grad = mod_grad + mpl[net.z(t)]
    mrg[d] = mod_grad
    mr_all = Spread(net, lambda i: mrg.at[i])
    mr_all.start()

    am_z = Zline(net, lambda s: azl.at[s])

    def am_arrive(t):
        s = net.z(t)
        total = am_total(t, 0)
        for r in (1, 2, 3):
            net.wait(axl.at[s, r - 1], am_chip + 4 * t + r)
            total = total + axl[s, r - 1].astype(f32)
        if t:
            azs[s] = total.astype(bf16)
            am_z.send(t, azs.at[s])
        else:
            aso[...] = total

    net.wait(pwl, pw_pair)
    pw_chip = net.sems(4)
    for r in (1, 2, 3):
        pwx[r] = pws[net.core, net.chips[r]] + pwl[net.chips[r]]
        net.send(pwx.at[r], pwy.at[r], pw_chip + r, (net.peer(r), m))
    pair_sum = pws[net.core, net.chip] + pwl[net.chip]

    am_out(0)
    am_arrive(1)
    am_arrive(3)

    total = esp[net.core, net.chip].astype(f32) + epl[net.chip].astype(f32)
    for r in (1, 2, 3):
        net.wait(exl.at[r - 1], es_chip + r)
        total = total + exl[r - 1].astype(f32)
    for k in range(2):
        ex_o[:, k, :] = total[:, 768 * k : 768 * k + 768]
    sh_o[...] = total[:, 1536:2304]

    am_arrive(2)

    for t in (1, 3, 2):
        p1_line.wait(t)
    r_line = Zline(net, lambda s: rpl.at[s])
    done = []
    for w in range(2):
        half = slice(w * UNIT, w * UNIT + UNIT)
        upstream = dkf[own(w), :]
        for t in (1, 3, 2):
            upstream = upstream + p1l[net.z(t), half, :].astype(f32)
        back = norm_back(upstream, n1[own(w), :], sp1[own(w), :][:, 0:1], mod_row(1, w))
        done.append(p2o[half, :] + back)
    pack(r_line, jnp.concatenate(done, axis=0), rps)

    for r in (1, 2, 3):
        mr_all.forward(r)

    mr_all.finish()
    before = bpg[:, :, 0:256].reshape(64, 256)
    sig = jax.nn.sigmoid(before)
    condition = (before * sig).astype(bf16).astype(f32)
    picks = bpg[:, :, 256:384].reshape(64, 128)
    grads = mrg[...].reshape(64, 1152)
    ctf[...] = condition.T
    mod_sums = mm(ctf[pl.ds(pl.multiple_of(d * 32, 32), 32), :], grads, NN, HIGH)
    for j in range(6):
        mod_o[j] = mod_sums[:, 192 * j : 192 * j + 192]
    cond_grad = mm(grads, msg[:, :, 128:1280].reshape(256, 1152).astype(f32), NT, HIGH)
    before_grad = cond_grad * (sig * (1.0 + before * (1.0 - sig)))
    cfull[...] = mm(before_grad, picks, TN, HIGH)
    for r in (1, 2, 3):
        net.wait(pwy.at[r], pw_chip + r)
        pair_sum = pair_sum + pwy[r]
    pco[...] = jnp.concatenate(
        [pair_sum, cfull[pl.ds(pl.multiple_of(d * 32, 32), 32), :]], axis=-1
    )
    pc_line = Zline(net, lambda s: pcl.at[s])
    for t in (1, 3, 2):
        pc_line.send(t, pco)

    unpack_out(o_line, opl, ops, out_o)
    unpack_out(r_line, rpl, rps, res_o)
    am_arrive(0)
    total = aso[...]
    for t in (1, 3, 2):
        total = total + azl[am_z.wait(t)].astype(f32)
    at_o[0] = total[:, 384:576]
    at_o[1] = total[:, 0:192]
    at_o[2] = total[:, 192:384]
    tall = jnp.concatenate([total[:, 512:768], jnp.zeros((32, 256), f32)], axis=0).T
    mg_o[...] = tall[64:256, 0:96]
    total = pco[...]
    for t in (1, 3, 2):
        total = total + pcl[pc_line.wait(t)]
    tall = jnp.concatenate([total[:, 0:128], jnp.zeros((96, 128), f32)], axis=0).T
    pair_o[...] = tall[0:HEADS, 0:32]
    class_o[...] = total[:, 128 : 128 + class_o.shape[1]]
    net.drain()


def layer_call(classes, *args):
    V = pltpu.VMEM
    scratch = [
        V((8, 32, 1280), bf16), V((4, 8, 96, 768), bf16), V((8, 96, 2304), bf16),
        V((4, 768, 128), bf16), V((4, 768, 128), bf16),
        V((8, 1152), f32), V((4, 8, 1152), f32), V((6, 8, 768), f32), V((8, 8, 384), f32),
        V((2, PAIRS, 256, 256), bf16),
        V((512, 768), f32), V((512, 128), f32), V((512, 768), bf16),
        V((512, 768), bf16), V((512, 768), bf16), V((128, 768), bf16), V((2, 1024, 256), f32),
        V((128, 768), bf16), V((128, 768), f32), V((128, 768), f32), V((128, 768), f32),
        V((128, 128), f32),
        V((4, 128, 768), bf16), V((4, 128, 768), bf16), V((4, 128, 768), bf16),
        V((4, 128, 1536), bf16), V((4, 128, 768), bf16), V((4, 128, 768), bf16),
        V((4, 128, 768), bf16), V((4, 128, 768), bf16), V((128, 768), f32), V((128, 768), f32),
        V((2, 4, 96, 2304), bf16), V((4, 96, 2304), bf16), V((3, 96, 2304), bf16),
        V((4, 512, 384), bf16), V((512, 768), f32), V((512, 768), f32), V((128, 768), bf16),
        V((128, 768), bf16), V((256, 768), bf16), V((4, 256, 384), bf16),
        V((4, 128, 768), bf16), V((4, 128, 768), bf16),
        V((4, 2, 4, 96, 768), bf16), V((4, 3, 96, 768), bf16),
        V((96, 768), f32), V((4, 96, 768), bf16), V((4, 96, 768), bf16),
        V((4, 8, 1152), f32), V((4, 8, 1152), f32), V((8, 8, 1152), f32),
        V((2, 4, 32, 128), f32), V((4, 32, 128), f32), V((4, 32, 128), f32), V((4, 32, 128), f32),
        V((32, 256), f32), V((4, 32, 256), f32),
        V((4, 192, 128), bf16), V((4, 192, 128), bf16), V((4, 192, 128), bf16),
        V((4, 192, 128), bf16), V((256, 64), f32), V((256, 128), f32),
        V((8, 256), f32),
        pltpu.SemaphoreType.DMA((160,)), pltpu.SemaphoreType.DMA((160,)),
        pltpu.SemaphoreType.DMA((2,)),
    ]
    whole = pl.BlockSpec(memory_space=pltpu.VMEM)
    outs = (
        ((512, 192), bf16), ((512, 192), bf16), ((2, 1024, 256), bf16), ((16, 256), bf16),
        ((3, 96, 192), f32), ((192, 96), f32), ((96, 2, 768), f32), ((96, 768), f32),
        ((6, 32, 192), f32), ((HEADS, 32), f32), ((32, classes), f32),
    )
    return pl.pallas_call(
        layer_kernel,
        out_shape=tuple(jax.ShapeDtypeStruct(s, t) for s, t in outs),
        in_specs=[whole] * 9
        + [pl.BlockSpec(memory_space=pl.ANY), whole]
        + [pl.BlockSpec(memory_space=pltpu.SMEM)] * 3,
        out_specs=(whole,) * len(outs),
        scratch_shapes=scratch,
        compiler_params=pltpu.CompilerParams(
            collective_id=0, has_side_effects=True, vmem_limit_bytes=67043328
        ),
        name="layer",
    )(*args)


def finish_kernel(*refs):
    ds, pw, out, res = refs[0:4]
    groups = [refs[4 + 3 * i : 7 + 3 * i] for i in range(7)]
    out_t, res_t, pair = refs[25:28]
    results = [refs[28 + 2 * i : 30 + 2 * i] for i in range(7)]
    block, sems = refs[42:44]
    step = pl.program_id(0)

    def put(c, at):
        rows = pl.ds((at % 2) * 32 + 8 * c, 8)
        return pltpu.make_async_copy(block.at[c], pair.at[at // 2, rows], sems.at[c])

    def update(index):
        (master, state, grad), (fresh, kept) = groups[index], results[index]
        old, slope = master[...], grad[...]
        first = BETA_ONE * state[0] + (1.0 - BETA_ONE) * slope
        second = BETA_TWO * state[1] + (1.0 - BETA_TWO) * slope * slope
        first_hat = first / (1.0 - BETA_ONE**STEP)
        second_hat = second / (1.0 - BETA_TWO**STEP)
        new = old - RATES[index] * (first_hat / (jnp.sqrt(second_hat) + ADAM_EPS) + DECAY * old)
        average = AVERAGE * state[2] + (1.0 - AVERAGE) * new
        for ref, values in ((fresh, (new, average)), (kept, (first, second))):
            for i in range(2):
                if index == 5:
                    ref[:, i, :] = values[i]
                else:
                    ref[i] = values[i]

    def turn(source, target):
        wide = jnp.concatenate([source[...].astype(f32), jnp.zeros((128, 64), f32)], axis=-1)
        target[...] = wide.T[0:192, :].astype(bf16)

    for c in range(4):

        @pl.when(step > 0)
        def _(c=c):
            put(c, step - 1).wait()

        for i in range(8):
            at = GROUP * (8 * c + i)
            block[c, i] = mm(ds[0, at : at + GROUP, :], pw[...], TN).astype(bf16)
        if c == 0:
            update(0)
            update(1)
            turn(out, out_t)
        elif c == 1:
            update(2)
        elif c == 2:
            update(3)
            turn(res, res_t)
        else:
            for index in (4, 5, 6):
                update(index)
        put(c, step).start()

    @pl.when(step == 3)
    def _():
        for c in range(4):
            put(c, step).wait()


def finish_call(ds, pw, out, res, *groups):
    def rows(shape, axis=-2):
        at = len(shape) + axis
        block = (*shape[:at], shape[at] // 4, *shape[at + 1 :])
        return pl.BlockSpec(block, lambda i: (0,) * at + (i,) + (0,) * (-1 - axis))

    def whole(shape):
        return pl.BlockSpec(tuple(shape), lambda i: (0,) * len(shape))

    in_specs = [
        pl.BlockSpec((1, 512, 256), lambda i: (i // 2, i % 2, 0)), whole((16, 256)),
        rows((512, 192)), rows((512, 192)),
    ]
    turned = pl.BlockSpec((192, 128), lambda i: (0, i))
    out_specs = [turned, turned, pl.BlockSpec(memory_space=pl.ANY)]
    outs = [
        jax.ShapeDtypeStruct((192, 512), bf16), jax.ShapeDtypeStruct((192, 512), bf16),
        jax.ShapeDtypeStruct((2, 64, 256, 256), bf16),
    ]
    for index in range(7):
        master, state, grad = groups[3 * index : 3 * index + 3]
        make = rows if index < 5 else whole
        if index == 2:
            make = lambda shape: rows(shape, -3)
        in_specs += [make(master.shape), make(state.shape), make(grad.shape)]
        shape = (2, *master.shape)
        if index == 5:
            shape = (master.shape[0], 2, master.shape[1])
        out_specs += [make(shape)] * 2
        outs += [jax.ShapeDtypeStruct(shape, f32)] * 2
    return pl.pallas_call(
        finish_kernel,
        grid=(4,),
        out_shape=tuple(outs),
        in_specs=in_specs,
        out_specs=tuple(out_specs),
        scratch_shapes=[pltpu.VMEM((4, 8, 256, 256), bf16), pltpu.SemaphoreType.DMA((4,))],
        compiler_params=pltpu.CompilerParams(vmem_limit_bytes=67043328),
        name="finish",
    )(ds, pw, out, res, *groups)


def fast_local(
    residues, pair_input, out_grad, bucket_layout, time_bins, fold_class,
    attend_weight, attend_state, merge_weight, merge_state, expand_weight, expand_state,
    shrink_weight, shrink_state, modulate_weight, modulate_state, pair_weight, pair_state,
    class_weight, class_state,
):
    classes = class_weight.shape[0]

    def thirds(v):
        return jnp.swapaxes(v, -3, -2).reshape(*v.shape[:-3], -1, v.shape[-1])

    def turned(v):
        return jnp.swapaxes(v, -2, -1)

    def same(v):
        return v

    views = (thirds, same, same, turned, thirds, turned, turned)
    masters = (
        attend_weight, merge_weight, expand_weight, shrink_weight, modulate_weight, pair_weight,
        class_weight,
    )
    states = (
        attend_state, merge_state, expand_state, shrink_state, modulate_state, pair_state,
        class_state,
    )
    flat = [view(master) for view, master in zip(views, masters)]
    out, res, ds, pw, *grads = layer_call(
        classes, flat[0].reshape(3, 96, 192), *flat[1:4], flat[4].reshape(6, 32, 192), *flat[5:],
        residues.T, out_grad.T, pair_input, jnp.asarray(WAVES), bucket_layout,
        time_bins, fold_class,
    )
    groups = []
    for view, master, state, grad in zip(views, flat, states, grads):
        groups += [master, view(state), grad.reshape(master.shape)]
    out, res, pair_grad, *results = finish_call(ds, pw, out, res, *groups)

    def back(index, v):
        if index in (0, 4):
            count = masters[index].shape[1]
            return jnp.swapaxes(v.reshape(2, count, -1, v.shape[-1]), 1, 2)
        if index == 5:
            return jnp.transpose(v, (1, 2, 0))
        return v if index in (1, 2) else turned(v)

    return (out.T, res.T, pair_grad, *(back(i // 2, v) for i, v in enumerate(results)))


def solution(mesh):
    quick = mesh.shape["dp"] == 8 and mesh.shape["mp"] == 4
    placed = (
        P("dp", "mp"),
        P("dp", "mp", None, None),
        P("dp", "mp"),
        P("dp"),
        P("dp", None),
        P("dp", None),
        P("dp", None, "mp"),
        P(None, "dp", None, "mp"),
        P("mp", "dp"),
        P(None, "mp", "dp"),
        P("dp", None, "mp"),
        P(None, "dp", None, "mp"),
        P("mp", "dp"),
        P(None, "mp", "dp"),
        P("dp", None, "mp"),
        P(None, "dp", None, "mp"),
        P("dp", None),
        P(None, "dp", None),
        P(None, "dp"),
        P(None, None, "dp"),
    )
    return jax.shard_map(
        fast_local if quick else local,
        mesh=mesh,
        in_specs=placed,
        out_specs=(
            P("dp", "mp"),
            P("dp", "mp"),
            P("dp", "mp", None, None),
            P(None, "dp", None, "mp"),
            P(None, "dp", None, "mp"),
            P(None, "mp", "dp"),
            P(None, "mp", "dp"),
            P(None, "dp", None, "mp"),
            P(None, "dp", None, "mp"),
            P(None, "mp", "dp"),
            P(None, "mp", "dp"),
            P(None, "dp", None, "mp"),
            P(None, "dp", None, "mp"),
            P(None, "dp", None),
            P(None, "dp", None),
            P(None, None, "dp"),
            P(None, None, "dp"),
        ),
        check_vma=False,
    )
```
